32 devices in a mesh: tiles: 8 (over z, x), chan: 4 (over y, core).
Axes of the slice: x: 2, y: 2, z: 4, core: 2. Of those that a mesh axis runs over, the one named last changes fastest.
Arguments:
- features: bfloat16 [512, 64, 256], P('tiles'), may hold values from -6 to 6
- weights: bfloat16 [27, 256, 256], P(None, None, 'chan')
- gain: bfloat16 [256], P('chan'), may hold values from 0.099609375 to 1.8984375
- rulebook: int32 [6144, 4], P('tiles'), may hold values from 0 to 191, as said below
- recv_list: int32 [8, 128], P('tiles'), may hold values from 0 to 63, as said below
- coarse_send: int32 [8, 8], P('tiles'), may hold values from 0 to 7, as said below
- coarse_place: int32 [8, 8], P('tiles'), may hold values from 0 to 7, as said below
Outputs:
- skip_features: bfloat16 [512, 64, 256], P('tiles', None, 'chan')
- coarse_features: bfloat16 [64, 64, 256], P('tiles', None, 'chan')
The draws below stay inside these ranges and needn't reach their ends.
Inputs may be any that keep to these rules, and one draw needn't show every extreme that they name: `rulebook`: Columns: input tile 0 to 63 of the device; kernel offset 0 to 26, or 27 for an empty row; direction 0 to 26, the input tile's place relative to the output tile, along each dimension 0 or equal to the kernel offset's nonzero component; target below 64 a tile of the device, else slot s = target - 64 for device d + dist(s // 16), which always exists. Empty rows have 0 in the other columns and direction 13. Each device has 192 or more live rows, some device none empty; every slot toward an existing device is named by a live row, and every tile has a row with offset 13, direction 13 and itself as input and target. `recv_list`: each tile of a device is named exactly twice in its row. `coarse_send`: strided owner map: coarse tile k of device s, global number p = s * 8 + k, goes to an owner that depends only on p % 8 (a permutation of the devices), in lane k // 8; slots of one row are distinct. `coarse_place`: the slot s + j of owner e holds the place of the coarse tile it receives; 8 marks a slot that carries nothing. Every coarse tile of the owner is written by exactly one slot.
All inputs are finite; a program needn't handle non-finite values.
Results may differ from the reference program's by a relative error of at most 0.0045.
Values may be sent and summed in bfloat16 or wider, within the bound.
No kernel may reach another device: no remote copies, remote signals or barrier semaphores. Data moves between devices by JAX's collectives and lax.ppermute only.
A program may use at most 128 MiB of HBM per device.

```python
import math
import jax
import jax.numpy as jnp
from jax import lax

C = 256
TILE_DEV = 64
NT = 512
NC = 64
PARENTS = 8
RULES_DEV = 768
CAPN = 16
CAP2 = 1
N_TILES = 8


def draw_weights(key, part):
    first, second = jax.random.split(jax.random.fold_in(key, 5), 2)
    column = jnp.arange(C, dtype=jnp.float32)
    ramp = 1.0 + 2.0 * column / (C - 1)
    spread = jax.random.uniform(second, (C,), jnp.float32)
    base = jax.random.normal(first, (27, C, C), jnp.float32)
    scale = 10.0 ** spread * ramp
    return (base * scale[None, None, :] / math.sqrt(C)).astype(jnp.bfloat16)


def draw_rulebook(key, part):
    device_count = NT // TILE_DEV
    tiles_here = TILE_DEV
    rows_here = RULES_DEV
    subkeys = jax.random.split(jax.random.fold_in(key, 11), 8)
    position = jnp.arange(rows_here, dtype=jnp.int32)[None, :]
    device_ids = jnp.arange(device_count, dtype=jnp.int32)[:, None]
    kernel = jax.random.randint(subkeys[0], (device_count, rows_here), 0, 27, jnp.int32)
    kernel = jnp.where(position < tiles_here, 13, kernel)
    coin_flips = jax.random.randint(subkeys[1], (device_count, rows_here, 3), 0, 2, jnp.int32)
    steps_tile = jnp.stack([kernel // 9 - 1, kernel // 3 % 3 - 1, kernel % 3 - 1], axis=-1) * coin_flips
    heading = (steps_tile[..., 0] + 1) * 9 + (steps_tile[..., 1] + 1) * 3 + steps_tile[..., 2] + 1
    target = jax.random.randint(subkeys[2], (device_count, rows_here), 0, 3 * tiles_here, jnp.int32)
    target = jnp.where(position < 3 * tiles_here, position, target)
    distances = jnp.array([1, 2, 3, 4, -1, -2, -3, -4], jnp.int32)
    group = jnp.clip((target - tiles_here) // CAPN, 0, 7)
    destination = device_ids + distances[group]
    missing = (target >= tiles_here) & ((destination < 0) | (destination >= device_count))
    local_pick = jax.random.randint(subkeys[7], (device_count, rows_here), 0, tiles_here, jnp.int32)
    target = jnp.where(missing, local_pick, target)
    source = jax.random.randint(subkeys[3], (device_count, rows_here), 0, tiles_here, jnp.int32)
    source = jnp.where(position < tiles_here, position, source)
    live_rows = jax.random.randint(subkeys[4], (device_count,), 3 * tiles_here, rows_here + 1, jnp.int32)
    fullest = jax.random.randint(subkeys[5], (), 0, device_count, jnp.int32)
    live_rows = jnp.where(jnp.arange(device_count, dtype=jnp.int32) == fullest, rows_here, live_rows)
    is_empty = position >= live_rows[:, None]
    kernel = jnp.where(is_empty, 27, kernel)
    heading = jnp.where(is_empty, 13, heading)
    target = jnp.where(is_empty, 0, target)
    source = jnp.where(is_empty, 0, source)
    shuffles = jax.vmap(lambda subkey: jax.random.permutation(subkey, rows_here))(jax.random.split(subkeys[6], device_count))
    ranking = shuffles.astype(jnp.int32) + jnp.where(is_empty, rows_here, 0)
    reorder = jnp.argsort(ranking, axis=1, stable=True)
    rulebook_rows = jnp.stack([source, kernel, heading, target], axis=-1)
    rulebook_rows = jnp.take_along_axis(rulebook_rows, reorder[:, :, None], axis=1)
    return rulebook_rows.reshape(device_count * rows_here, 4).astype(jnp.int32)


def draw_recv_list(key, part):
    device_count = NT // TILE_DEV
    subkeys = jax.random.split(jax.random.fold_in(key, 23), device_count)
    mixed = jax.vmap(lambda subkey: jax.random.permutation(subkey, 2 * TILE_DEV))(subkeys)
    return (mixed % TILE_DEV).astype(jnp.int32)


def coarse_maps(key):
    device_count = NT // TILE_DEV
    owners = jax.random.permutation(jax.random.fold_in(key, 31), device_count).astype(jnp.int32)
    sender = jnp.arange(device_count, dtype=jnp.int32)[:, None]
    parent = jnp.arange(PARENTS, dtype=jnp.int32)[None, :]
    whole = sender * PARENTS + parent
    owner = owners[whole % device_count]
    lane = parent // device_count + jnp.zeros_like(whole)
    send_slots = (owner * CAP2 + lane).astype(jnp.int32)
    received = jnp.zeros((device_count, device_count * CAP2), jnp.int32)
    received = received.at[owner.reshape(-1), (sender * CAP2 + lane).reshape(-1)].set(1)
    rank = jnp.cumsum(received, axis=1).astype(jnp.int32) - 1
    owner_keys = jax.random.split(jax.random.fold_in(key, 37), device_count)
    orders = jax.vmap(lambda subkey: jax.random.permutation(subkey, PARENTS))(owner_keys).astype(jnp.int32)
    chosen = jnp.take_along_axis(orders, jnp.clip(rank, 0, PARENTS - 1), axis=1)
    places = jnp.where(received > 0, chosen, PARENTS)
    return (send_slots, places.astype(jnp.int32))


def draw_coarse_send(key, part):
    return coarse_maps(key)[0]


def draw_coarse_place(key, part):
    return coarse_maps(key)[1]


def shard_levels(own_key, dims, cuts, smallest, largest):
    loudness, own = 1.0, jax.random.fold_in(own_key, 6)
    for dim, shards_of in cuts:
        steps = jnp.exp(jax.random.uniform(jax.random.fold_in(own, dim), (shards_of,), jnp.float32, smallest / len(cuts), largest / len(cuts)))
        loudness = loudness * jnp.repeat(steps, dims[dim] // shards_of).reshape([-1 if axis == dim else 1 for axis in range(len(dims))])
    return loudness


def gaussian(key, extent, deviation, limit, cuts=(), kind=jnp.bfloat16):
    level = shard_levels(key, extent, cuts, -0.22, 0.18) if cuts else 1.0
    values = jax.random.normal(key, extent, jnp.float32) * deviation * level
    return jnp.minimum(jnp.maximum(values, -limit), limit).astype(kind)


def setup_inputs(seed: int = 0) -> dict:
    arg_keys = jax.random.split(jax.random.key(seed), 8)
    return {
        "features": gaussian(arg_keys[0], (NT, 64, C), 1.0, 6.0, ((0, 8),)),
        "weights": draw_weights(jax.random.fold_in(arg_keys[7], 71), 0),
        "gain": jnp.clip(1.0 + 0.18 * jax.random.normal(arg_keys[2], (C,), jnp.float32), 0.099609375, 1.8984375).astype(jnp.bfloat16),
        "rulebook": draw_rulebook(jax.random.fold_in(arg_keys[7], 71), 0),
        "recv_list": draw_recv_list(jax.random.fold_in(arg_keys[7], 71), 0),
        "coarse_send": draw_coarse_send(jax.random.fold_in(arg_keys[7], 71), 0),
        "coarse_place": draw_coarse_place(jax.random.fold_in(arg_keys[7], 71), 0),
    }


epsilon = 1e-05

def offsets(code):
    return jnp.stack([code // 9 - 1, code // 3 % 3 - 1, code % 3 - 1], axis=-1)

def shift_table(kernel, heading):
    voxel = jnp.arange(64, dtype=jnp.int32)
    corner = jnp.stack([voxel // 16, voxel // 4 % 4, voxel % 4], axis=-1)
    source = corner[None, :, :] + offsets(jnp.minimum(kernel, 26))[:, None, :] - 4 * offsets(heading)[:, None, :]
    inside = jnp.all((source >= 0) & (source < 4), axis=-1) & (kernel < 27)[:, None]
    source = jnp.clip(source, 0, 3)
    where_from = (source[..., 0] * 16 + source[..., 1] * 4 + source[..., 2]).astype(jnp.int32)
    return (where_from, inside)

def pool_blocks(values):
    dims_in = values.shape
    blocked = values.astype(jnp.float32).reshape(dims_in[:-2] + (2, 2, 2, 2, 2, 2, dims_in[-1]))
    return lax.optimization_barrier(jnp.mean(blocked, axis=(-6, -4, -2))).reshape(dims_in[:-2] + (8, dims_in[-1])).astype(jnp.bfloat16)

def assemble(placed):
    number = placed.shape[0]
    blocked = placed.reshape(number, 2, 2, 2, 2, 2, 2, placed.shape[-1])
    return blocked.transpose(0, 1, 4, 2, 5, 3, 6, 7).reshape(number, 64, placed.shape[-1])

def device_conv(features, rules, weights):
    block_rows = min(128, rules.shape[0])
    grouped = rules.reshape(rules.shape[0] // block_rows, block_rows, 4)

    def step_rules(totals, group):
        where_from, inside = shift_table(group[:, 1], group[:, 2])
        fetched = features[group[:, 0]]
        chosen = jnp.take_along_axis(fetched, where_from[:, :, None], axis=1)
        chosen = jnp.where(inside[:, :, None], chosen, jnp.zeros_like(chosen))
        kernels = weights[jnp.minimum(group[:, 1], 26)].astype(jnp.float32)
        partial_out = jnp.einsum('bvc,bcq->bvq', chosen.astype(jnp.float32), kernels, precision=lax.Precision.HIGHEST)
        return (totals.at[group[:, 3]].add(partial_out), None)
    start = jnp.zeros((3 * TILE_DEV, 64, weights.shape[2]), jnp.float32)
    totals, unused = lax.scan(step_rules, start, grouped)
    return (totals[:TILE_DEV], totals[TILE_DEV:].astype(jnp.bfloat16))

def collect(triple):
    return triple[0].at[triple[2]].add(triple[1].astype(jnp.float32))

def reference(features, weights, gain, rulebook, recv_list, coarse_send, coarse_place):
    local_part = features.reshape(N_TILES, TILE_DEV, 64, C)
    rule_part = rulebook.reshape(N_TILES, RULES_DEV, 4)
    local_sum, sent = lax.map(lambda pair: device_conv(pair[0], pair[1], weights), (local_part, rule_part))
    sent_groups = sent.reshape(N_TILES, 8, CAPN, 64, C)
    pieces = []
    for group in range(8):
        distance = group + 1 if group < 4 else 3 - group
        piece = sent_groups[:, group]
        blank = jnp.zeros_like(piece[:abs(distance)])
        if distance > 0:
            moved = jnp.concatenate([blank, piece[:-distance]], axis=0)
        else:
            moved = jnp.concatenate([piece[-distance:], blank], axis=0)
        pieces.append(moved)
    received = jnp.stack(pieces, axis=1).reshape(N_TILES, 2 * TILE_DEV, 64, C)
    convolved = lax.map(collect, (local_sum, received, recv_list))
    mean_square = lax.optimization_barrier(jnp.mean(convolved * convolved, axis=-1, keepdims=True))
    hidden = jax.nn.silu(gain.astype(jnp.float32) * convolved * lax.rsqrt(mean_square + epsilon))
    skip_features = (local_part.astype(jnp.float32) + hidden).astype(jnp.bfloat16)
    pooled = pool_blocks(skip_features)
    parents = assemble(pooled.reshape(N_TILES * PARENTS, 8, 8, C)).reshape(N_TILES, PARENTS, 64, C)
    outbound = jax.vmap(lambda tiles_out, slots: jnp.zeros((N_TILES * CAP2, 64, C), jnp.bfloat16).at[slots].set(tiles_out))(parents, coarse_send)
    arrived = outbound.reshape(N_TILES, N_TILES, CAP2, 64, C).transpose(1, 0, 2, 3, 4).reshape(N_TILES, N_TILES * CAP2, 64, C)
    placed = jax.vmap(lambda landed, where_to: jnp.zeros((PARENTS, 64, C), jnp.bfloat16).at[where_to].set(landed, mode='drop'))(arrived, coarse_place)
    coarse_features = placed.reshape(NC, 64, C)
    return (skip_features.reshape(NT, 64, C), coarse_features)
```

```python
import functools

import jax
import jax.numpy as jnp
import numpy as np
from jax import lax
from jax.experimental import pallas as pl
from jax.experimental.pallas import tpu as pltpu
from jax.sharding import PartitionSpec as P

EPS = 1e-05
REACH = 4
VOX = 64
HALF = 32
BF = jnp.bfloat16
F32 = jnp.float32
PAD = 64
UNROLL = 8


def matchings(n):
    found = []
    for d in range(REACH, 0, -1):
        for parity in (0, 1):
            pairs = [(i, i + d) for i in range(n - d) if (i // d) % 2 == parity]
            if pairs:
                rest = [i for i in range(n) if all(i not in p for p in pairs)]
                fill = list(zip(rest[::2], rest[1::2]))
                both = pairs + fill
                found.append((d, parity, both + [(b, a) for a, b in both]))
    return found


def role(e, n, d, parity):
    low = jnp.logical_and(lax.rem(lax.div(e, d), 2) == parity, e + d < n)
    high = jnp.logical_and(e >= d, lax.rem(lax.div(jnp.maximum(e - d, 0), d), 2) == parity)
    return low, high


def lane_iota(shape):
    return lax.broadcasted_iota(jnp.int32, shape, len(shape) - 1)


def dims_of(code):
    return (lax.div(code, 9) - 1, lax.rem(lax.div(code, 3), 3) - 1, lax.rem(code, 3) - 1)


def conv_kernel(n, ways, tile_count, rules_ref, f_ref, w_ref, *rest):
    sends = rest[: len(ways)]
    local_ref, y_ref, acc_ref, words_v, words_s, sem = rest[len(ways) :]
    rows = tile_count * VOX
    span = rows + 2 * PAD
    rule_rows = rules_ref.shape[1]
    e = lax.axis_index("tiles")
    tile = rules_ref[0:1, :]
    kernel = rules_ref[1:2, :]
    heading = rules_ref[2:3, :]
    code = jnp.minimum(kernel, 26)
    shift = jnp.zeros_like(code)
    need = jnp.where(kernel < 27, 0, 1 << 23) + jnp.where(lax.rem(code, 2) == 0, 1 << 21, 1 << 22)
    for dim, (step, turn) in enumerate(zip(dims_of(code), dims_of(heading))):
        move = step - 4 * turn
        shift = shift + move * (16, 4, 1)[dim]
        need = need + jnp.left_shift(jnp.full_like(move, 1), move + (3 + 7 * dim))
    words_v[0:1, :] = lax.div(code, 2) * span + PAD + tile * VOX + shift
    words_v[1:2, :] = rules_ref[3:4, :]
    words_v[2:3, :] = need
    copy = pltpu.make_async_copy(words_v, words_s, sem)
    copy.start()

    def zero(i, c):
        acc_ref[i] = jnp.zeros((VOX, 128), F32)
        return c

    lax.fori_loop(0, 3 * tile_count, zero, 0)

    chunk = 512
    depth = w_ref.shape[0]
    for q in range(0, depth, 256):
        width = min(256, depth - q)

        def product(i, c, q=q, width=width):
            at = pl.multiple_of(i * chunk, chunk)
            part = lax.dot_general(
                f_ref[pl.ds(at, chunk), :],
                w_ref[q : q + width, :],
                (((1,), (1,)), ((), ())),
                preferred_element_type=F32,
            )
            for s in range(0, width, 128):
                wide = min(128, width - s)
                base = ((q + s) // 128) * span + PAD
                y_ref[pl.ds(pl.multiple_of(base + at, 8), chunk), 0:wide] = part[:, s : s + wide]
            return c

        lax.fori_loop(0, rows // chunk, product, 0)

    voxel = lax.broadcasted_iota(jnp.int32, (VOX, 128), 0)
    lane = lane_iota((VOX, 128))
    have = jnp.where(lane < 64, 1 << 21, 1 << 22)
    for dim, place in enumerate((lax.div(voxel, 16), lax.rem(lax.div(voxel, 4), 4), lax.rem(voxel, 4))):
        have = have + jnp.left_shift(jnp.full_like(place, 15), 3 - place + 7 * dim)
    copy.wait()

    def rule(i, c):
        for u in range(UNROLL):
            r = i * UNROLL + u
            need_r = words_s[2, r]
            taken = y_ref[pl.ds(words_s[0, r], VOX), :]
            t = words_s[1, r]
            acc_ref[t] = acc_ref[t] + jnp.where((have & need_r) == need_r, taken, 0.0)
        return c

    lax.fori_loop(0, rule_rows // UNROLL, rule, 0)

    first = lane_iota((HALF, 128)) < 64

    def folded(t):
        low = acc_ref[t, 0:HALF, :]
        high = acc_ref[t, HALF:VOX, :]
        low = low + pltpu.roll(low, 64, 1)
        high = high + pltpu.roll(high, 64, 1)
        return jnp.where(first, low, high)

    slots = 2 * tile_count // 8
    for (d, parity, _), send_ref in zip(ways, sends):
        low, _high = role(e, n, d, parity)
        base = tile_count + slots * jnp.where(low, d - 1, d + 3)

        def emit(i, c, send_ref=send_ref, base=base):
            send_ref[i] = folded(base + i).astype(BF)
            return c

        lax.fori_loop(0, slots, emit, 0)

    def keep(t, c):
        local_ref[t] = folded(t)
        return c

    lax.fori_loop(0, tile_count, keep, 0)


def own_kernel(f_ref, _after, out_ref):
    c = lax.axis_index("chan")
    at = pl.multiple_of(lax.div(c, 2) * 128, 128)
    odd = lax.rem(c, 2)
    first = lane_iota((HALF, 128)) < 64

    def pack(t, s):
        block = f_ref[t, :, pl.ds(at, 128)].astype(F32)
        low, high = block[:HALF], block[HALF:]
        even_form = jnp.where(first, low, pltpu.roll(high, 64, 1))
        odd_form = jnp.where(first, pltpu.roll(low, 64, 1), high)
        out_ref[t] = jnp.where(odd == 1, odd_form, even_form)
        return s

    lax.fori_loop(0, f_ref.shape[0], pack, 0)


def combine_kernel(n, ways, local_ref, list_ref, *rest):
    blocks = rest[: len(ways)]
    conv_ref, sums_ref = rest[len(ways) :]
    e = lax.axis_index("tiles")
    tile_count = local_ref.shape[0]
    slots = blocks[0].shape[0]
    conv_ref[...] = local_ref[...]
    for (d, parity, _), block in zip(ways, blocks):
        low, high = role(e, n, d, parity)
        base = slots * jnp.where(low, d + 3, d - 1)

        @pl.when(jnp.logical_or(low, high))
        def _(block=block, base=base):
            for i in range(slots):
                t = list_ref[0, base + i]
                conv_ref[t] = conv_ref[t] + block[i].astype(F32)

    rows = tile_count * HALF
    pick = (lane_iota((2, 256)) // 64 % 2 == lax.broadcasted_iota(jnp.int32, (2, 256), 0)).astype(BF)
    step = 512
    for at in range(0, rows, step):
        value = conv_ref[at // HALF : (at + step) // HALF].reshape(step, 128)
        square = value * value
        top = square.astype(BF)
        rest_of = (square - top.astype(F32)).astype(BF)
        sums_ref[:, at : at + step] = lax.dot_general(
            pick,
            jnp.concatenate([top, rest_of], axis=1),
            (((1,), (1,)), ((), ())),
            preferred_element_type=F32,
        )


def norm_kernel(channels, conv_ref, own_ref, gain_ref, pool_ref, slot_ref, s0, s1, s2, s3, skip_ref, out_ref):
    tile_count = conv_ref.shape[0]
    total = jnp.concatenate([s0[...], s1[...], s2[...], s3[...]], axis=0)
    parts = []
    for _ in range(3):
        top = total.astype(BF)
        parts.append(top.astype(F32))
        total = total - top.astype(F32)
    parts = jnp.concatenate(parts, axis=0).astype(BF)
    count = parts.shape[0]
    spread = (lane_iota((count, 128)) // 64 == lax.broadcasted_iota(jnp.int32, (count, 128), 0) % 2).astype(BF)
    gain = gain_ref[...]
    for k in range(tile_count // 8):
        mean_square = lax.dot_general(
            parts[:, k * 256 : (k + 1) * 256],
            spread,
            (((0,), (0,)), ((), ())),
            preferred_element_type=F32,
        ) * (1.0 / channels)
        value = conv_ref[8 * k : 8 * k + 8].reshape(256, 128)
        v = gain * value * lax.rsqrt(mean_square + EPS)
        hidden = v / (1.0 + jnp.exp(-v))
        whole = (own_ref[8 * k : 8 * k + 8].reshape(256, 128) + hidden).astype(BF)
        cut = whole.reshape(8, HALF, 128)
        skip_ref[8 * k : 8 * k + 8, 0:HALF, :] = cut[:, :, 0:64]
        skip_ref[8 * k : 8 * k + 8, HALF:VOX, :] = cut[:, :, 64:128]
        pooled = jnp.dot(pool_ref[...], whole, preferred_element_type=F32)
        out_ref[slot_ref[0, k]] = pooled.astype(BF)


def place_kernel(place_ref, landed_ref, out_ref):
    parents = out_ref.shape[0]
    for i in range(landed_ref.shape[0]):
        where = place_ref[0, i]

        @pl.when(where < parents)
        def _(i=i, where=where):
            for ox in range(2):
                for px in range(2):
                    row = 16 * (2 * ox + px)
                    out_ref[where, row : row + 16, :] = landed_ref[i, 16 * ox : 16 * ox + 16, 64 * px : 64 * px + 64]


def pool_matrix():
    out = np.zeros((2, 4, 4, 2, 2, 2, 2, 4, 4), np.float32)
    for ox in range(2):
        for y in range(4):
            for z in range(4):
                out[ox, y, z, ox, y // 2, z // 2, :, 2 * (y % 2) : 2 * (y % 2) + 2, 2 * (z % 2) : 2 * (z % 2) + 2] = 0.125
    return out.reshape(32, 256)


VM = pl.BlockSpec(memory_space=pltpu.VMEM)
SM = pl.BlockSpec(memory_space=pltpu.SMEM)


def body(n, features, weights, gain, rulebook, recv_list, coarse_send, coarse_place):
    tile_count, _, channels = features.shape
    offsets, _, quarter = weights.shape
    rule_rows = rulebook.shape[0]
    ways = matchings(n)
    slots = tile_count // 4
    span = tile_count * VOX + 2 * PAD
    pairs = (offsets + 1) // 2
    params = pltpu.CompilerParams(vmem_limit_bytes=58 * 1024 * 1024)
    small = pltpu.CompilerParams(vmem_limit_bytes=24 * 1024 * 1024)

    flat_weights = weights.transpose(0, 2, 1).reshape(offsets * quarter, channels)
    block = jax.ShapeDtypeStruct((slots, HALF, 128), BF)
    made = pl.pallas_call(
        functools.partial(conv_kernel, n, ways, tile_count),
        out_shape=[block] * len(ways) + [jax.ShapeDtypeStruct((tile_count, HALF, 128), F32)],
        in_specs=[VM] * 3,
        out_specs=[VM] * (len(ways) + 1),
        scratch_shapes=[
            pltpu.VMEM((pairs * span, 128), F32),
            pltpu.VMEM((3 * tile_count, VOX, 128), F32),
            pltpu.VMEM((8, rule_rows), jnp.int32),
            pltpu.SMEM((8, rule_rows), jnp.int32),
            pltpu.SemaphoreType.DMA,
        ],
        compiler_params=params,
        name="rules",
    )(rulebook.T, features.reshape(tile_count * VOX, channels), flat_weights)
    sends, local = made[:-1], made[-1]
    arrivals = [lax.ppermute(x, "tiles", way[2]) for x, way in zip(sends, ways)]
    own = pl.pallas_call(
        own_kernel,
        out_shape=jax.ShapeDtypeStruct((tile_count, HALF, 128), F32),
        in_specs=[VM, pl.BlockSpec(memory_space=pl.ANY)],
        out_specs=VM,
        compiler_params=small,
        cost_estimate=pl.CostEstimate(flops=2000000, bytes_accessed=4000000, transcendentals=0),
        name="own",
    )(features, local)
    conv, sums = pl.pallas_call(
        functools.partial(combine_kernel, n, ways),
        out_shape=[
            jax.ShapeDtypeStruct((tile_count, HALF, 128), F32),
            jax.ShapeDtypeStruct((2, tile_count * HALF), F32),
        ],
        in_specs=[VM, SM] + [VM] * len(ways),
        out_specs=[VM, VM],
        compiler_params=small,
        name="combine",
    )(local, recv_list, *arrivals)
    wide = lax.axis_size("chan")
    others = [lax.ppermute(sums, "chan", [(i, i ^ m) for i in range(wide)]) for m in range(1, wide)]
    slot_count = coarse_place.shape[1]
    parent_count = tile_count // 8
    skip, outbound = pl.pallas_call(
        functools.partial(norm_kernel, channels),
        out_shape=[
            jax.ShapeDtypeStruct((tile_count, VOX, quarter), BF),
            jax.ShapeDtypeStruct((slot_count, HALF, 128), BF),
        ],
        in_specs=[VM] * 4 + [SM] + [VM] * 4,
        out_specs=[VM, VM],
        compiler_params=small,
        name="norm",
    )(
        conv,
        own,
        jnp.tile(gain.astype(F32), 2).reshape(1, 128),
        jnp.asarray(pool_matrix(), BF),
        coarse_send,
        sums,
        *others,
    )
    landed = lax.all_to_all(outbound, "tiles", split_axis=0, concat_axis=0, tiled=True)
    coarse = pl.pallas_call(
        place_kernel,
        out_shape=jax.ShapeDtypeStruct((parent_count, VOX, quarter), BF),
        in_specs=[SM, VM],
        out_specs=VM,
        compiler_params=small,
        name="place",
    )(coarse_place, landed)
    return (skip, coarse)


def solution(mesh):
    in_specs = (
        P("tiles", None, None),
        P(None, None, "chan"),
        P("chan"),
        P("tiles", None),
        P("tiles", None),
        P("tiles", None),
        P("tiles", None),
    )
    out_specs = (P("tiles", None, "chan"), P("tiles", None, "chan"))
    return jax.shard_map(
        functools.partial(body, mesh.shape["tiles"]),
        mesh=mesh,
        in_specs=in_specs,
        out_specs=out_specs,
        check_vma=False,
    )
```

```python
import functools

import jax
import jax.numpy as jnp
import numpy as np
from jax import lax
from jax.experimental import pallas as pl
from jax.experimental.pallas import tpu as pltpu
from jax.sharding import PartitionSpec as P

EPS = 1e-05
REACH = 4
VOX = 64
HALF = 32
BF = jnp.bfloat16
F32 = jnp.float32
PAD = 64
UNROLL = 8


def matchings(n):
    found = []
    for d in range(REACH, 0, -1):
        for parity in (0, 1):
            pairs = [(i, i + d) for i in range(n - d) if (i // d) % 2 == parity]
            if pairs:
                rest = [i for i in range(n) if all(i not in p for p in pairs)]
                fill = list(zip(rest[::2], rest[1::2]))
                both = pairs + fill
                found.append((d, parity, both + [(b, a) for a, b in both]))
    return found


def role(e, n, d, parity):
    low = jnp.logical_and(lax.rem(lax.div(e, d), 2) == parity, e + d < n)
    high = jnp.logical_and(e >= d, lax.rem(lax.div(jnp.maximum(e - d, 0), d), 2) == parity)
    return low, high


def lane_iota(shape):
    return lax.broadcasted_iota(jnp.int32, shape, len(shape) - 1)


def dims_of(code):
    return (lax.div(code, 9) - 1, lax.rem(lax.div(code, 3), 3) - 1, lax.rem(code, 3) - 1)


def conv_kernel(n, ways, tile_count, rules_ref, f_ref, w_ref, *rest):
    sends = rest[: len(ways)]
    local_ref, y_ref, acc_ref, words_v, words_s, sem = rest[len(ways) :]
    rows = tile_count * VOX
    span = rows + 2 * PAD
    rule_rows = rules_ref.shape[1]
    e = lax.axis_index("tiles")
    tile = rules_ref[0:1, :]
    kernel = rules_ref[1:2, :]
    heading = rules_ref[2:3, :]
    code = jnp.minimum(kernel, 26)
    shift = jnp.zeros_like(code)
    need = jnp.where(kernel < 27, 0, 1 << 23) + jnp.where(lax.rem(code, 2) == 0, 1 << 21, 1 << 22)
    for dim, (step, turn) in enumerate(zip(dims_of(code), dims_of(heading))):
        move = step - 4 * turn
        shift = shift + move * (16, 4, 1)[dim]
        need = need + jnp.left_shift(jnp.full_like(move, 1), move + (3 + 7 * dim))
    words_v[0:1, :] = lax.div(code, 2) * span + PAD + tile * VOX + shift
    words_v[1:2, :] = rules_ref[3:4, :]
    words_v[2:3, :] = need
    copy = pltpu.make_async_copy(words_v, words_s, sem)
    copy.start()

    def zero(i, c):
        acc_ref[i] = jnp.zeros((VOX, 128), F32)
        return c

    lax.fori_loop(0, 3 * tile_count, zero, 0, unroll=8)

    chunk = rows
    depth = w_ref.shape[0]
    for q in range(0, depth, 256):
        width = min(256, depth - q)

        def product(i, c, q=q, width=width):
            at = pl.multiple_of(i * chunk, chunk)
            part = lax.dot_general(
                f_ref[pl.ds(at, chunk), :],
                w_ref[q : q + width, :],
                (((1,), (1,)), ((), ())),
                preferred_element_type=F32,
            )
            for s in range(0, width, 128):
                wide = min(128, width - s)
                base = ((q + s) // 128) * span + PAD
                y_ref[pl.ds(pl.multiple_of(base + at, 8), chunk), 0:wide] = part[:, s : s + wide]
            return c

        lax.fori_loop(0, rows // chunk, product, 0)

    voxel = lax.broadcasted_iota(jnp.int32, (VOX, 128), 0)
    lane = lane_iota((VOX, 128))
    have = jnp.where(lane < 64, 1 << 21, 1 << 22)
    for dim, place in enumerate((lax.div(voxel, 16), lax.rem(lax.div(voxel, 4), 4), lax.rem(voxel, 4))):
        have = have + jnp.left_shift(jnp.full_like(place, 15), 3 - place + 7 * dim)
    copy.wait()

    def rule(i, c):
        for u in range(UNROLL):
            r = i * UNROLL + u
            need_r = words_s[2, r]
            taken = y_ref[pl.ds(words_s[0, r], VOX), :]
            t = words_s[1, r]
            acc_ref[t] = acc_ref[t] + jnp.where((have & need_r) == need_r, taken, 0.0)
        return c

    lax.fori_loop(0, rule_rows // UNROLL, rule, 0)

    first = lane_iota((HALF, 128)) < 64

    def folded(t):
        low = acc_ref[t, 0:HALF, :]
        high = acc_ref[t, HALF:VOX, :]
        low = low + pltpu.roll(low, 64, 1)
        high = high + pltpu.roll(high, 64, 1)
        return jnp.where(first, low, high)

    slots = 2 * tile_count // 8
    for (d, parity, _), send_ref in zip(ways, sends):
        low, _high = role(e, n, d, parity)
        base = tile_count + slots * jnp.where(low, d - 1, d + 3)

        def emit(i, c, send_ref=send_ref, base=base):
            send_ref[i] = folded(base + i).astype(BF)
            return c

        lax.fori_loop(0, slots, emit, 0, unroll=16)

    def keep(t, c):
        local_ref[t] = folded(t)
        return c

    lax.fori_loop(0, tile_count, keep, 0, unroll=16)


def own_kernel(f_ref, _after, out_ref):
    c = lax.axis_index("chan")
    at = pl.multiple_of(lax.div(c, 2) * 128, 128)
    odd = lax.rem(c, 2)
    first = lane_iota((HALF, 128)) < 64

    def pack(t, s):
        block = f_ref[t, :, pl.ds(at, 128)].astype(F32)
        low, high = block[:HALF], block[HALF:]
        even_form = jnp.where(first, low, pltpu.roll(high, 64, 1))
        odd_form = jnp.where(first, pltpu.roll(low, 64, 1), high)
        out_ref[t] = jnp.where(odd == 1, odd_form, even_form)
        return s

    lax.fori_loop(0, f_ref.shape[0], pack, 0, unroll=8)


def combine_kernel(n, ways, local_ref, list_ref, _own, *rest):
    blocks = rest[: len(ways)]
    conv_ref, sums_ref = rest[len(ways) :]
    e = lax.axis_index("tiles")
    tile_count = local_ref.shape[0]
    slots = blocks[0].shape[0]
    conv_ref[...] = local_ref[...]
    for (d, parity, _), block in zip(ways, blocks):
        low, high = role(e, n, d, parity)
        base = slots * jnp.where(low, d + 3, d - 1)

        @pl.when(jnp.logical_or(low, high))
        def _(block=block, base=base):
            for i in range(slots):
                t = list_ref[0, base + i]
                conv_ref[t] = conv_ref[t] + block[i].astype(F32)

    rows = tile_count * HALF
    pick = (lane_iota((2, 256)) // 64 % 2 == lax.broadcasted_iota(jnp.int32, (2, 256), 0)).astype(BF)
    step = 512
    for at in range(0, rows, step):
        value = conv_ref[at // HALF : (at + step) // HALF].reshape(step, 128)
        square = value * value
        top = square.astype(BF)
        rest_of = (square - top.astype(F32)).astype(BF)
        sums_ref[:, at : at + step] = lax.dot_general(
            pick,
            jnp.concatenate([top, rest_of], axis=1),
            (((1,), (1,)), ((), ())),
            preferred_element_type=F32,
        )


def norm_kernel(channels, conv_ref, own_ref, gain_ref, pool_ref, slot_ref, s0, s1, s2, s3, skip_ref, out_ref):
    tile_count = conv_ref.shape[0]
    total = jnp.concatenate([s0[...], s1[...], s2[...], s3[...]], axis=0)
    parts = []
    for _ in range(3):
        top = total.astype(BF)
        parts.append(top.astype(F32))
        total = total - top.astype(F32)
    parts = jnp.concatenate(parts, axis=0).astype(BF)
    count = parts.shape[0]
    spread = (lane_iota((count, 128)) // 64 == lax.broadcasted_iota(jnp.int32, (count, 128), 0) % 2).astype(BF)
    gain = gain_ref[...]
    for k in range(tile_count // 8):
        mean_square = lax.dot_general(
            parts[:, k * 256 : (k + 1) * 256],
            spread,
            (((0,), (0,)), ((), ())),
            preferred_element_type=F32,
        ) * (1.0 / channels)
        value = conv_ref[8 * k : 8 * k + 8].reshape(256, 128)
        v = gain * value * lax.rsqrt(mean_square + EPS)
        hidden = v / (1.0 + jnp.exp(-v))
        whole = (own_ref[8 * k : 8 * k + 8].reshape(256, 128) + hidden).astype(BF)
        cut = whole.reshape(8, HALF, 128)
        skip_ref[8 * k : 8 * k + 8, 0:HALF, :] = cut[:, :, 0:64]
        skip_ref[8 * k : 8 * k + 8, HALF:VOX, :] = cut[:, :, 64:128]
        pooled = jnp.dot(pool_ref[...], whole, preferred_element_type=F32)
        out_ref[slot_ref[0, k]] = pooled.astype(BF)


def place_kernel(place_ref, landed_ref, out_ref):
    parents = out_ref.shape[0]
    for i in range(landed_ref.shape[0]):
        where = place_ref[0, i]

        @pl.when(where < parents)
        def _(i=i, where=where):
            for ox in range(2):
                for px in range(2):
                    row = 16 * (2 * ox + px)
                    out_ref[where, row : row + 16, :] = landed_ref[i, 16 * ox : 16 * ox + 16, 64 * px : 64 * px + 64]


def pool_matrix():
    out = np.zeros((2, 4, 4, 2, 2, 2, 2, 4, 4), np.float32)
    for ox in range(2):
        for y in range(4):
            for z in range(4):
                out[ox, y, z, ox, y // 2, z // 2, :, 2 * (y % 2) : 2 * (y % 2) + 2, 2 * (z % 2) : 2 * (z % 2) + 2] = 0.125
    return out.reshape(32, 256)


VM = pl.BlockSpec(memory_space=pltpu.VMEM)
SM = pl.BlockSpec(memory_space=pltpu.SMEM)


def call_rules(n, features, weights, rulebook):
    tile_count, _, channels = features.shape
    offsets, _, quarter = weights.shape
    rule_rows = rulebook.shape[0]
    ways = matchings(n)
    slots = tile_count // 4
    span = tile_count * VOX + 2 * PAD
    pairs = (offsets + 1) // 2
    flat_weights = weights.transpose(0, 2, 1).reshape(offsets * quarter, channels)
    block = jax.ShapeDtypeStruct((slots, HALF, 128), BF)
    return pl.pallas_call(
        functools.partial(conv_kernel, n, ways, tile_count),
        out_shape=[block] * len(ways) + [jax.ShapeDtypeStruct((tile_count, HALF, 128), F32)],
        in_specs=[VM] * 3,
        out_specs=[VM] * (len(ways) + 1),
        scratch_shapes=[
            pltpu.VMEM((pairs * span, 128), F32),
            pltpu.VMEM((3 * tile_count, VOX, 128), F32),
            pltpu.VMEM((8, rule_rows), jnp.int32),
            pltpu.SMEM((8, rule_rows), jnp.int32),
            pltpu.SemaphoreType.DMA,
        ],
        compiler_params=pltpu.CompilerParams(vmem_limit_bytes=48 * 1024 * 1024),
        name="rules",
    )(rulebook.T, features.reshape(tile_count * VOX, channels), flat_weights)


def body(n, features, weights, gain, rulebook, recv_list, coarse_send, coarse_place):
    tile_count, _, channels = features.shape
    quarter = weights.shape[2]
    ways = matchings(n)
    small = pltpu.CompilerParams(vmem_limit_bytes=12 * 1024 * 1024)

    made = call_rules(n, features, weights, rulebook)
    sends, local = made[:-1], made[-1]
    arrivals = [lax.ppermute(x, "tiles", way[2]) for x, way in zip(sends, ways)]
    own = pl.pallas_call(
        own_kernel,
        out_shape=jax.ShapeDtypeStruct((tile_count, HALF, 128), F32),
        in_specs=[VM, pl.BlockSpec(memory_space=pl.ANY)],
        out_specs=VM,
        compiler_params=small,
        cost_estimate=pl.CostEstimate(flops=2000000, bytes_accessed=4000000, transcendentals=0),
        name="own",
    )(features, local)
    conv, sums = pl.pallas_call(
        functools.partial(combine_kernel, n, ways),
        out_shape=[
            jax.ShapeDtypeStruct((tile_count, HALF, 128), F32),
            jax.ShapeDtypeStruct((2, tile_count * HALF), F32),
        ],
        in_specs=[VM, SM, pl.BlockSpec(memory_space=pl.ANY)] + [VM] * len(ways),
        out_specs=[VM, VM],
        compiler_params=small,
        name="combine",
    )(local, recv_list, own, *arrivals)
    wide = lax.axis_size("chan")
    others = [lax.ppermute(sums, "chan", [(i, i ^ m) for i in range(wide)]) for m in range(1, wide)]
    slot_count = coarse_place.shape[1]
    parent_count = tile_count // 8
    skip, outbound = pl.pallas_call(
        functools.partial(norm_kernel, channels),
        out_shape=[
            jax.ShapeDtypeStruct((tile_count, VOX, quarter), BF),
            jax.ShapeDtypeStruct((slot_count, HALF, 128), BF),
        ],
        in_specs=[VM] * 4 + [SM] + [VM] * 4,
        out_specs=[VM, VM],
        compiler_params=small,
        name="norm",
    )(
        conv,
        own,
        jnp.tile(gain.astype(F32), 2).reshape(1, 128),
        jnp.asarray(pool_matrix(), BF),
        coarse_send,
        sums,
        *others,
    )
    landed = lax.all_to_all(outbound, "tiles", split_axis=0, concat_axis=0, tiled=True)
    coarse = pl.pallas_call(
        place_kernel,
        out_shape=jax.ShapeDtypeStruct((parent_count, VOX, quarter), BF),
        in_specs=[SM, VM],
        out_specs=VM,
        compiler_params=small,
        name="place",
    )(coarse_place, landed)
    return (skip, coarse)


def solution(mesh):
    in_specs = (
        P("tiles", None, None),
        P(None, None, "chan"),
        P("chan"),
        P("tiles", None),
        P("tiles", None),
        P("tiles", None),
        P("tiles", None),
    )
    out_specs = (P("tiles", None, "chan"), P("tiles", None, "chan"))
    return jax.shard_map(
        functools.partial(body, mesh.shape["tiles"]),
        mesh=mesh,
        in_specs=in_specs,
        out_specs=out_specs,
        check_vma=False,
    )
```

```python
import functools

import jax
import jax.numpy as jnp
import numpy as np
from jax import lax
from jax.experimental import pallas as pl
from jax.experimental.pallas import tpu as pltpu
from jax.sharding import PartitionSpec as P

EPS = 1e-05
REACH = 4
VOX = 64
HALF = 32
BF = jnp.bfloat16
F32 = jnp.float32
PAD = 64
UNROLL = 8


def matchings(n):
    found = []
    for d in range(REACH, 0, -1):
        for parity in (0, 1):
            pairs = [(i, i + d) for i in range(n - d) if (i // d) % 2 == parity]
            if pairs:
                rest = [i for i in range(n) if all(i not in p for p in pairs)]
                fill = list(zip(rest[::2], rest[1::2]))
                both = pairs + fill
                found.append((d, parity, both + [(b, a) for a, b in both]))
    return found


def role(e, n, d, parity):
    low = jnp.logical_and(lax.rem(lax.div(e, d), 2) == parity, e + d < n)
    high = jnp.logical_and(e >= d, lax.rem(lax.div(jnp.maximum(e - d, 0), d), 2) == parity)
    return low, high


def lane_iota(shape):
    return lax.broadcasted_iota(jnp.int32, shape, len(shape) - 1)


def dims_of(code):
    return (lax.div(code, 9) - 1, lax.rem(lax.div(code, 3), 3) - 1, lax.rem(code, 3) - 1)


def rules_matmul(f_ref, w_ref, y_ref, beside=None):
    rows = f_ref.shape[0]
    span = rows + 2 * PAD
    depth = w_ref.shape[0]
    steps = range(0, depth, 256)
    for number, q in enumerate(steps):
        width = min(256, depth - q)
        part = lax.dot_general(
            f_ref[...],
            w_ref[q : q + width, :],
            (((1,), (1,)), ((), ())),
            preferred_element_type=F32,
        )
        for s in range(0, width, 128):
            wide = min(128, width - s)
            base = ((q + s) // 128) * span + PAD
            y_ref[base : base + rows, 0:wide] = part[:, s : s + wide]
        if beside is not None:
            beside(number, len(steps))


def rules_add(words, lists, start, count, y_ref, acc_ref):
    voxel = lax.broadcasted_iota(jnp.int32, (VOX, 128), 0)
    have = jnp.where(lane_iota((VOX, 128)) < 64, 1 << 21, 1 << 22)
    for dim, place in enumerate((lax.div(voxel, 16), lax.rem(lax.div(voxel, 4), 4), lax.rem(voxel, 4))):
        have = have + jnp.left_shift(jnp.full_like(place, 15), 3 - place + 7 * dim)

    def several(i, c):
        for u in range(UNROLL):
            r = lists[start + i * UNROLL + u]
            packed = words[0, r]
            need = words[1, r]
            taken = y_ref[pl.ds(lax.shift_right_logical(packed, 8), VOX), :]
            t = packed & 255
            acc_ref[t] = acc_ref[t] + jnp.where((have & need) == need, taken, 0.0)
        return c

    lax.fori_loop(0, lax.div(count + (UNROLL - 1), UNROLL), several, 0)


def zero_blocks(acc_ref):
    def zero(i, c):
        acc_ref[i] = jnp.zeros((VOX, 128), F32)
        return c

    lax.fori_loop(0, acc_ref.shape[0], zero, 0, unroll=8)


def folded(acc_ref, t):
    first = lane_iota((HALF, 128)) < 64
    low = acc_ref[t, 0:HALF, :]
    high = acc_ref[t, HALF:VOX, :]
    low = low + pltpu.roll(low, 64, 1)
    high = high + pltpu.roll(high, 64, 1)
    return jnp.where(first, low, high)


def emit_sends(n, ways, acc_ref, sends):
    e = lax.axis_index("tiles")
    slots = sends[0].shape[0]
    for (d, parity, _), send_ref in zip(ways, sends):
        low, _high = role(e, n, d, parity)
        base = slots * ((d - 1) % 2 + jnp.where(low, 0, 2))

        def emit(i, c, send_ref=send_ref, base=base):
            send_ref[i] = folded(acc_ref, base + i).astype(BF)
            return c

        lax.fori_loop(0, slots, emit, 0, unroll=16)


def far_kernel(n, ways, tile_count, rules_hbm, f_hbm, w_hbm, *rest):
    sends = rest[: len(ways)]
    words_v, lists, y_ref, acc_ref, f_ref, w_ref, rules_ref, words_s, sems = rest[len(ways) :]
    rows = tile_count * VOX
    span = rows + 2 * PAD
    rule_rows = rules_ref.shape[1]
    wide = words_v.shape[1]
    slots = tile_count // 4
    copies = [
        pltpu.make_async_copy(src, dst, sems.at[i])
        for i, (src, dst) in enumerate(((rules_hbm, rules_ref), (w_hbm, w_ref), (f_hbm, f_ref)))
    ]
    for copy in copies:
        copy.start()
    before = lax.broadcasted_iota(jnp.int32, (rule_rows, rule_rows), 0)
    before = (before <= lane_iota((rule_rows, rule_rows))).astype(F32).astype(BF)
    zero_blocks(acc_ref)
    copies[0].wait()
    tile = rules_ref[0:1, :]
    kernel = rules_ref[1:2, :]
    heading = rules_ref[2:3, :]
    target = rules_ref[3:4, :]
    code = jnp.minimum(kernel, 26)
    shift = jnp.zeros_like(code)
    need = jnp.where(lax.rem(code, 2) == 0, 1 << 21, 1 << 22)
    for dim, (step, turn) in enumerate(zip(dims_of(code), dims_of(heading))):
        move = step - 4 * turn
        shift = shift + move * (16, 4, 1)[dim]
        need = need + jnp.left_shift(jnp.full_like(move, 1), move + (3 + 7 * dim))
    sent = jnp.maximum(target - tile_count, 0)
    group = lax.div(sent, slots)
    place = (lax.div(group, 4) * 2 + lax.rem(group, 2)) * slots + lax.rem(sent, slots)
    near = lax.rem(group, 4) < 2
    part = jnp.where(target < tile_count, 2, jnp.where(near, 1, 0))
    part = jnp.where(kernel < 27, part, 3)
    kind = lax.broadcasted_iota(jnp.int32, (8, rule_rows), 0)
    flags = jnp.where(kind == part, 1.0, 0.0)
    upto = jnp.dot(flags.astype(BF), before, preferred_element_type=F32)
    at = jnp.sum(flags * (upto - 1.0 + (kind * wide).astype(F32)), axis=0, keepdims=True)
    first_row = lax.div(code, 2) * span + PAD + tile * VOX + shift
    words_v[...] = jnp.zeros(words_v.shape, jnp.int32)
    words_v[0:1, 0:rule_rows] = first_row * 256 + jnp.where(target < tile_count, target, place)
    words_v[1:2, 0:rule_rows] = need
    words_v[2:3, 0:rule_rows] = at.astype(jnp.int32)
    words_v[0:1, rule_rows:wide] = jnp.full((1, wide - rule_rows), PAD * 256, jnp.int32)
    words_v[1:2, rule_rows:wide] = jnp.full((1, wide - rule_rows), 1 << 23, jnp.int32)
    totals = jnp.broadcast_to(upto[0:3, rule_rows - 1 : rule_rows], (3, 128))
    words_v[3:6, 0:128] = totals.astype(jnp.int32)
    to_scalars = pltpu.make_async_copy(words_v, words_s, sems.at[3])
    to_scalars.start()
    to_scalars.wait()
    copies[1].wait()
    copies[2].wait()

    def list_some(number, count):
        share = -(-rule_rows // count)
        for r in range(number * share, min(rule_rows, (number + 1) * share)):
            lists[words_s[2, r]] = r

    rules_matmul(f_ref, w_ref, y_ref, list_some)
    for c in range(3):
        for u in range(UNROLL):
            lists[c * wide + words_s[3 + c, 0] + u] = rule_rows
    rules_add(words_s, lists, 0, words_s[3, 0], y_ref, acc_ref)
    emit_sends(n, ways, acc_ref, sends)


def near_kernel(n, ways, words, lists, f_ref, w_ref, *rest):
    sends = rest[: len(ways)]
    y_ref, acc_ref = rest[len(ways) :]
    zero_blocks(acc_ref)
    rules_matmul(f_ref, w_ref, y_ref)
    rules_add(words, lists, words.shape[1], words[4, 0], y_ref, acc_ref)
    emit_sends(n, ways, acc_ref, sends)


def local_kernel(words, lists, f_ref, w_ref, _after, local_ref, own_ref, y_ref, acc_ref):
    tile_count = acc_ref.shape[0]
    zero_blocks(acc_ref)
    rules_matmul(f_ref, w_ref, y_ref)
    rules_add(words, lists, 2 * words.shape[1], words[5, 0], y_ref, acc_ref)
    c = lax.axis_index("chan")
    at = pl.multiple_of(lax.div(c, 2) * 128, 128)
    odd = lax.rem(c, 2) == 1
    first = lane_iota((HALF, 128)) < 64

    def keep(t, c):
        local_ref[t] = folded(acc_ref, t)
        block = f_ref[pl.ds(pl.multiple_of(t * VOX, VOX), VOX), pl.ds(at, 128)].astype(F32)
        low, high = block[:HALF], block[HALF:]
        even_form = jnp.where(first, low, pltpu.roll(high, 64, 1))
        odd_form = jnp.where(first, pltpu.roll(low, 64, 1), high)
        own_ref[t] = jnp.where(odd, odd_form, even_form)
        return c

    lax.fori_loop(0, tile_count, keep, 0, unroll=8)


def combine_kernel(n, ways, local_ref, list_ref, *rest):
    blocks = rest[: len(ways)]
    conv_ref, sums_ref = rest[len(ways) :]
    e = lax.axis_index("tiles")
    tile_count = local_ref.shape[0]
    slots = blocks[0].shape[0]
    conv_ref[...] = local_ref[...]
    for (d, parity, _), block in zip(ways, blocks):
        low, high = role(e, n, d, parity)
        base = slots * jnp.where(low, d + 3, d - 1)

        @pl.when(jnp.logical_or(low, high))
        def _(block=block, base=base):
            for i in range(slots):
                t = list_ref[0, base + i]
                conv_ref[t] = conv_ref[t] + block[i].astype(F32)

    rows = tile_count * HALF
    pick = (lane_iota((2, 256)) // 64 % 2 == lax.broadcasted_iota(jnp.int32, (2, 256), 0)).astype(BF)
    step = 512
    for at in range(0, rows, step):
        value = conv_ref[at // HALF : (at + step) // HALF].reshape(step, 128)
        square = value * value
        top = square.astype(BF)
        rest_of = (square - top.astype(F32)).astype(BF)
        sums_ref[:, at : at + step] = lax.dot_general(
            pick,
            jnp.concatenate([top, rest_of], axis=1),
            (((1,), (1,)), ((), ())),
            preferred_element_type=F32,
        )


def norm_kernel(channels, conv_ref, own_ref, gain_ref, pool_ref, slot_ref, s0, s1, s2, s3, skip_ref, out_ref):
    tile_count = conv_ref.shape[0]
    total = jnp.concatenate([s0[...], s1[...], s2[...], s3[...]], axis=0)
    parts = []
    for _ in range(3):
        top = total.astype(BF)
        parts.append(top.astype(F32))
        total = total - top.astype(F32)
    parts = jnp.concatenate(parts, axis=0).astype(BF)
    count = parts.shape[0]
    spread = (lane_iota((count, 128)) // 64 == lax.broadcasted_iota(jnp.int32, (count, 128), 0) % 2).astype(BF)
    gain = gain_ref[...]
    for k in range(tile_count // 8):
        mean_square = lax.dot_general(
            parts[:, k * 256 : (k + 1) * 256],
            spread,
            (((0,), (0,)), ((), ())),
            preferred_element_type=F32,
        ) * (1.0 / channels)
        value = conv_ref[8 * k : 8 * k + 8].reshape(256, 128)
        v = gain * value * lax.rsqrt(mean_square + EPS)
        hidden = v / (1.0 + jnp.exp(-v))
        whole = (own_ref[8 * k : 8 * k + 8].reshape(256, 128) + hidden).astype(BF)
        cut = whole.reshape(8, HALF, 128)
        skip_ref[8 * k : 8 * k + 8, 0:HALF, :] = cut[:, :, 0:64]
        skip_ref[8 * k : 8 * k + 8, HALF:VOX, :] = cut[:, :, 64:128]
        pooled = jnp.dot(pool_ref[...], whole, preferred_element_type=F32)
        out_ref[slot_ref[0, k]] = pooled.astype(BF)


def place_kernel(place_ref, landed_ref, out_ref):
    parents = out_ref.shape[0]
    for i in range(landed_ref.shape[0]):
        where = place_ref[0, i]

        @pl.when(where < parents)
        def _(i=i, where=where):
            for ox in range(2):
                for px in range(2):
                    row = 16 * (2 * ox + px)
                    out_ref[where, row : row + 16, :] = landed_ref[i, 16 * ox : 16 * ox + 16, 64 * px : 64 * px + 64]


def pool_matrix():
    out = np.zeros((2, 4, 4, 2, 2, 2, 2, 4, 4), np.float32)
    for ox in range(2):
        for y in range(4):
            for z in range(4):
                out[ox, y, z, ox, y // 2, z // 2, :, 2 * (y % 2) : 2 * (y % 2) + 2, 2 * (z % 2) : 2 * (z % 2) + 2] = 0.125
    return out.reshape(32, 256)


VM = pl.BlockSpec(memory_space=pltpu.VMEM)
SM = pl.BlockSpec(memory_space=pltpu.SMEM)
ANY = pl.BlockSpec(memory_space=pl.ANY)
HBM = pl.BlockSpec(memory_space=pltpu.HBM)


def call_rules(n, features, weights, rulebook):
    tile_count, _, channels = features.shape
    offsets, _, quarter = weights.shape
    rule_rows = rulebook.shape[0]
    ways = matchings(n)
    far = [way for way in ways if way[0] > 2]
    near = [way for way in ways if way[0] <= 2]
    slots = tile_count // 4
    span = tile_count * VOX + 2 * PAD
    pairs = (offsets + 1) // 2
    wide = rule_rows + 128
    flat = features.reshape(tile_count * VOX, channels)
    flat_weights = weights.transpose(0, 2, 1).reshape(offsets * quarter, channels)
    block = jax.ShapeDtypeStruct((slots, HALF, 128), BF)
    whole = jax.ShapeDtypeStruct((tile_count, HALF, 128), F32)
    work = [pltpu.VMEM((pairs * span, 128), F32), pltpu.VMEM((tile_count, VOX, 128), F32)]
    flops = 2 * tile_count * VOX * channels * offsets * quarter
    shared = dict(
        compiler_params=pltpu.CompilerParams(vmem_limit_bytes=44 * 1024 * 1024),
        cost_estimate=pl.CostEstimate(flops=flops, bytes_accessed=8 << 20, transcendentals=0),
    )
    made = pl.pallas_call(
        functools.partial(far_kernel, n, far, tile_count),
        out_shape=[block] * len(far)
        + [jax.ShapeDtypeStruct((8, wide), jnp.int32), jax.ShapeDtypeStruct((4 * wide,), jnp.int32)],
        in_specs=[HBM] * 3,
        out_specs=[VM] * (len(far) + 1) + [SM],
        scratch_shapes=work
        + [
            pltpu.VMEM(flat.shape, BF),
            pltpu.VMEM(flat_weights.shape, BF),
            pltpu.VMEM((4, rule_rows), jnp.int32),
            pltpu.SMEM((8, wide), jnp.int32),
            pltpu.SemaphoreType.DMA((4,)),
        ],
        name="far",
        **shared,
    )(rulebook.T, flat, flat_weights)
    far_sends, words, lists = made[: len(far)], made[-2], made[-1]
    near_sends = pl.pallas_call(
        functools.partial(near_kernel, n, near),
        out_shape=[block] * len(near),
        in_specs=[SM, SM, VM, VM],
        out_specs=[VM] * len(near),
        scratch_shapes=work,
        name="near",
        **shared,
    )(words, lists, flat, flat_weights)
    local, own = pl.pallas_call(
        local_kernel,
        out_shape=[whole, whole],
        in_specs=[SM, SM, VM, VM, ANY],
        out_specs=[VM, VM],
        scratch_shapes=work,
        name="local",
        **shared,
    )(words, lists, flat, flat_weights, near_sends[0])
    return list(far_sends) + list(near_sends), local, own


def body(n, features, weights, gain, rulebook, recv_list, coarse_send, coarse_place):
    tile_count, _, channels = features.shape
    quarter = weights.shape[2]
    ways = matchings(n)
    small = pltpu.CompilerParams(vmem_limit_bytes=12 * 1024 * 1024)

    sends, local, own = call_rules(n, features, weights, rulebook)
    arrivals = [lax.ppermute(x, "tiles", way[2]) for x, way in zip(sends, ways)]
    conv, sums = pl.pallas_call(
        functools.partial(combine_kernel, n, ways),
        out_shape=[
            jax.ShapeDtypeStruct((tile_count, HALF, 128), F32),
            jax.ShapeDtypeStruct((2, tile_count * HALF), F32),
        ],
        in_specs=[VM, SM] + [VM] * len(ways),
        out_specs=[VM, VM],
        compiler_params=small,
        name="combine",
    )(local, recv_list, *arrivals)
    wide = lax.axis_size("chan")
    others = [lax.ppermute(sums, "chan", [(i, i ^ m) for i in range(wide)]) for m in range(1, wide)]
    slot_count = coarse_place.shape[1]
    parent_count = tile_count // 8
    skip, outbound = pl.pallas_call(
        functools.partial(norm_kernel, channels),
        out_shape=[
            jax.ShapeDtypeStruct((tile_count, VOX, quarter), BF),
            jax.ShapeDtypeStruct((slot_count, HALF, 128), BF),
        ],
        in_specs=[VM] * 4 + [SM] + [VM] * 4,
        out_specs=[VM, VM],
        compiler_params=small,
        name="norm",
    )(
        conv,
        own,
        jnp.tile(gain.astype(F32), 2).reshape(1, 128),
        jnp.asarray(pool_matrix(), BF),
        coarse_send,
        sums,
        *others,
    )
    landed = lax.all_to_all(outbound, "tiles", split_axis=0, concat_axis=0, tiled=True)
    coarse = pl.pallas_call(
        place_kernel,
        out_shape=jax.ShapeDtypeStruct((parent_count, VOX, quarter), BF),
        in_specs=[SM, VM],
        out_specs=VM,
        compiler_params=small,
        name="place",
    )(coarse_place, landed)
    return (skip, coarse)


def solution(mesh):
    in_specs = (
        P("tiles", None, None),
        P(None, None, "chan"),
        P("chan"),
        P("tiles", None),
        P("tiles", None),
        P("tiles", None),
        P("tiles", None),
    )
    out_specs = (P("tiles", None, "chan"), P("tiles", None, "chan"))
    return jax.shard_map(
        functools.partial(body, mesh.shape["tiles"]),
        mesh=mesh,
        in_specs=in_specs,
        out_specs=out_specs,
        check_vma=False,
    )
```

```python
import functools

import jax
import jax.numpy as jnp
import numpy as np
from jax import lax
from jax.experimental import pallas as pl
from jax.experimental.pallas import tpu as pltpu
from jax.sharding import PartitionSpec as P

EPS = 1e-05
REACH = 4
VOX = 64
HALF = 32
BF = jnp.bfloat16
F32 = jnp.float32
PAD = 64
UNROLL = 8


def matchings(n):
    found = []
    for d in range(REACH, 0, -1):
        for parity in (0, 1):
            pairs = [(i, i + d) for i in range(n - d) if (i // d) % 2 == parity]
            if pairs:
                rest = [i for i in range(n) if all(i not in p for p in pairs)]
                fill = list(zip(rest[::2], rest[1::2]))
                both = pairs + fill
                found.append((d, parity, both + [(b, a) for a, b in both]))
    return found


def role(e, n, d, parity):
    low = jnp.logical_and(lax.rem(lax.div(e, d), 2) == parity, e + d < n)
    high = jnp.logical_and(e >= d, lax.rem(lax.div(jnp.maximum(e - d, 0), d), 2) == parity)
    return low, high


def lane_iota(shape):
    return lax.broadcasted_iota(jnp.int32, shape, len(shape) - 1)


def dims_of(code):
    return (lax.div(code, 9) - 1, lax.rem(lax.div(code, 3), 3) - 1, lax.rem(code, 3) - 1)


def rules_matmul(f_ref, w_ref, y_ref, beside=None):
    rows = f_ref.shape[0]
    span = rows + 2 * PAD
    depth = w_ref.shape[0]
    steps = range(0, depth, 256)
    for number, q in enumerate(steps):
        width = min(256, depth - q)
        part = lax.dot_general(
            f_ref[...],
            w_ref[q : q + width, :],
            (((1,), (1,)), ((), ())),
            preferred_element_type=F32,
        )
        for s in range(0, width, 128):
            wide = min(128, width - s)
            base = ((q + s) // 128) * span + PAD
            y_ref[base : base + rows, 0:wide] = part[:, s : s + wide]
        if beside is not None:
            beside(number, len(steps))


def rules_add(words, lists, start, count, y_ref, acc_ref):
    voxel = lax.broadcasted_iota(jnp.int32, (VOX, 128), 0)
    have = jnp.where(lane_iota((VOX, 128)) < 64, 1 << 21, 1 << 22)
    for dim, place in enumerate((lax.div(voxel, 16), lax.rem(lax.div(voxel, 4), 4), lax.rem(voxel, 4))):
        have = have + jnp.left_shift(jnp.full_like(place, 15), 3 - place + 7 * dim)

    def several(i, c):
        for u in range(UNROLL):
            r = lists[start + i * UNROLL + u]
            packed = words[0, r]
            need = words[1, r]
            taken = y_ref[pl.ds(lax.shift_right_logical(packed, 8), VOX), :]
            t = packed & 255
            acc_ref[t] = acc_ref[t] + jnp.where((have & need) == need, taken, 0.0)
        return c

    lax.fori_loop(0, lax.div(count + (UNROLL - 1), UNROLL), several, 0)


def zero_blocks(acc_ref):
    def zero(i, c):
        acc_ref[i] = jnp.zeros((VOX, 128), F32)
        return c

    lax.fori_loop(0, acc_ref.shape[0], zero, 0, unroll=8)


def folded(acc_ref, t):
    first = lane_iota((HALF, 128)) < 64
    low = acc_ref[t, 0:HALF, :]
    high = acc_ref[t, HALF:VOX, :]
    low = low + pltpu.roll(low, 64, 1)
    high = high + pltpu.roll(high, 64, 1)
    return jnp.where(first, low, high)


def emit_sends(n, ways, acc_ref, sends):
    e = lax.axis_index("tiles")
    slots = sends[0].shape[0]
    for (d, parity, _), send_ref in zip(ways, sends):
        low, _high = role(e, n, d, parity)
        base = slots * ((d - 1) % 2 + jnp.where(low, 0, 2))

        def emit(i, c, send_ref=send_ref, base=base):
            send_ref[i] = folded(acc_ref, base + i).astype(BF)
            return c

        lax.fori_loop(0, slots, emit, 0, unroll=16)


def far_kernel(n, ways, tile_count, rules_hbm, f_hbm, w_hbm, *rest):
    sends = rest[: len(ways)]
    f_ref, w_ref, words_v, lists, y_ref, acc_ref, rules_ref, words_s, sems = rest[len(ways) :]
    rows = tile_count * VOX
    span = rows + 2 * PAD
    rule_rows = rules_ref.shape[1]
    wide = words_v.shape[1]
    slots = tile_count // 4
    copies = [
        pltpu.make_async_copy(src, dst, sems.at[i])
        for i, (src, dst) in enumerate(((rules_hbm, rules_ref), (w_hbm, w_ref), (f_hbm, f_ref)))
    ]
    for copy in copies:
        copy.start()
    before = lax.broadcasted_iota(jnp.int32, (rule_rows, rule_rows), 0)
    before = (before <= lane_iota((rule_rows, rule_rows))).astype(F32).astype(BF)
    zero_blocks(acc_ref)
    copies[0].wait()
    tile = rules_ref[0:1, :]
    kernel = rules_ref[1:2, :]
    heading = rules_ref[2:3, :]
    target = rules_ref[3:4, :]
    code = jnp.minimum(kernel, 26)
    shift = jnp.zeros_like(code)
    need = jnp.where(lax.rem(code, 2) == 0, 1 << 21, 1 << 22)
    for dim, (step, turn) in enumerate(zip(dims_of(code), dims_of(heading))):
        move = step - 4 * turn
        shift = shift + move * (16, 4, 1)[dim]
        need = need + jnp.left_shift(jnp.full_like(move, 1), move + (3 + 7 * dim))
    sent = jnp.maximum(target - tile_count, 0)
    group = lax.div(sent, slots)
    place = (lax.div(group, 4) * 2 + lax.rem(group, 2)) * slots + lax.rem(sent, slots)
    near = lax.rem(group, 4) < 2
    part = jnp.where(target < tile_count, 2, jnp.where(near, 1, 0))
    part = jnp.where(kernel < 27, part, 3)
    kind = lax.broadcasted_iota(jnp.int32, (8, rule_rows), 0)
    flags = jnp.where(kind == part, 1.0, 0.0)
    upto = jnp.dot(flags.astype(BF), before, preferred_element_type=F32)
    at = jnp.sum(flags * (upto - 1.0 + (kind * wide).astype(F32)), axis=0, keepdims=True)
    first_row = lax.div(code, 2) * span + PAD + tile * VOX + shift
    words_v[...] = jnp.zeros(words_v.shape, jnp.int32)
    words_v[0:1, 0:rule_rows] = first_row * 256 + jnp.where(target < tile_count, target, place)
    words_v[1:2, 0:rule_rows] = need
    words_v[2:3, 0:rule_rows] = at.astype(jnp.int32)
    words_v[0:1, rule_rows:wide] = jnp.full((1, wide - rule_rows), PAD * 256, jnp.int32)
    words_v[1:2, rule_rows:wide] = jnp.full((1, wide - rule_rows), 1 << 23, jnp.int32)
    totals = jnp.broadcast_to(upto[0:3, rule_rows - 1 : rule_rows], (3, 128))
    words_v[3:6, 0:128] = totals.astype(jnp.int32)
    to_scalars = pltpu.make_async_copy(words_v, words_s, sems.at[3])
    to_scalars.start()
    to_scalars.wait()
    copies[1].wait()
    copies[2].wait()

    def list_some(number, count):
        share = -(-rule_rows // count)
        for r in range(number * share, min(rule_rows, (number + 1) * share)):
            lists[words_s[2, r]] = r

    rules_matmul(f_ref, w_ref, y_ref, list_some)
    for c in range(3):
        for u in range(UNROLL):
            lists[c * wide + words_s[3 + c, 0] + u] = rule_rows
    rules_add(words_s, lists, 0, words_s[3, 0], y_ref, acc_ref)
    emit_sends(n, ways, acc_ref, sends)


def near_kernel(n, ways, words, lists, f_ref, w_ref, *rest):
    sends = rest[: len(ways)]
    y_ref, acc_ref = rest[len(ways) :]
    zero_blocks(acc_ref)
    rules_matmul(f_ref, w_ref, y_ref)
    rules_add(words, lists, words.shape[1], words[4, 0], y_ref, acc_ref)
    emit_sends(n, ways, acc_ref, sends)


def add_arrivals(n, ways, blocks, list_ref, out_ref):
    e = lax.axis_index("tiles")
    slots = blocks[0].shape[0]
    for (d, parity, _), block in zip(ways, blocks):
        low, high = role(e, n, d, parity)
        base = slots * jnp.where(low, d + 3, d - 1)

        @pl.when(jnp.logical_or(low, high))
        def _(block=block, base=base):
            for i in range(slots):
                t = list_ref[0, base + i]
                out_ref[t] = out_ref[t] + block[i].astype(F32)


def local_kernel(n, ways, words, lists, list_ref, f_ref, w_ref, *rest):
    blocks = rest[: len(ways)]
    local_ref, own_ref, y_ref, acc_ref = rest[len(ways) :]
    tile_count = acc_ref.shape[0]
    zero_blocks(acc_ref)
    rules_matmul(f_ref, w_ref, y_ref)
    rules_add(words, lists, 2 * words.shape[1], words[5, 0], y_ref, acc_ref)
    c = lax.axis_index("chan")
    at = pl.multiple_of(lax.div(c, 2) * 128, 128)
    odd = lax.rem(c, 2) == 1
    first = lane_iota((HALF, 128)) < 64

    def keep(t, c):
        local_ref[t] = folded(acc_ref, t)
        block = f_ref[pl.ds(pl.multiple_of(t * VOX, VOX), VOX), pl.ds(at, 128)].astype(F32)
        low, high = block[:HALF], block[HALF:]
        even_form = jnp.where(first, low, pltpu.roll(high, 64, 1))
        odd_form = jnp.where(first, pltpu.roll(low, 64, 1), high)
        own_ref[t] = jnp.where(odd, odd_form, even_form)
        return c

    lax.fori_loop(0, tile_count, keep, 0, unroll=8)
    add_arrivals(n, ways, blocks, list_ref, local_ref)


def combine_kernel(n, ways, local_ref, list_ref, *rest):
    blocks = rest[: len(ways)]
    conv_ref, sums_ref = rest[len(ways) :]
    tile_count = local_ref.shape[0]
    conv_ref[...] = local_ref[...]
    add_arrivals(n, ways, blocks, list_ref, conv_ref)
    rows = tile_count * HALF
    pick = (lane_iota((2, 256)) // 64 % 2 == lax.broadcasted_iota(jnp.int32, (2, 256), 0)).astype(BF)
    step = 512
    for at in range(0, rows, step):
        value = conv_ref[at // HALF : (at + step) // HALF].reshape(step, 128)
        square = value * value
        top = square.astype(BF)
        rest_of = (square - top.astype(F32)).astype(BF)
        sums_ref[:, at : at + step] = lax.dot_general(
            pick,
            jnp.concatenate([top, rest_of], axis=1),
            (((1,), (1,)), ((), ())),
            preferred_element_type=F32,
        )


def norm_kernel(channels, conv_ref, own_ref, gain_ref, pool_ref, slot_ref, s0, s1, s2, s3, skip_ref, out_ref):
    tile_count = conv_ref.shape[0]
    total = jnp.concatenate([s0[...], s1[...], s2[...], s3[...]], axis=0)
    parts = []
    for _ in range(3):
        top = total.astype(BF)
        parts.append(top.astype(F32))
        total = total - top.astype(F32)
    parts = jnp.concatenate(parts, axis=0).astype(BF)
    count = parts.shape[0]
    spread = (lane_iota((count, 128)) // 64 == lax.broadcasted_iota(jnp.int32, (count, 128), 0) % 2).astype(BF)
    gain = gain_ref[...]
    for k in range(tile_count // 8):
        mean_square = lax.dot_general(
            parts[:, k * 256 : (k + 1) * 256],
            spread,
            (((0,), (0,)), ((), ())),
            preferred_element_type=F32,
        ) * (1.0 / channels)
        value = conv_ref[8 * k : 8 * k + 8].reshape(256, 128)
        v = gain * value * lax.rsqrt(mean_square + EPS)
        hidden = v / (1.0 + jnp.exp(-v))
        whole = (own_ref[8 * k : 8 * k + 8].reshape(256, 128) + hidden).astype(BF)
        cut = whole.reshape(8, HALF, 128)
        skip_ref[8 * k : 8 * k + 8, 0:HALF, :] = cut[:, :, 0:64]
        skip_ref[8 * k : 8 * k + 8, HALF:VOX, :] = cut[:, :, 64:128]
        pooled = jnp.dot(pool_ref[...], whole, preferred_element_type=F32)
        out_ref[slot_ref[0, k]] = pooled.astype(BF)


def place_kernel(place_ref, landed_ref, out_ref):
    parents = out_ref.shape[0]
    for i in range(landed_ref.shape[0]):
        where = place_ref[0, i]

        @pl.when(where < parents)
        def _(i=i, where=where):
            for ox in range(2):
                for px in range(2):
                    row = 16 * (2 * ox + px)
                    out_ref[where, row : row + 16, :] = landed_ref[i, 16 * ox : 16 * ox + 16, 64 * px : 64 * px + 64]


def pool_matrix():
    out = np.zeros((2, 4, 4, 2, 2, 2, 2, 4, 4), np.float32)
    for ox in range(2):
        for y in range(4):
            for z in range(4):
                out[ox, y, z, ox, y // 2, z // 2, :, 2 * (y % 2) : 2 * (y % 2) + 2, 2 * (z % 2) : 2 * (z % 2) + 2] = 0.125
    return out.reshape(32, 256)


VM = pl.BlockSpec(memory_space=pltpu.VMEM)
SM = pl.BlockSpec(memory_space=pltpu.SMEM)
ANY = pl.BlockSpec(memory_space=pl.ANY)
HBM = pl.BlockSpec(memory_space=pltpu.HBM)


def call_rules(n, features, weights, rulebook, recv_list):
    tile_count, _, channels = features.shape
    offsets, _, quarter = weights.shape
    rule_rows = rulebook.shape[0]
    ways = matchings(n)
    far = [way for way in ways if way[0] > 2]
    near = [way for way in ways if way[0] <= 2]
    slots = tile_count // 4
    span = tile_count * VOX + 2 * PAD
    pairs = (offsets + 1) // 2
    wide = rule_rows + 128
    flat = features.reshape(tile_count * VOX, channels)
    flat_weights = weights.transpose(0, 2, 1).reshape(offsets * quarter, channels)
    block = jax.ShapeDtypeStruct((slots, HALF, 128), BF)
    whole = jax.ShapeDtypeStruct((tile_count, HALF, 128), F32)
    work = [pltpu.VMEM((pairs * span, 128), F32), pltpu.VMEM((tile_count, VOX, 128), F32)]
    flops = 2 * tile_count * VOX * channels * offsets * quarter
    shared = dict(
        compiler_params=pltpu.CompilerParams(vmem_limit_bytes=44 * 1024 * 1024),
        cost_estimate=pl.CostEstimate(flops=flops, bytes_accessed=8 << 20, transcendentals=0),
    )
    made = pl.pallas_call(
        functools.partial(far_kernel, n, far, tile_count),
        out_shape=[block] * len(far)
        + [jax.ShapeDtypeStruct(flat.shape, BF), jax.ShapeDtypeStruct(flat_weights.shape, BF)]
        + [jax.ShapeDtypeStruct((8, wide), jnp.int32), jax.ShapeDtypeStruct((4 * wide,), jnp.int32)],
        in_specs=[HBM] * 3,
        out_specs=[VM] * (len(far) + 3) + [SM],
        scratch_shapes=work
        + [
            pltpu.VMEM((4, rule_rows), jnp.int32),
            pltpu.SMEM((8, wide), jnp.int32),
            pltpu.SemaphoreType.DMA((4,)),
        ],
        name="far",
        **shared,
    )(*(pltpu.with_memory_space_constraint(x, pltpu.HBM) for x in (rulebook.T, flat, flat_weights)))
    far_sends = made[: len(far)]
    held, held_weights, words, lists = made[len(far) :]
    arrivals = [lax.ppermute(x, "tiles", way[2]) for x, way in zip(far_sends, far)]
    near_sends = pl.pallas_call(
        functools.partial(near_kernel, n, near),
        out_shape=[block] * len(near),
        in_specs=[SM, SM, VM, VM],
        out_specs=[VM] * len(near),
        scratch_shapes=work,
        name="near",
        **shared,
    )(words, lists, held, held_weights)
    near_arrivals = [lax.ppermute(x, "tiles", way[2]) for x, way in zip(near_sends, near)]
    local, own = pl.pallas_call(
        functools.partial(local_kernel, n, far),
        out_shape=[whole, whole],
        in_specs=[SM, SM, SM, VM, VM] + [VM] * len(far),
        out_specs=[VM, VM],
        scratch_shapes=work,
        name="local",
        **shared,
    )(words, lists, recv_list, held, held_weights, *arrivals)
    return near, near_arrivals, local, own


def body(n, features, weights, gain, rulebook, recv_list, coarse_send, coarse_place):
    tile_count, _, channels = features.shape
    quarter = weights.shape[2]
    small = pltpu.CompilerParams(vmem_limit_bytes=12 * 1024 * 1024)

    near, arrivals, local, own = call_rules(n, features, weights, rulebook, recv_list)
    conv, sums = pl.pallas_call(
        functools.partial(combine_kernel, n, near),
        out_shape=[
            jax.ShapeDtypeStruct((tile_count, HALF, 128), F32),
            jax.ShapeDtypeStruct((2, tile_count * HALF), F32),
        ],
        in_specs=[VM, SM] + [VM] * len(near),
        out_specs=[VM, VM],
        compiler_params=small,
        name="combine",
    )(local, recv_list, *arrivals)
    wide = lax.axis_size("chan")
    others = [lax.ppermute(sums, "chan", [(i, i ^ m) for i in range(wide)]) for m in range(1, wide)]
    slot_count = coarse_place.shape[1]
    parent_count = tile_count // 8
    skip, outbound = pl.pallas_call(
        functools.partial(norm_kernel, channels),
        out_shape=[
            jax.ShapeDtypeStruct((tile_count, VOX, quarter), BF),
            jax.ShapeDtypeStruct((slot_count, HALF, 128), BF),
        ],
        in_specs=[VM] * 4 + [SM] + [VM] * 4,
        out_specs=[VM, VM],
        compiler_params=small,
        name="norm",
    )(
        conv,
        own,
        jnp.tile(gain.astype(F32), 2).reshape(1, 128),
        jnp.asarray(pool_matrix(), BF),
        coarse_send,
        sums,
        *others,
    )
    landed = lax.all_to_all(outbound, "tiles", split_axis=0, concat_axis=0, tiled=True)
    coarse = pl.pallas_call(
        place_kernel,
        out_shape=jax.ShapeDtypeStruct((parent_count, VOX, quarter), BF),
        in_specs=[SM, VM],
        out_specs=VM,
        compiler_params=small,
        name="place",
    )(coarse_place, landed)
    return (skip, coarse)


def solution(mesh):
    in_specs = (
        P("tiles", None, None),
        P(None, None, "chan"),
        P("chan"),
        P("tiles", None),
        P("tiles", None),
        P("tiles", None),
        P("tiles", None),
    )
    out_specs = (P("tiles", None, "chan"), P("tiles", None, "chan"))
    return jax.shard_map(
        functools.partial(body, mesh.shape["tiles"]),
        mesh=mesh,
        in_specs=in_specs,
        out_specs=out_specs,
        check_vma=False,
    )
```

```python
import functools

import jax
import jax.numpy as jnp
import numpy as np
from jax import lax
from jax.experimental import pallas as pl
from jax.experimental.pallas import tpu as pltpu
from jax.sharding import PartitionSpec as P

EPS = 1e-05
REACH = 4
VOX = 64
HALF = 32
BF = jnp.bfloat16
F32 = jnp.float32
PAD = 64
UNROLL = 8
PARTS = 2
PER_PART = 7


def matchings(n):
    found = []
    for d in range(REACH, 0, -1):
        for parity in (0, 1):
            pairs = [(i, i + d) for i in range(n - d) if (i // d) % 2 == parity]
            if pairs:
                rest = [i for i in range(n) if all(i not in p for p in pairs)]
                fill = list(zip(rest[::2], rest[1::2]))
                both = pairs + fill
                found.append((d, parity, both + [(b, a) for a, b in both]))
    return found


def role(e, n, d, parity):
    low = jnp.logical_and(lax.rem(lax.div(e, d), 2) == parity, e + d < n)
    high = jnp.logical_and(e >= d, lax.rem(lax.div(jnp.maximum(e - d, 0), d), 2) == parity)
    return low, high


def lane_iota(shape):
    return lax.broadcasted_iota(jnp.int32, shape, len(shape) - 1)


def dims_of(code):
    return (lax.div(code, 9) - 1, lax.rem(lax.div(code, 3), 3) - 1, lax.rem(code, 3) - 1)


def rules_matmul(f_ref, w_ref, y_refs, beside=None):
    rows = f_ref.shape[0]
    span = rows + 2 * PAD
    depth = w_ref.shape[0]
    steps = range(0, depth, 256)
    for number, q in enumerate(steps):
        width = min(256, depth - q)
        part = lax.dot_general(
            f_ref[...],
            w_ref[q : q + width, :],
            (((1,), (1,)), ((), ())),
            preferred_element_type=F32,
        )
        for s in range(0, width, 128):
            wide = min(128, width - s)
            y_ref = y_refs[(q + s) // 128 // PER_PART]
            base = ((q + s) // 128 % PER_PART) * span + PAD
            y_ref[base : base + rows, 0:wide] = part[:, s : s + wide]
        if beside is not None:
            beside(number, len(steps))


def rules_add(words, lists, part, y_refs, acc_ref):
    voxel = lax.broadcasted_iota(jnp.int32, (VOX, 128), 0)
    have = jnp.where(lane_iota((VOX, 128)) < 64, 1 << 21, 1 << 22)
    for dim, place in enumerate((lax.div(voxel, 16), lax.rem(lax.div(voxel, 4), 4), lax.rem(voxel, 4))):
        have = have + jnp.left_shift(jnp.full_like(place, 15), 3 - place + 7 * dim)

    for which, y_ref in enumerate(y_refs):
        kind = part * PARTS + which
        add_listed(words, lists, kind * words.shape[1], words[3, 128 * kind], have, y_ref, acc_ref)


def add_listed(words, lists, start, count, have, y_ref, acc_ref):
    def several(i, c):
        for u in range(UNROLL):
            r = lists[start + i * UNROLL + u]
            packed = words[0, r]
            need = words[1, r]
            taken = y_ref[pl.ds(lax.shift_right_logical(packed, 8), VOX), :]
            t = packed & 255
            acc_ref[t] = acc_ref[t] + jnp.where((have & need) == need, taken, 0.0)
        return c

    lax.fori_loop(0, lax.div(count + (UNROLL - 1), UNROLL), several, 0)


def zero_blocks(acc_ref):
    def zero(i, c):
        acc_ref[i] = jnp.zeros((VOX, 128), F32)
        return c

    lax.fori_loop(0, acc_ref.shape[0], zero, 0, unroll=8)


def folded(acc_ref, t):
    first = lane_iota((HALF, 128)) < 64
    low = acc_ref[t, 0:HALF, :]
    high = acc_ref[t, HALF:VOX, :]
    low = low + pltpu.roll(low, 64, 1)
    high = high + pltpu.roll(high, 64, 1)
    return jnp.where(first, low, high)


def emit_sends(n, ways, acc_ref, sends):
    e = lax.axis_index("tiles")
    slots = sends[0].shape[0]
    for (d, parity, _), send_ref in zip(ways, sends):
        low, _high = role(e, n, d, parity)
        base = slots * ((d - 1) % 2 + jnp.where(low, 0, 2))

        def emit(i, c, send_ref=send_ref, base=base):
            send_ref[i] = folded(acc_ref, base + i).astype(BF)
            return c

        lax.fori_loop(0, slots, emit, 0, unroll=16)


def far_kernel(n, ways, tile_count, rules_hbm, f_hbm, w_hbm, *rest):
    sends = rest[: len(ways)]
    f_ref = rest[len(ways)]
    y_refs = rest[len(ways) + 1 : len(ways) + 1 + PARTS]
    words_v, lists, acc_ref, w_ref, rules_ref, words_s, sems = rest[len(ways) + 1 + PARTS :]
    rows = tile_count * VOX
    span = rows + 2 * PAD
    rule_rows = rules_ref.shape[1]
    wide = words_v.shape[1]
    slots = tile_count // 4
    copies = [
        pltpu.make_async_copy(src, dst, sems.at[i])
        for i, (src, dst) in enumerate(((rules_hbm, rules_ref), (w_hbm, w_ref), (f_hbm, f_ref)))
    ]
    for copy in copies:
        copy.start()
    before = lax.broadcasted_iota(jnp.int32, (rule_rows, rule_rows), 0)
    before = (before <= lane_iota((rule_rows, rule_rows))).astype(F32).astype(BF)
    zero_blocks(acc_ref)
    copies[0].wait()
    tile = rules_ref[0:1, :]
    kernel = rules_ref[1:2, :]
    heading = rules_ref[2:3, :]
    target = rules_ref[3:4, :]
    code = jnp.minimum(kernel, 26)
    shift = jnp.zeros_like(code)
    need = jnp.where(lax.rem(code, 2) == 0, 1 << 21, 1 << 22)
    for dim, (step, turn) in enumerate(zip(dims_of(code), dims_of(heading))):
        move = step - 4 * turn
        shift = shift + move * (16, 4, 1)[dim]
        need = need + jnp.left_shift(jnp.full_like(move, 1), move + (3 + 7 * dim))
    sent = jnp.maximum(target - tile_count, 0)
    group = lax.div(sent, slots)
    place = (lax.div(group, 4) * 2 + lax.rem(group, 2)) * slots + lax.rem(sent, slots)
    near = lax.rem(group, 4) < 2
    part = jnp.where(target < tile_count, 2, jnp.where(near, 1, 0))
    pair = lax.div(code, 2)
    part = jnp.where(kernel < 27, part * PARTS + lax.div(pair, PER_PART), 3 * PARTS)
    kind = lax.broadcasted_iota(jnp.int32, (8, rule_rows), 0)
    flags = jnp.where(kind == part, 1.0, 0.0)
    upto = jnp.dot(flags.astype(BF), before, preferred_element_type=F32)
    at = jnp.sum(flags * (upto - 1.0 + (kind * wide).astype(F32)), axis=0, keepdims=True)
    first_row = lax.rem(pair, PER_PART) * span + PAD + tile * VOX + shift
    words_v[...] = jnp.zeros(words_v.shape, jnp.int32)
    words_v[0:1, 0:rule_rows] = first_row * 256 + jnp.where(target < tile_count, target, place)
    words_v[1:2, 0:rule_rows] = need
    words_v[2:3, 0:rule_rows] = at.astype(jnp.int32)
    words_v[0:1, rule_rows:wide] = jnp.full((1, wide - rule_rows), PAD * 256, jnp.int32)
    words_v[1:2, rule_rows:wide] = jnp.full((1, wide - rule_rows), 1 << 23, jnp.int32)
    for c in range(3 * PARTS):
        total = upto[c : c + 1, rule_rows - 1 : rule_rows]
        words_v[3:4, 128 * c : 128 * c + 128] = jnp.broadcast_to(total, (1, 128)).astype(jnp.int32)
    to_scalars = pltpu.make_async_copy(words_v, words_s, sems.at[3])
    to_scalars.start()
    to_scalars.wait()
    copies[1].wait()
    copies[2].wait()

    def list_some(number, count):
        share = -(-rule_rows // count)
        for r in range(number * share, min(rule_rows, (number + 1) * share)):
            lists[words_s[2, r]] = r

    rules_matmul(f_ref, w_ref, y_refs, list_some)
    for c in range(3 * PARTS):
        for u in range(UNROLL):
            lists[c * wide + words_s[3, 128 * c] + u] = rule_rows
    rules_add(words_s, lists, 0, y_refs, acc_ref)
    emit_sends(n, ways, acc_ref, sends)


def near_kernel(n, ways, words, lists, *rest):
    y_refs, rest = rest[:PARTS], rest[PARTS:]
    sends = rest[: len(ways)]
    acc_ref = rest[len(ways)]
    zero_blocks(acc_ref)
    rules_add(words, lists, 1, y_refs, acc_ref)
    emit_sends(n, ways, acc_ref, sends)


def add_arrivals(n, ways, blocks, list_ref, out_ref):
    e = lax.axis_index("tiles")
    slots = blocks[0].shape[0]
    for (d, parity, _), block in zip(ways, blocks):
        low, high = role(e, n, d, parity)
        base = slots * jnp.where(low, d + 3, d - 1)

        @pl.when(jnp.logical_or(low, high))
        def _(block=block, base=base):
            for i in range(slots):
                t = list_ref[0, base + i]
                out_ref[t] = out_ref[t] + block[i].astype(F32)


def local_kernel(n, ways, words, lists, list_ref, f_ref, *rest):
    y_refs, rest = rest[:PARTS], rest[PARTS:]
    blocks = rest[: len(ways)]
    local_ref, own_ref, acc_ref = rest[len(ways) :]
    tile_count = acc_ref.shape[0]
    zero_blocks(acc_ref)
    rules_add(words, lists, 2, y_refs, acc_ref)
    c = lax.axis_index("chan")
    at = pl.multiple_of(lax.div(c, 2) * 128, 128)
    odd = lax.rem(c, 2) == 1
    first = lane_iota((HALF, 128)) < 64

    def keep(t, c):
        local_ref[t] = folded(acc_ref, t)
        block = f_ref[pl.ds(pl.multiple_of(t * VOX, VOX), VOX), pl.ds(at, 128)].astype(F32)
        low, high = block[:HALF], block[HALF:]
        even_form = jnp.where(first, low, pltpu.roll(high, 64, 1))
        odd_form = jnp.where(first, pltpu.roll(low, 64, 1), high)
        own_ref[t] = jnp.where(odd, odd_form, even_form)
        return c

    lax.fori_loop(0, tile_count, keep, 0, unroll=8)
    add_arrivals(n, ways, blocks, list_ref, local_ref)


def combine_kernel(n, ways, local_ref, list_ref, *rest):
    blocks = rest[: len(ways)]
    conv_ref, sums_ref = rest[len(ways) :]
    tile_count = local_ref.shape[0]
    conv_ref[...] = local_ref[...]
    add_arrivals(n, ways, blocks, list_ref, conv_ref)
    rows = tile_count * HALF
    pick = (lane_iota((2, 256)) // 64 % 2 == lax.broadcasted_iota(jnp.int32, (2, 256), 0)).astype(BF)
    step = 512
    for at in range(0, rows, step):
        value = conv_ref[at // HALF : (at + step) // HALF].reshape(step, 128)
        square = value * value
        top = square.astype(BF)
        rest_of = (square - top.astype(F32)).astype(BF)
        sums_ref[:, at : at + step] = lax.dot_general(
            pick,
            jnp.concatenate([top, rest_of], axis=1),
            (((1,), (1,)), ((), ())),
            preferred_element_type=F32,
        )


def norm_kernel(channels, conv_ref, own_ref, gain_ref, pool_ref, slot_ref, s0, s1, s2, s3, skip_ref, out_ref):
    tile_count = conv_ref.shape[0]
    total = jnp.concatenate([s0[...], s1[...], s2[...], s3[...]], axis=0)
    parts = []
    for _ in range(3):
        top = total.astype(BF)
        parts.append(top.astype(F32))
        total = total - top.astype(F32)
    parts = jnp.concatenate(parts, axis=0).astype(BF)
    count = parts.shape[0]
    spread = (lane_iota((count, 128)) // 64 == lax.broadcasted_iota(jnp.int32, (count, 128), 0) % 2).astype(BF)
    gain = gain_ref[...]
    for k in range(tile_count // 8):
        mean_square = lax.dot_general(
            parts[:, k * 256 : (k + 1) * 256],
            spread,
            (((0,), (0,)), ((), ())),
            preferred_element_type=F32,
        ) * (1.0 / channels)
        value = conv_ref[8 * k : 8 * k + 8].reshape(256, 128)
        v = gain * value * lax.rsqrt(mean_square + EPS)
        hidden = v / (1.0 + jnp.exp(-v))
        whole = (own_ref[8 * k : 8 * k + 8].reshape(256, 128) + hidden).astype(BF)
        cut = whole.reshape(8, HALF, 128)
        skip_ref[8 * k : 8 * k + 8, 0:HALF, :] = cut[:, :, 0:64]
        skip_ref[8 * k : 8 * k + 8, HALF:VOX, :] = cut[:, :, 64:128]
        pooled = jnp.dot(pool_ref[...], whole, preferred_element_type=F32)
        out_ref[slot_ref[0, k]] = pooled.astype(BF)


def place_kernel(place_ref, landed_ref, out_ref):
    parents = out_ref.shape[0]
    for i in range(landed_ref.shape[0]):
        where = place_ref[0, i]

        @pl.when(where < parents)
        def _(i=i, where=where):
            for ox in range(2):
                for px in range(2):
                    row = 16 * (2 * ox + px)
                    out_ref[where, row : row + 16, :] = landed_ref[i, 16 * ox : 16 * ox + 16, 64 * px : 64 * px + 64]


def pool_matrix():
    out = np.zeros((2, 4, 4, 2, 2, 2, 2, 4, 4), np.float32)
    for ox in range(2):
        for y in range(4):
            for z in range(4):
                out[ox, y, z, ox, y // 2, z // 2, :, 2 * (y % 2) : 2 * (y % 2) + 2, 2 * (z % 2) : 2 * (z % 2) + 2] = 0.125
    return out.reshape(32, 256)


VM = pl.BlockSpec(memory_space=pltpu.VMEM)
SM = pl.BlockSpec(memory_space=pltpu.SMEM)
ANY = pl.BlockSpec(memory_space=pl.ANY)
HBM = pl.BlockSpec(memory_space=pltpu.HBM)


def call_rules(n, features, weights, rulebook, recv_list):
    tile_count, _, channels = features.shape
    offsets, _, quarter = weights.shape
    rule_rows = rulebook.shape[0]
    ways = matchings(n)
    far = [way for way in ways if way[0] > 2]
    near = [way for way in ways if way[0] <= 2]
    slots = tile_count // 4
    span = tile_count * VOX + 2 * PAD
    wide = rule_rows + 128
    flat = features.reshape(tile_count * VOX, channels)
    flat_weights = weights.transpose(0, 2, 1).reshape(offsets * quarter, channels)
    block = jax.ShapeDtypeStruct((slots, HALF, 128), BF)
    whole = jax.ShapeDtypeStruct((tile_count, HALF, 128), F32)
    work = [pltpu.VMEM((tile_count, VOX, 128), F32)]
    flops = 2 * tile_count * VOX * channels * offsets * quarter
    shared = dict(
        compiler_params=pltpu.CompilerParams(vmem_limit_bytes=16 * 1024 * 1024),
        cost_estimate=pl.CostEstimate(flops=flops, bytes_accessed=8 << 20, transcendentals=0),
    )
    made = pl.pallas_call(
        functools.partial(far_kernel, n, far, tile_count),
        out_shape=[block] * len(far)
        + [jax.ShapeDtypeStruct(flat.shape, BF), jax.ShapeDtypeStruct((PER_PART * span, 128), F32)]
        + [jax.ShapeDtypeStruct((PER_PART * span, 128), F32)] * (PARTS - 1)
        + [jax.ShapeDtypeStruct((8, wide), jnp.int32), jax.ShapeDtypeStruct(((3 * PARTS + 1) * wide,), jnp.int32)],
        in_specs=[HBM] * 3,
        out_specs=[VM] * (len(far) + 2 + PARTS) + [SM],
        scratch_shapes=work
        + [
            pltpu.VMEM(flat_weights.shape, BF),
            pltpu.VMEM((4, rule_rows), jnp.int32),
            pltpu.SMEM((8, wide), jnp.int32),
            pltpu.SemaphoreType.DMA((4,)),
        ],
        name="far",
        **shared,
    )(*(pltpu.with_memory_space_constraint(x, pltpu.HBM) for x in (rulebook.T, flat, flat_weights)))
    far_sends = made[: len(far)]
    held, *products, words, lists = made[len(far) :]
    arrivals = [lax.ppermute(x, "tiles", way[2]) for x, way in zip(far_sends, far)]
    near_sends = pl.pallas_call(
        functools.partial(near_kernel, n, near),
        out_shape=[block] * len(near),
        in_specs=[SM, SM] + [VM] * PARTS,
        out_specs=[VM] * len(near),
        scratch_shapes=work,
        name="near",
        **shared,
    )(words, lists, *products)
    near_arrivals = [lax.ppermute(x, "tiles", way[2]) for x, way in zip(near_sends, near)]
    local, own = pl.pallas_call(
        functools.partial(local_kernel, n, far),
        out_shape=[whole, whole],
        in_specs=[SM, SM, SM, VM] + [VM] * (PARTS + len(far)),
        out_specs=[VM, VM],
        scratch_shapes=work,
        name="local",
        **shared,
    )(words, lists, recv_list, held, *products, *arrivals)
    return near, near_arrivals, local, own


def body(n, features, weights, gain, rulebook, recv_list, coarse_send, coarse_place):
    tile_count, _, channels = features.shape
    quarter = weights.shape[2]
    small = pltpu.CompilerParams(vmem_limit_bytes=12 * 1024 * 1024)

    near, arrivals, local, own = call_rules(n, features, weights, rulebook, recv_list)
    conv, sums = pl.pallas_call(
        functools.partial(combine_kernel, n, near),
        out_shape=[
            jax.ShapeDtypeStruct((tile_count, HALF, 128), F32),
            jax.ShapeDtypeStruct((2, tile_count * HALF), F32),
        ],
        in_specs=[VM, SM] + [VM] * len(near),
        out_specs=[VM, VM],
        compiler_params=small,
        name="combine",
    )(local, recv_list, *arrivals)
    wide = lax.axis_size("chan")
    others = [lax.ppermute(sums, "chan", [(i, i ^ m) for i in range(wide)]) for m in range(1, wide)]
    slot_count = coarse_place.shape[1]
    parent_count = tile_count // 8
    skip, outbound = pl.pallas_call(
        functools.partial(norm_kernel, channels),
        out_shape=[
            jax.ShapeDtypeStruct((tile_count, VOX, quarter), BF),
            jax.ShapeDtypeStruct((slot_count, HALF, 128), BF),
        ],
        in_specs=[VM] * 4 + [SM] + [VM] * 4,
        out_specs=[VM, VM],
        compiler_params=small,
        name="norm",
    )(
        conv,
        own,
        jnp.tile(gain.astype(F32), 2).reshape(1, 128),
        jnp.asarray(pool_matrix(), BF),
        coarse_send,
        sums,
        *others,
    )
    landed = lax.all_to_all(outbound, "tiles", split_axis=0, concat_axis=0, tiled=True)
    coarse = pl.pallas_call(
        place_kernel,
        out_shape=jax.ShapeDtypeStruct((parent_count, VOX, quarter), BF),
        in_specs=[SM, VM],
        out_specs=VM,
        compiler_params=small,
        name="place",
    )(coarse_place, landed)
    return (skip, coarse)


def solution(mesh):
    in_specs = (
        P("tiles", None, None),
        P(None, None, "chan"),
        P("chan"),
        P("tiles", None),
        P("tiles", None),
        P("tiles", None),
        P("tiles", None),
    )
    out_specs = (P("tiles", None, "chan"), P("tiles", None, "chan"))
    return jax.shard_map(
        functools.partial(body, mesh.shape["tiles"]),
        mesh=mesh,
        in_specs=in_specs,
        out_specs=out_specs,
        check_vma=False,
    )
```

```python
import functools

import jax
import jax.numpy as jnp
import numpy as np
from jax import lax
from jax.experimental import pallas as pl
from jax.experimental.pallas import tpu as pltpu
from jax.sharding import PartitionSpec as P

EPS = 1e-05
REACH = 4
VOX = 64
HALF = 32
BF = jnp.bfloat16
F32 = jnp.float32
PAD = 64
UNROLL = 8
PARTS = 2
PER_PART = 7


def perfect(n):
    real = [(i, j) for i in range(n) for j in range(i + 1, n) if j - i <= REACH]
    fill = [(0, 1), (0, 1), (0, 2), (6, 7), (6, 7), (5, 7)]
    first = [(i, i + REACH) for i in range(n - REACH)]
    start = [(p, True) for p in real if p not in first] + [(p, False) for p in fill]

    def crossing(found):
        return -sum(i < n // 2 <= j for (i, j), _ in found)

    def split(left):
        if not left:
            return []
        here = left[0]

        def grow(chosen, rest):
            used = {i for p, _ in chosen for i in p}
            if len(used) == n:
                yield chosen, rest
                return
            low = min(set(range(n)) - used)
            for k, item in enumerate(rest):
                if low in item[0] and not used & set(item[0]):
                    yield from grow(chosen + [item], rest[:k] + rest[k + 1 :])

        for chosen, rest in grow([here], left[1:]):
            more = split(rest)
            if more is not None:
                return [chosen] + more
        return None

    found = split(start)
    return None if found is None else [[(p, True) for p in first]] + sorted(found, key=crossing)


def matchings(n):
    found = perfect(n) if n == 2 * REACH else None
    if found is None:
        found = []
        for d in range(REACH, 0, -1):
            for parity in (0, 1):
                pairs = [(i, i + d) for i in range(n - d) if (i // d) % 2 == parity]
                rest = [i for i in range(n) if all(i not in p for p in pairs)]
                if pairs:
                    found.append([(p, True) for p in pairs] + [(p, False) for p in zip(rest[::2], rest[1::2])])
    routes = [[q for p, _ in way for q in (p, p[::-1])] for way in found]
    table = np.full((n, 16), -1, np.int32)
    table[:, 15] = 0
    for m, way in enumerate(found):
        for pair, is_real in way:
            for e, other in (pair, pair[::-1]):
                if is_real:
                    gap = other - e
                    table[e, m] = REACH - 1 + gap if gap > 0 else -gap - 1
                    table[e, 15] += m << (4 * (gap - 1 if gap > 0 else REACH - 1 - gap))
    return routes, table


def pick(e, values):
    found = jnp.int32(int(values[0]))
    for i in range(1, len(values)):
        found = jnp.where(e == i, jnp.int32(int(values[i])), found)
    return found


def lane_iota(shape):
    return lax.broadcasted_iota(jnp.int32, shape, len(shape) - 1)


def dims_of(code):
    return (lax.div(code, 9) - 1, lax.rem(lax.div(code, 3), 3) - 1, lax.rem(code, 3) - 1)


def rules_matmul(f_ref, w_ref, y_refs, beside=None):
    rows = f_ref.shape[0]
    span = rows + 2 * PAD
    depth = w_ref.shape[0]
    steps = range(0, depth, 256)
    for number, q in enumerate(steps):
        width = min(256, depth - q)
        part = lax.dot_general(
            f_ref[...],
            w_ref[q : q + width, :],
            (((1,), (1,)), ((), ())),
            preferred_element_type=F32,
        )
        for s in range(0, width, 128):
            wide = min(128, width - s)
            y_ref = y_refs[(q + s) // 128 // PER_PART]
            base = ((q + s) // 128 % PER_PART) * span + PAD
            y_ref[base : base + rows, 0:wide] = part[:, s : s + wide]
        if beside is not None:
            beside(number, len(steps))


def rules_add(words, lists, part, y_refs, acc_ref):
    voxel = lax.broadcasted_iota(jnp.int32, (VOX, 128), 0)
    have = jnp.where(lane_iota((VOX, 128)) < 64, 1 << 21, 1 << 22)
    for dim, place in enumerate((lax.div(voxel, 16), lax.rem(lax.div(voxel, 4), 4), lax.rem(voxel, 4))):
        have = have + jnp.left_shift(jnp.full_like(place, 15), 3 - place + 7 * dim)

    for which, y_ref in enumerate(y_refs):
        kind = part * PARTS + which
        add_listed(words, lists, kind * words.shape[1], words[3, 128 * kind], have, y_ref, acc_ref)


def add_listed(words, lists, start, count, have, y_ref, acc_ref):
    def several(i, c):
        for u in range(UNROLL):
            r = lists[start + i * UNROLL + u]
            packed = words[0, r]
            need = words[1, r]
            taken = y_ref[pl.ds(lax.shift_right_logical(packed, 8), VOX), :]
            t = packed & 255
            acc_ref[t] = acc_ref[t] + jnp.where((have & need) == need, taken, 0.0)
        return c

    lax.fori_loop(0, lax.div(count + (UNROLL - 1), UNROLL), several, 0)


def zero_blocks(acc_ref):
    def zero(i, c):
        acc_ref[i] = jnp.zeros((VOX, 128), F32)
        return c

    lax.fori_loop(0, acc_ref.shape[0], zero, 0, unroll=8)


def folded(acc_ref, t):
    first = lane_iota((HALF, 128)) < 64
    low = acc_ref[t, 0:HALF, :]
    high = acc_ref[t, HALF:VOX, :]
    low = low + pltpu.roll(low, 64, 1)
    high = high + pltpu.roll(high, 64, 1)
    return jnp.where(first, low, high)


def emit_sends(acc_ref, sends):
    slots = sends[0].shape[0]
    for m, send_ref in enumerate(sends):

        def emit(i, c, send_ref=send_ref, base=slots * m):
            send_ref[i] = folded(acc_ref, base + i).astype(BF)
            return c

        lax.fori_loop(0, slots, emit, 0, unroll=16)


def far_kernel(count, table, tile_count, rules_hbm, f_hbm, w_hbm, *rest):
    sends, rest = rest[:count], rest[count:]
    f_ref, y_refs, rest = rest[0], rest[1 : 1 + PARTS], rest[1 + PARTS :]
    words_v, lists, acc_ref, w_ref, rules_ref, words_s, sems = rest
    rows = tile_count * VOX
    span = rows + 2 * PAD
    rule_rows = rules_ref.shape[1]
    wide = words_v.shape[1]
    slots = tile_count // 4
    copies = [
        pltpu.make_async_copy(src, dst, sems.at[i])
        for i, (src, dst) in enumerate(((rules_hbm, rules_ref), (w_hbm, w_ref), (f_hbm, f_ref)))
    ]
    for copy in copies:
        copy.start()
    before = lax.broadcasted_iota(jnp.int32, (rule_rows, rule_rows), 0)
    before = (before <= lane_iota((rule_rows, rule_rows))).astype(F32).astype(BF)
    zero_blocks(acc_ref)
    copies[0].wait()
    tile = rules_ref[0:1, :]
    kernel = rules_ref[1:2, :]
    heading = rules_ref[2:3, :]
    target = rules_ref[3:4, :]
    code = jnp.minimum(kernel, 26)
    shift = jnp.zeros_like(code)
    need = jnp.where(lax.rem(code, 2) == 0, 1 << 21, 1 << 22)
    for dim, (step, turn) in enumerate(zip(dims_of(code), dims_of(heading))):
        move = step - 4 * turn
        shift = shift + move * (16, 4, 1)[dim]
        need = need + jnp.left_shift(jnp.full_like(move, 1), move + (3 + 7 * dim))
    sent = jnp.maximum(target - tile_count, 0)
    group = lax.div(sent, slots)
    coded = jnp.full_like(group, pick(lax.axis_index("tiles"), table[:, 15]))
    way = lax.shift_right_logical(coded, 4 * group) & 15
    near = way >= count
    place = jnp.where(near, way - count, way) * slots + lax.rem(sent, slots)
    part = jnp.where(target < tile_count, 2, jnp.where(near, 1, 0))
    pair = lax.div(code, 2)
    part = jnp.where(kernel < 27, part * PARTS + lax.div(pair, PER_PART), 3 * PARTS)
    kind = lax.broadcasted_iota(jnp.int32, (8, rule_rows), 0)
    flags = jnp.where(kind == part, 1.0, 0.0)
    upto = jnp.dot(flags.astype(BF), before, preferred_element_type=F32)
    at = jnp.sum(flags * (upto - 1.0 + (kind * wide).astype(F32)), axis=0, keepdims=True)
    first_row = lax.rem(pair, PER_PART) * span + PAD + tile * VOX + shift
    words_v[...] = jnp.zeros(words_v.shape, jnp.int32)
    words_v[0:1, 0:rule_rows] = first_row * 256 + jnp.where(target < tile_count, target, place)
    words_v[1:2, 0:rule_rows] = need
    words_v[2:3, 0:rule_rows] = at.astype(jnp.int32)
    words_v[0:1, rule_rows:wide] = jnp.full((1, wide - rule_rows), PAD * 256, jnp.int32)
    words_v[1:2, rule_rows:wide] = jnp.full((1, wide - rule_rows), 1 << 23, jnp.int32)
    for c in range(3 * PARTS):
        total = upto[c : c + 1, rule_rows - 1 : rule_rows]
        words_v[3:4, 128 * c : 128 * c + 128] = jnp.broadcast_to(total, (1, 128)).astype(jnp.int32)
    to_scalars = pltpu.make_async_copy(words_v, words_s, sems.at[3])
    to_scalars.start()
    copies[1].wait()
    copies[2].wait()

    def list_some(number, steps):
        if number == 0:
            to_scalars.wait()
        share = -(-rule_rows // (steps - 1))
        for r in range(number * share, min(rule_rows, (number + 1) * share)):
            lists[words_s[2, r]] = r

    rules_matmul(f_ref, w_ref, y_refs, list_some)
    for c in range(3 * PARTS):
        for u in range(UNROLL):
            lists[c * wide + words_s[3, 128 * c] + u] = rule_rows
    rules_add(words_s, lists, 0, y_refs, acc_ref)
    emit_sends(acc_ref, sends)


def near_kernel(words, lists, *rest):
    y_refs, sends, acc_ref = rest[:PARTS], rest[PARTS:-1], rest[-1]
    zero_blocks(acc_ref)
    rules_add(words, lists, 1, y_refs, acc_ref)
    emit_sends(acc_ref, sends)


def add_arrivals(first, table, blocks, list_ref, out_ref):
    e = lax.axis_index("tiles")
    slots = blocks[0].shape[0]
    for m, block in enumerate(blocks):
        group = pick(e, table[:, first + m])

        @pl.when(group >= 0)
        def _(block=block, group=group):
            for i in range(slots):
                t = list_ref[0, group * slots + i]
                out_ref[t] = out_ref[t] + block[i].astype(F32)


def local_kernel(table, words, lists, list_ref, *rest):
    y_refs, blocks = rest[:PARTS], rest[PARTS:-2]
    local_ref, acc_ref = rest[-2:]
    zero_blocks(acc_ref)
    rules_add(words, lists, 2, y_refs, acc_ref)

    def keep(t, c):
        local_ref[t] = folded(acc_ref, t)
        return c

    lax.fori_loop(0, acc_ref.shape[0], keep, 0, unroll=16)
    add_arrivals(0, table, blocks, list_ref, local_ref)


def own_kernel(f_ref, _after, own_ref):
    c = lax.axis_index("chan")
    at = pl.multiple_of(lax.div(c, 2) * 128, 128)
    odd = lax.rem(c, 2) == 1
    first = lane_iota((HALF, 128)) < 64

    def pack(t, c):
        block = f_ref[pl.ds(pl.multiple_of(t * VOX, VOX), VOX), pl.ds(at, 128)].astype(F32)
        low, high = block[:HALF], block[HALF:]
        even_form = jnp.where(first, low, pltpu.roll(high, 64, 1))
        odd_form = jnp.where(first, pltpu.roll(low, 64, 1), high)
        own_ref[t] = jnp.where(odd, odd_form, even_form)
        return c

    lax.fori_loop(0, own_ref.shape[0], pack, 0, unroll=8)


def combine_kernel(first, table, list_ref, local_ref, *rest):
    blocks = rest[:-2]
    conv_ref, sums_ref = rest[-2:]
    tile_count = local_ref.shape[0]
    conv_ref[...] = local_ref[...]
    add_arrivals(first, table, blocks, list_ref, conv_ref)
    rows = tile_count * HALF
    pick = (lane_iota((2, 256)) // 64 % 2 == lax.broadcasted_iota(jnp.int32, (2, 256), 0)).astype(BF)
    step = 512
    for at in range(0, rows, step):
        value = conv_ref[at // HALF : (at + step) // HALF].reshape(step, 128)
        square = value * value
        top = square.astype(BF)
        rest_of = (square - top.astype(F32)).astype(BF)
        sums_ref[:, at : at + step] = lax.dot_general(
            pick,
            jnp.concatenate([top, rest_of], axis=1),
            (((1,), (1,)), ((), ())),
            preferred_element_type=F32,
        )


def norm_kernel(channels, conv_ref, own_ref, gain_ref, pool_ref, slot_ref, s0, s1, s2, s3, whole_ref, out_ref):
    tile_count = conv_ref.shape[0]
    total = jnp.concatenate([s0[...], s1[...], s2[...], s3[...]], axis=0)
    parts = []
    for _ in range(3):
        top = total.astype(BF)
        parts.append(top.astype(F32))
        total = total - top.astype(F32)
    parts = jnp.concatenate(parts, axis=0).astype(BF)
    count = parts.shape[0]
    spread = (lane_iota((count, 128)) // 64 == lax.broadcasted_iota(jnp.int32, (count, 128), 0) % 2).astype(BF)
    gain = gain_ref[...]
    for k in range(tile_count // 8):
        mean_square = lax.dot_general(
            parts[:, k * 256 : (k + 1) * 256],
            spread,
            (((0,), (0,)), ((), ())),
            preferred_element_type=F32,
        ) * (1.0 / channels)
        value = conv_ref[8 * k : 8 * k + 8].reshape(256, 128)
        v = gain * value * lax.rsqrt(mean_square + EPS)
        half = 0.5 * v
        hidden = half + half * jnp.tanh(half)
        whole = (own_ref[8 * k : 8 * k + 8].reshape(256, 128) + hidden).astype(BF)
        whole_ref[8 * k : 8 * k + 8] = whole.reshape(8, HALF, 128)
        pooled = jnp.dot(pool_ref[...], whole, preferred_element_type=F32)
        out_ref[slot_ref[0, k]] = pooled.astype(BF)


def unpack_kernel(whole_ref, skip_ref):
    skip_ref[:, 0:HALF, :] = whole_ref[:, :, 0:64]
    skip_ref[:, HALF:VOX, :] = whole_ref[:, :, 64:128]


def place_kernel(place_ref, landed_ref, out_ref):
    parents = out_ref.shape[0]
    for i in range(landed_ref.shape[0]):
        where = place_ref[0, i]

        @pl.when(where < parents)
        def _(i=i, where=where):
            for ox in range(2):
                for px in range(2):
                    row = 16 * (2 * ox + px)
                    out_ref[where, row : row + 16, :] = landed_ref[i, 16 * ox : 16 * ox + 16, 64 * px : 64 * px + 64]


def pool_matrix():
    out = np.zeros((2, 4, 4, 2, 2, 2, 2, 4, 4), np.float32)
    for ox in range(2):
        for y in range(4):
            for z in range(4):
                out[ox, y, z, ox, y // 2, z // 2, :, 2 * (y % 2) : 2 * (y % 2) + 2, 2 * (z % 2) : 2 * (z % 2) + 2] = 0.125
    return out.reshape(32, 256)


VM = pl.BlockSpec(memory_space=pltpu.VMEM)
SM = pl.BlockSpec(memory_space=pltpu.SMEM)
ANY = pl.BlockSpec(memory_space=pl.ANY)
HBM = pl.BlockSpec(memory_space=pltpu.HBM)


def call_rules(n, features, weights, rulebook, recv_list):
    tile_count, _, channels = features.shape
    offsets, _, quarter = weights.shape
    rule_rows = rulebook.shape[0]
    routes, table = matchings(n)
    count = len(routes) // 2
    slots = tile_count // 4
    span = tile_count * VOX + 2 * PAD
    wide = rule_rows + 128
    flat = features.reshape(tile_count * VOX, channels)
    flat_weights = weights.transpose(0, 2, 1).reshape(offsets * quarter, channels)
    block = jax.ShapeDtypeStruct((slots, HALF, 128), BF)
    whole = jax.ShapeDtypeStruct((tile_count, HALF, 128), F32)
    work = [pltpu.VMEM((tile_count, VOX, 128), F32)]
    flops = 2 * tile_count * VOX * channels * offsets * quarter
    shared = dict(
        compiler_params=pltpu.CompilerParams(vmem_limit_bytes=16 * 1024 * 1024),
        cost_estimate=pl.CostEstimate(flops=flops, bytes_accessed=8 << 20, transcendentals=0),
    )
    made = pl.pallas_call(
        functools.partial(far_kernel, count, table, tile_count),
        out_shape=[block] * count
        + [jax.ShapeDtypeStruct(flat.shape, BF), jax.ShapeDtypeStruct((PER_PART * span, 128), F32)]
        + [jax.ShapeDtypeStruct((PER_PART * span, 128), F32)] * (PARTS - 1)
        + [jax.ShapeDtypeStruct((8, wide), jnp.int32), jax.ShapeDtypeStruct(((3 * PARTS + 1) * wide,), jnp.int32)],
        in_specs=[HBM] * 3,
        out_specs=[VM] * (count + 2 + PARTS) + [SM],
        scratch_shapes=work
        + [
            pltpu.VMEM(flat_weights.shape, BF),
            pltpu.VMEM((4, rule_rows), jnp.int32),
            pltpu.SMEM((8, wide), jnp.int32),
            pltpu.SemaphoreType.DMA((4,)),
        ],
        name="far",
        **shared,
    )(*(pltpu.with_memory_space_constraint(x, pltpu.HBM) for x in (rulebook.T, flat, flat_weights)))
    far_sends = made[:count]
    held, *products, words, lists = made[count:]
    arrivals = [lax.ppermute(x, "tiles", route) for x, route in zip(far_sends, routes[:count])]
    near_sends = pl.pallas_call(
        near_kernel,
        out_shape=[block] * (len(routes) - count),
        in_specs=[SM, SM] + [VM] * PARTS,
        out_specs=[VM] * (len(routes) - count),
        scratch_shapes=work,
        name="near",
        **shared,
    )(words, lists, *products)
    near_arrivals = [lax.ppermute(x, "tiles", route) for x, route in zip(near_sends, routes[count:])]
    local = pl.pallas_call(
        functools.partial(local_kernel, table),
        out_shape=whole,
        in_specs=[SM] * 3 + [VM] * (PARTS + count),
        out_specs=VM,
        scratch_shapes=work,
        name="local",
        **shared,
    )(words, lists, recv_list, *products, *arrivals)
    return count, table, held, local, near_arrivals


def body(n, features, weights, gain, rulebook, recv_list, coarse_send, coarse_place):
    tile_count, _, channels = features.shape
    quarter = weights.shape[2]
    small = pltpu.CompilerParams(vmem_limit_bytes=12 * 1024 * 1024)

    count, table, held, local, arrivals = call_rules(n, features, weights, rulebook, recv_list)
    conv, sums = pl.pallas_call(
        functools.partial(combine_kernel, count, table),
        out_shape=[
            jax.ShapeDtypeStruct((tile_count, HALF, 128), F32),
            jax.ShapeDtypeStruct((2, tile_count * HALF), F32),
        ],
        in_specs=[SM] + [VM] * (1 + len(arrivals)),
        out_specs=[VM, VM],
        compiler_params=small,
        name="combine",
    )(recv_list, local, *arrivals)
    own = pl.pallas_call(
        own_kernel,
        out_shape=jax.ShapeDtypeStruct((tile_count, HALF, 128), F32),
        in_specs=[VM, ANY],
        out_specs=VM,
        compiler_params=small,
        name="own",
    )(held, sums)
    wide = lax.axis_size("chan")
    others = [lax.ppermute(sums, "chan", [(i, i ^ m) for i in range(wide)]) for m in range(1, wide)]
    slot_count = coarse_place.shape[1]
    parent_count = tile_count // 8
    packed, outbound = pl.pallas_call(
        functools.partial(norm_kernel, channels),
        out_shape=[
            jax.ShapeDtypeStruct((tile_count, HALF, 128), BF),
            jax.ShapeDtypeStruct((slot_count, HALF, 128), BF),
        ],
        in_specs=[VM] * 4 + [SM] + [VM] * 4,
        out_specs=[VM, VM],
        compiler_params=small,
        name="norm",
    )(
        conv,
        own,
        jnp.tile(gain.astype(F32), 2).reshape(1, 128),
        jnp.asarray(pool_matrix(), BF),
        coarse_send,
        sums,
        *others,
    )
    landed = lax.all_to_all(outbound, "tiles", split_axis=0, concat_axis=0, tiled=True)
    skip = pl.pallas_call(
        unpack_kernel,
        out_shape=jax.ShapeDtypeStruct((tile_count, VOX, quarter), BF),
        in_specs=[VM],
        out_specs=VM,
        compiler_params=small,
        name="unpack",
    )(packed)
    coarse = pl.pallas_call(
        place_kernel,
        out_shape=jax.ShapeDtypeStruct((parent_count, VOX, quarter), BF),
        in_specs=[SM, VM],
        out_specs=VM,
        compiler_params=small,
        name="place",
    )(coarse_place, landed)
    return (skip, coarse)


def solution(mesh):
    in_specs = (
        P("tiles", None, None),
        P(None, None, "chan"),
        P("chan"),
        P("tiles", None),
        P("tiles", None),
        P("tiles", None),
        P("tiles", None),
    )
    out_specs = (P("tiles", None, "chan"), P("tiles", None, "chan"))
    return jax.shard_map(
        functools.partial(body, mesh.shape["tiles"]),
        mesh=mesh,
        in_specs=in_specs,
        out_specs=out_specs,
        check_vma=False,
    )
```

```python
import functools

import jax
import jax.numpy as jnp
import numpy as np
from jax import lax
from jax.experimental import pallas as pl
from jax.experimental.pallas import tpu as pltpu
from jax.sharding import PartitionSpec as P

EPS = 1e-05
REACH = 4
VOX = 64
HALF = 32
BF = jnp.bfloat16
F32 = jnp.float32
PAD = 64
UNROLL = 8
PARTS = 2
PER_PART = 7


def perfect(n):
    real = [(i, j) for i in range(n) for j in range(i + 1, n) if j - i <= REACH]
    fill = [(0, 1), (0, 1), (0, 2), (6, 7), (6, 7), (5, 7)]
    first = [(i, i + REACH) for i in range(n - REACH)]
    start = [(p, True) for p in real if p not in first] + [(p, False) for p in fill]

    def crossing(found):
        return -sum(i < n // 2 <= j for (i, j), _ in found)

    def split(left):
        if not left:
            return []
        here = left[0]

        def grow(chosen, rest):
            used = {i for p, _ in chosen for i in p}
            if len(used) == n:
                yield chosen, rest
                return
            low = min(set(range(n)) - used)
            for k, item in enumerate(rest):
                if low in item[0] and not used & set(item[0]):
                    yield from grow(chosen + [item], rest[:k] + rest[k + 1 :])

        for chosen, rest in grow([here], left[1:]):
            more = split(rest)
            if more is not None:
                return [chosen] + more
        return None

    found = split(start)
    return None if found is None else [[(p, True) for p in first]] + sorted(found, key=crossing)


def matchings(n):
    found = perfect(n) if n == 2 * REACH else None
    if found is None:
        found = []
        for d in range(REACH, 0, -1):
            for parity in (0, 1):
                pairs = [(i, i + d) for i in range(n - d) if (i // d) % 2 == parity]
                rest = [i for i in range(n) if all(i not in p for p in pairs)]
                if pairs:
                    found.append([(p, True) for p in pairs] + [(p, False) for p in zip(rest[::2], rest[1::2])])
    routes = [[q for p, _ in way for q in (p, p[::-1])] for way in found]
    table = np.full((n, 16), -1, np.int32)
    table[:, 15] = 0
    for m, way in enumerate(found):
        for pair, is_real in way:
            for e, other in (pair, pair[::-1]):
                if is_real:
                    gap = other - e
                    table[e, m] = REACH - 1 + gap if gap > 0 else -gap - 1
                    table[e, 15] += m << (4 * (gap - 1 if gap > 0 else REACH - 1 - gap))
    return routes, table


def pick(e, values):
    found = jnp.int32(int(values[0]))
    for i in range(1, len(values)):
        found = jnp.where(e == i, jnp.int32(int(values[i])), found)
    return found


def lane_iota(shape):
    return lax.broadcasted_iota(jnp.int32, shape, len(shape) - 1)


def dims_of(code):
    return (lax.div(code, 9) - 1, lax.rem(lax.div(code, 3), 3) - 1, lax.rem(code, 3) - 1)


def rules_matmul(f_ref, w_ref, y_refs, beside=None):
    rows = f_ref.shape[0]
    span = rows + 2 * PAD
    depth = w_ref.shape[0]
    steps = range(0, depth, 256)
    for number, q in enumerate(steps):
        width = min(256, depth - q)
        part = lax.dot_general(
            f_ref[...],
            w_ref[q : q + width, :],
            (((1,), (1,)), ((), ())),
            preferred_element_type=F32,
        )
        for s in range(0, width, 128):
            wide = min(128, width - s)
            y_ref = y_refs[(q + s) // 128 // PER_PART]
            base = ((q + s) // 128 % PER_PART) * span + PAD
            y_ref[base : base + rows, 0:wide] = part[:, s : s + wide]
        if beside is not None:
            beside(number, len(steps))


def rules_add(words, lists, part, y_refs, acc_ref):
    voxel = lax.broadcasted_iota(jnp.int32, (VOX, 128), 0)
    have = jnp.where(lane_iota((VOX, 128)) < 64, 1 << 21, 1 << 22)
    for dim, place in enumerate((lax.div(voxel, 16), lax.rem(lax.div(voxel, 4), 4), lax.rem(voxel, 4))):
        have = have + jnp.left_shift(jnp.full_like(place, 15), 3 - place + 7 * dim)

    for which, y_ref in enumerate(y_refs):
        kind = part * PARTS + which
        add_listed(words, lists, kind * words.shape[1], words[3, 128 * kind], have, y_ref, acc_ref)


def add_listed(words, lists, start, count, have, y_ref, acc_ref):
    def several(i, c):
        for u in range(UNROLL):
            r = lists[start + i * UNROLL + u]
            packed = words[0, r]
            need = words[1, r]
            taken = y_ref[pl.ds(lax.shift_right_logical(packed, 8), VOX), :]
            t = packed & 255
            acc_ref[t] = acc_ref[t] + jnp.where((have & need) == need, taken, 0.0)
        return c

    lax.fori_loop(0, lax.div(count + (UNROLL - 1), UNROLL), several, 0)


def zero_blocks(acc_ref):
    def zero(i, c):
        acc_ref[i] = jnp.zeros((VOX, 128), F32)
        return c

    lax.fori_loop(0, acc_ref.shape[0], zero, 0, unroll=8)


def folded(acc_ref, t):
    first = lane_iota((HALF, 128)) < 64
    low = acc_ref[t, 0:HALF, :]
    high = acc_ref[t, HALF:VOX, :]
    low = low + pltpu.roll(low, 64, 1)
    high = high + pltpu.roll(high, 64, 1)
    return jnp.where(first, low, high)


def emit_sends(acc_ref, sends):
    slots = sends[0].shape[0]
    for m, send_ref in enumerate(sends):

        def emit(i, c, send_ref=send_ref, base=slots * m):
            send_ref[i] = folded(acc_ref, base + i).astype(BF)
            return c

        lax.fori_loop(0, slots, emit, 0, unroll=16)


def far_kernel(count, table, tile_count, rules_hbm, f_hbm, w_hbm, *rest):
    sends, rest = rest[:count], rest[count:]
    f_ref, y_refs, rest = rest[0], rest[1 : 1 + PARTS], rest[1 + PARTS :]
    words_v, lists_v, acc_ref, w_ref, rules_ref, words_s, lists, sems = rest
    rows = tile_count * VOX
    span = rows + 2 * PAD
    rule_rows = rules_ref.shape[1]
    wide = words_v.shape[1]
    slots = tile_count // 4
    copies = [
        pltpu.make_async_copy(src, dst, sems.at[i])
        for i, (src, dst) in enumerate(((rules_hbm, rules_ref), (w_hbm, w_ref), (f_hbm, f_ref)))
    ]
    for copy in copies:
        copy.start()
    before = lax.broadcasted_iota(jnp.int32, (rule_rows, rule_rows), 0)
    before = (before <= lane_iota((rule_rows, rule_rows))).astype(F32).astype(BF)
    zero_blocks(acc_ref)
    copies[0].wait()
    tile = rules_ref[0:1, :]
    kernel = rules_ref[1:2, :]
    heading = rules_ref[2:3, :]
    target = rules_ref[3:4, :]
    code = jnp.minimum(kernel, 26)
    shift = jnp.zeros_like(code)
    need = jnp.where(lax.rem(code, 2) == 0, 1 << 21, 1 << 22)
    for dim, (step, turn) in enumerate(zip(dims_of(code), dims_of(heading))):
        move = step - 4 * turn
        shift = shift + move * (16, 4, 1)[dim]
        need = need + jnp.left_shift(jnp.full_like(move, 1), move + (3 + 7 * dim))
    sent = jnp.maximum(target - tile_count, 0)
    group = lax.div(sent, slots)
    coded = jnp.full_like(group, pick(lax.axis_index("tiles"), table[:, 15]))
    way = lax.shift_right_logical(coded, 4 * group) & 15
    near = way >= count
    place = jnp.where(near, way - count, way) * slots + lax.rem(sent, slots)
    part = jnp.where(target < tile_count, 2, jnp.where(near, 1, 0))
    pair = lax.div(code, 2)
    part = jnp.where(kernel < 27, part * PARTS + lax.div(pair, PER_PART), 3 * PARTS)
    kind = lax.broadcasted_iota(jnp.int32, (8, rule_rows), 0)
    flags = jnp.where(kind == part, 1.0, 0.0)
    upto = jnp.dot(flags.astype(BF), before, preferred_element_type=F32)
    at = jnp.sum(flags * (upto - 1.0 + (kind * wide).astype(F32)), axis=0, keepdims=True)
    first_row = lax.rem(pair, PER_PART) * span + PAD + tile * VOX + shift
    words_v[...] = jnp.zeros(words_v.shape, jnp.int32)
    words_v[0:1, 0:rule_rows] = first_row * 256 + jnp.where(target < tile_count, target, place)
    words_v[1:2, 0:rule_rows] = need
    words_v[2:3, 0:rule_rows] = at.astype(jnp.int32)
    words_v[0:1, rule_rows:wide] = jnp.full((1, wide - rule_rows), PAD * 256, jnp.int32)
    words_v[1:2, rule_rows:wide] = jnp.full((1, wide - rule_rows), 1 << 23, jnp.int32)
    for c in range(3 * PARTS):
        total = upto[c : c + 1, rule_rows - 1 : rule_rows]
        words_v[3:4, 128 * c : 128 * c + 128] = jnp.broadcast_to(total, (1, 128)).astype(jnp.int32)
    to_scalars = pltpu.make_async_copy(words_v, words_s, sems.at[3])
    to_scalars.start()
    copies[1].wait()
    copies[2].wait()

    def list_some(number, steps):
        if number == 0:
            to_scalars.wait()
        share = -(-rule_rows // (steps - 1))
        for r in range(number * share, min(rule_rows, (number + 1) * share)):
            lists[words_s[2, r]] = r

    rules_matmul(f_ref, w_ref, y_refs, list_some)
    for c in range(3 * PARTS):
        for u in range(UNROLL):
            lists[c * wide + words_s[3, 128 * c] + u] = rule_rows
    hand_on = pltpu.make_async_copy(lists, lists_v, sems.at[4])
    hand_on.start()
    rules_add(words_s, lists, 0, y_refs, acc_ref)
    emit_sends(acc_ref, sends)
    hand_on.wait()


def near_kernel(words_v, lists_v, *rest):
    y_refs, sends = rest[:PARTS], rest[PARTS:-4]
    acc_ref, words, lists, sems = rest[-4:]
    copies = [
        pltpu.make_async_copy(words_v, words, sems.at[0]),
        pltpu.make_async_copy(lists_v, lists, sems.at[1]),
    ]
    for copy in copies:
        copy.start()
    zero_blocks(acc_ref)
    for copy in copies:
        copy.wait()
    rules_add(words, lists, 1, y_refs, acc_ref)
    emit_sends(acc_ref, sends)


def add_arrivals(first, table, blocks, list_ref, out_ref):
    e = lax.axis_index("tiles")
    slots = blocks[0].shape[0]
    for m, block in enumerate(blocks):
        group = pick(e, table[:, first + m])

        @pl.when(group >= 0)
        def _(block=block, group=group):
            for i in range(slots):
                t = list_ref[0, group * slots + i]
                out_ref[t] = out_ref[t] + block[i].astype(F32)


def local_kernel(words_v, lists_v, _after, *rest):
    y_refs, (local_ref, acc_ref, words, lists, sems) = rest[:PARTS], rest[PARTS:]
    copies = [
        pltpu.make_async_copy(words_v, words, sems.at[0]),
        pltpu.make_async_copy(lists_v, lists, sems.at[1]),
    ]
    for copy in copies:
        copy.start()
    zero_blocks(acc_ref)
    for copy in copies:
        copy.wait()
    rules_add(words, lists, 2, y_refs, acc_ref)

    def keep(t, c):
        local_ref[t] = folded(acc_ref, t)
        return c

    lax.fori_loop(0, acc_ref.shape[0], keep, 0, unroll=16)


def arrive_kernel(first, table, list_v, local_ref, *rest):
    blocks = rest[:-3]
    out_ref, list_ref, sem = rest[-3:]
    copy = pltpu.make_async_copy(list_v, list_ref, sem)
    copy.start()
    out_ref[...] = local_ref[...]
    copy.wait()
    add_arrivals(first, table, blocks, list_ref, out_ref)


def own_kernel(f_ref, _after, own_ref):
    c = lax.axis_index("chan")
    at = pl.multiple_of(lax.div(c, 2) * 128, 128)
    odd = lax.rem(c, 2) == 1
    first = lane_iota((HALF, 128)) < 64

    def pack(t, c):
        block = f_ref[pl.ds(pl.multiple_of(t * VOX, VOX), VOX), pl.ds(at, 128)].astype(F32)
        low, high = block[:HALF], block[HALF:]
        even_form = jnp.where(first, low, pltpu.roll(high, 64, 1))
        odd_form = jnp.where(first, pltpu.roll(low, 64, 1), high)
        own_ref[t] = jnp.where(odd, odd_form, even_form)
        return c

    lax.fori_loop(0, own_ref.shape[0], pack, 0, unroll=8)


def combine_kernel(first, table, list_v, local_ref, *rest):
    blocks = rest[:-4]
    conv_ref, sums_ref, list_ref, sem = rest[-4:]
    copy = pltpu.make_async_copy(list_v, list_ref, sem)
    copy.start()
    tile_count = local_ref.shape[0]
    conv_ref[...] = local_ref[...]
    copy.wait()
    add_arrivals(first, table, blocks, list_ref, conv_ref)
    rows = tile_count * HALF
    pick = (lane_iota((2, 256)) // 64 % 2 == lax.broadcasted_iota(jnp.int32, (2, 256), 0)).astype(BF)
    step = 512
    for at in range(0, rows, step):
        value = conv_ref[at // HALF : (at + step) // HALF].reshape(step, 128)
        square = value * value
        top = square.astype(BF)
        rest_of = (square - top.astype(F32)).astype(BF)
        sums_ref[:, at : at + step] = lax.dot_general(
            pick,
            jnp.concatenate([top, rest_of], axis=1),
            (((1,), (1,)), ((), ())),
            preferred_element_type=F32,
        )


def norm_kernel(channels, conv_ref, own_ref, gain_ref, pool_ref, slot_v, s0, s1, s2, s3, whole_ref, out_ref, slot_ref, sem):
    copy = pltpu.make_async_copy(slot_v, slot_ref, sem)
    copy.start()
    tile_count = conv_ref.shape[0]
    total = jnp.concatenate([s0[...], s1[...], s2[...], s3[...]], axis=0)
    parts = []
    for _ in range(3):
        top = total.astype(BF)
        parts.append(top.astype(F32))
        total = total - top.astype(F32)
    parts = jnp.concatenate(parts, axis=0).astype(BF)
    count = parts.shape[0]
    spread = (lane_iota((count, 128)) // 64 == lax.broadcasted_iota(jnp.int32, (count, 128), 0) % 2).astype(BF)
    gain = gain_ref[...]
    for k in range(tile_count // 8):
        mean_square = lax.dot_general(
            parts[:, k * 256 : (k + 1) * 256],
            spread,
            (((0,), (0,)), ((), ())),
            preferred_element_type=F32,
        ) * (1.0 / channels)
        value = conv_ref[8 * k : 8 * k + 8].reshape(256, 128)
        v = gain * value * lax.rsqrt(mean_square + EPS)
        half = 0.5 * v
        hidden = half + half * jnp.tanh(half)
        whole = (own_ref[8 * k : 8 * k + 8].reshape(256, 128) + hidden).astype(BF)
        whole_ref[8 * k : 8 * k + 8] = whole.reshape(8, HALF, 128)
        pooled = jnp.dot(pool_ref[...], whole, preferred_element_type=F32)
        if k == 0:
            copy.wait()
        out_ref[slot_ref[0, k]] = pooled.astype(BF)


def unpack_kernel(whole_ref, skip_ref):
    skip_ref[:, 0:HALF, :] = whole_ref[:, :, 0:64]
    skip_ref[:, HALF:VOX, :] = whole_ref[:, :, 64:128]


def place_kernel(place_ref, landed_ref, out_ref):
    slots = landed_ref.shape[0]
    where = [jnp.broadcast_to(place_ref[:, i : i + 1], (HALF, 128)) for i in range(slots)]
    for p in range(out_ref.shape[0]):
        block = landed_ref[0].astype(F32)
        for i in range(1, slots):
            block = jnp.where(where[i] == p, landed_ref[i].astype(F32), block)
        block = block.astype(BF)
        for ox in range(2):
            for px in range(2):
                row = 16 * (2 * ox + px)
                out_ref[p, row : row + 16, :] = block[16 * ox : 16 * ox + 16, 64 * px : 64 * px + 64]


def pool_matrix():
    out = np.zeros((2, 4, 4, 2, 2, 2, 2, 4, 4), np.float32)
    for ox in range(2):
        for y in range(4):
            for z in range(4):
                out[ox, y, z, ox, y // 2, z // 2, :, 2 * (y % 2) : 2 * (y % 2) + 2, 2 * (z % 2) : 2 * (z % 2) + 2] = 0.125
    return out.reshape(32, 256)


VM = pl.BlockSpec(memory_space=pltpu.VMEM)
SM = pl.BlockSpec(memory_space=pltpu.SMEM)
ANY = pl.BlockSpec(memory_space=pl.ANY)
HBM = pl.BlockSpec(memory_space=pltpu.HBM)


def call_rules(n, features, weights, rulebook, recv_list):
    tile_count, _, channels = features.shape
    offsets, _, quarter = weights.shape
    rule_rows = rulebook.shape[0]
    routes, table = matchings(n)
    count = len(routes) // 2
    slots = tile_count // 4
    span = tile_count * VOX + 2 * PAD
    wide = rule_rows + 128
    lists_shape = ((3 * PARTS + 1) * wide,)
    scalars = [pltpu.SMEM((8, wide), jnp.int32), pltpu.SMEM(lists_shape, jnp.int32)]
    flat = features.reshape(tile_count * VOX, channels)
    flat_weights = weights.transpose(0, 2, 1).reshape(offsets * quarter, channels)
    block = jax.ShapeDtypeStruct((slots, HALF, 128), BF)
    whole = jax.ShapeDtypeStruct((tile_count, HALF, 128), F32)
    work = [pltpu.VMEM((tile_count, VOX, 128), F32)]
    flops = 2 * tile_count * VOX * channels * offsets * quarter
    shared = dict(
        compiler_params=pltpu.CompilerParams(vmem_limit_bytes=16 * 1024 * 1024),
        cost_estimate=pl.CostEstimate(flops=flops, bytes_accessed=8 << 20, transcendentals=0),
    )
    made = pl.pallas_call(
        functools.partial(far_kernel, count, table, tile_count),
        out_shape=[block] * count
        + [jax.ShapeDtypeStruct(flat.shape, BF), jax.ShapeDtypeStruct((PER_PART * span, 128), F32)]
        + [jax.ShapeDtypeStruct((PER_PART * span, 128), F32)] * (PARTS - 1)
        + [jax.ShapeDtypeStruct((8, wide), jnp.int32), jax.ShapeDtypeStruct(lists_shape, jnp.int32)],
        in_specs=[HBM] * 3,
        out_specs=[VM] * (count + 3 + PARTS),
        scratch_shapes=work
        + [
            pltpu.VMEM(flat_weights.shape, BF),
            pltpu.VMEM((4, rule_rows), jnp.int32),
            *scalars,
            pltpu.SemaphoreType.DMA((5,)),
        ],
        name="far",
        **shared,
    )(*(pltpu.with_memory_space_constraint(x, pltpu.HBM) for x in (rulebook.T, flat, flat_weights)))
    far_sends = made[:count]
    held, *products, words, lists = made[count:]
    arrivals = [lax.ppermute(x, "tiles", route) for x, route in zip(far_sends, routes[:count])]
    near_sends = pl.pallas_call(
        near_kernel,
        out_shape=[block] * (len(routes) - count),
        in_specs=[VM] * (2 + PARTS),
        out_specs=[VM] * (len(routes) - count),
        scratch_shapes=work + scalars + [pltpu.SemaphoreType.DMA((2,))],
        name="near",
        **shared,
    )(words, lists, *products)
    near_arrivals = [lax.ppermute(x, "tiles", route) for x, route in zip(near_sends, routes[count:])]
    local = pl.pallas_call(
        local_kernel,
        out_shape=whole,
        in_specs=[VM, VM, ANY] + [VM] * PARTS,
        out_specs=VM,
        scratch_shapes=work + scalars + [pltpu.SemaphoreType.DMA((2,))],
        name="local",
        **shared,
    )(words, lists, near_sends[0], *products)
    local = pl.pallas_call(
        functools.partial(arrive_kernel, 0, table),
        out_shape=whole,
        in_specs=[VM] * (2 + count),
        out_specs=VM,
        scratch_shapes=[pltpu.SMEM(recv_list.shape, jnp.int32), pltpu.SemaphoreType.DMA],
        compiler_params=pltpu.CompilerParams(vmem_limit_bytes=12 * 1024 * 1024),
        name="arrive",
    )(recv_list, local, *arrivals)
    return count, table, held, local, near_arrivals


def body(n, features, weights, gain, rulebook, recv_list, coarse_send, coarse_place):
    tile_count, _, channels = features.shape
    quarter = weights.shape[2]
    small = pltpu.CompilerParams(vmem_limit_bytes=12 * 1024 * 1024)

    count, table, held, local, arrivals = call_rules(n, features, weights, rulebook, recv_list)
    conv, sums = pl.pallas_call(
        functools.partial(combine_kernel, count, table),
        out_shape=[
            jax.ShapeDtypeStruct((tile_count, HALF, 128), F32),
            jax.ShapeDtypeStruct((2, tile_count * HALF), F32),
        ],
        in_specs=[VM] * (2 + len(arrivals)),
        out_specs=[VM, VM],
        scratch_shapes=[pltpu.SMEM(recv_list.shape, jnp.int32), pltpu.SemaphoreType.DMA],
        compiler_params=small,
        name="combine",
    )(recv_list, local, *arrivals)
    own = pl.pallas_call(
        own_kernel,
        out_shape=jax.ShapeDtypeStruct((tile_count, HALF, 128), F32),
        in_specs=[VM, ANY],
        out_specs=VM,
        compiler_params=small,
        name="own",
    )(held, sums)
    wide = lax.axis_size("chan")
    others = [lax.ppermute(sums, "chan", [(i, i ^ m) for i in range(wide)]) for m in range(1, wide)]
    slot_count = coarse_place.shape[1]
    parent_count = tile_count // 8
    packed, outbound = pl.pallas_call(
        functools.partial(norm_kernel, channels),
        out_shape=[
            jax.ShapeDtypeStruct((tile_count, HALF, 128), BF),
            jax.ShapeDtypeStruct((slot_count, HALF, 128), BF),
        ],
        in_specs=[VM] * 9,
        out_specs=[VM, VM],
        scratch_shapes=[pltpu.SMEM(coarse_send.shape, jnp.int32), pltpu.SemaphoreType.DMA],
        compiler_params=small,
        name="norm",
    )(
        conv,
        own,
        jnp.tile(gain.astype(F32), 2).reshape(1, 128),
        jnp.asarray(pool_matrix(), BF),
        coarse_send,
        sums,
        *others,
    )
    landed = lax.all_to_all(outbound, "tiles", split_axis=0, concat_axis=0, tiled=True)
    skip = pl.pallas_call(
        unpack_kernel,
        out_shape=jax.ShapeDtypeStruct((tile_count, VOX, quarter), BF),
        in_specs=[VM],
        out_specs=VM,
        compiler_params=small,
        name="unpack",
    )(packed)
    coarse = pl.pallas_call(
        place_kernel,
        out_shape=jax.ShapeDtypeStruct((parent_count, VOX, quarter), BF),
        in_specs=[VM, VM],
        out_specs=VM,
        compiler_params=small,
        name="place",
    )(coarse_place, landed)
    return (skip, coarse)


def solution(mesh):
    in_specs = (
        P("tiles", None, None),
        P(None, None, "chan"),
        P("chan"),
        P("tiles", None),
        P("tiles", None),
        P("tiles", None),
        P("tiles", None),
    )
    out_specs = (P("tiles", None, "chan"), P("tiles", None, "chan"))
    return jax.shard_map(
        functools.partial(body, mesh.shape["tiles"]),
        mesh=mesh,
        in_specs=in_specs,
        out_specs=out_specs,
        check_vma=False,
    )
```

```python
import functools

import jax
import jax.numpy as jnp
import numpy as np
from jax import lax
from jax.experimental import pallas as pl
from jax.experimental.pallas import tpu as pltpu
from jax.sharding import PartitionSpec as P

EPS = 1e-05
REACH = 4
VOX = 64
HALF = 32
BF = jnp.bfloat16
F32 = jnp.float32
PAD = 64
UNROLL = 8
PARTS = 2
PER_PART = 7
ORDER = (0, 4, 5, 1, 2, 6, 3)


def perfect(n):
    real = [(i, j) for i in range(n) for j in range(i + 1, n) if j - i <= REACH]
    fill = [(0, 1), (0, 1), (0, 2), (6, 7), (6, 7), (5, 7)]
    first = [(i, i + REACH) for i in range(n - REACH)]
    start = [(p, True) for p in real if p not in first] + [(p, False) for p in fill]

    def crossing(found):
        return -sum(i < n // 2 <= j for (i, j), _ in found)

    def split(left):
        if not left:
            return []
        here = left[0]

        def grow(chosen, rest):
            used = {i for p, _ in chosen for i in p}
            if len(used) == n:
                yield chosen, rest
                return
            low = min(set(range(n)) - used)
            for k, item in enumerate(rest):
                if low in item[0] and not used & set(item[0]):
                    yield from grow(chosen + [item], rest[:k] + rest[k + 1 :])

        for chosen, rest in grow([here], left[1:]):
            more = split(rest)
            if more is not None:
                return [chosen] + more
        return None

    found = split(start)
    return None if found is None else [[(p, True) for p in first]] + sorted(found, key=crossing)


def matchings(n):
    found = perfect(n) if n == 2 * REACH else None
    if found is not None:
        found = [found[i] for i in ORDER]
    if found is None:
        found = []
        for d in range(REACH, 0, -1):
            for parity in (0, 1):
                pairs = [(i, i + d) for i in range(n - d) if (i // d) % 2 == parity]
                rest = [i for i in range(n) if all(i not in p for p in pairs)]
                if pairs:
                    found.append([(p, True) for p in pairs] + [(p, False) for p in zip(rest[::2], rest[1::2])])
    routes = [[q for p, _ in way for q in (p, p[::-1])] for way in found]
    table = np.full((n, 16), -1, np.int32)
    table[:, 15] = 0
    for m, way in enumerate(found):
        for pair, is_real in way:
            for e, other in (pair, pair[::-1]):
                if is_real:
                    gap = other - e
                    table[e, m] = REACH - 1 + gap if gap > 0 else -gap - 1
                    table[e, 15] += m << (4 * (gap - 1 if gap > 0 else REACH - 1 - gap))
    return routes, table


def pick(e, values):
    found = jnp.int32(int(values[0]))
    for i in range(1, len(values)):
        found = jnp.where(e == i, jnp.int32(int(values[i])), found)
    return found


def lane_iota(shape):
    return lax.broadcasted_iota(jnp.int32, shape, len(shape) - 1)


def dims_of(code):
    return (lax.div(code, 9) - 1, lax.rem(lax.div(code, 3), 3) - 1, lax.rem(code, 3) - 1)


def rules_matmul(f_ref, w_ref, y_refs, beside=None):
    rows = f_ref.shape[0]
    span = rows + 2 * PAD
    depth = w_ref.shape[0]
    steps = range(0, depth, 256)
    for number, q in enumerate(steps):
        width = min(256, depth - q)
        part = lax.dot_general(
            f_ref[...],
            w_ref[q : q + width, :],
            (((1,), (1,)), ((), ())),
            preferred_element_type=F32,
        )
        for s in range(0, width, 128):
            wide = min(128, width - s)
            y_ref = y_refs[(q + s) // 128 // PER_PART]
            base = ((q + s) // 128 % PER_PART) * span + PAD
            y_ref[base : base + rows, 0:wide] = part[:, s : s + wide]
        if beside is not None:
            beside(number, len(steps))


def rules_add(words, lists, part, y_refs, acc_ref):
    voxel = lax.broadcasted_iota(jnp.int32, (VOX, 128), 0)
    have = jnp.where(lane_iota((VOX, 128)) < 64, 1 << 21, 1 << 22)
    for dim, place in enumerate((lax.div(voxel, 16), lax.rem(lax.div(voxel, 4), 4), lax.rem(voxel, 4))):
        have = have + jnp.left_shift(jnp.full_like(place, 15), 3 - place + 7 * dim)

    for which, y_ref in enumerate(y_refs):
        kind = part * PARTS + which
        add_listed(words, lists, kind * words.shape[1], words[3, 128 * kind], have, y_ref, acc_ref)


def add_listed(words, lists, start, count, have, y_ref, acc_ref):
    def several(i, c):
        for u in range(UNROLL):
            r = lists[start + i * UNROLL + u]
            packed = words[0, r]
            need = words[1, r]
            taken = y_ref[pl.ds(lax.shift_right_logical(packed, 8), VOX), :]
            t = packed & 255
            acc_ref[t] = acc_ref[t] + jnp.where((have & need) == need, taken, 0.0)
        return c

    lax.fori_loop(0, lax.div(count + (UNROLL - 1), UNROLL), several, 0)


def zero_blocks(acc_ref):
    def zero(i, c):
        acc_ref[i] = jnp.zeros((VOX, 128), F32)
        return c

    lax.fori_loop(0, acc_ref.shape[0], zero, 0, unroll=8)


def folded(acc_ref, t):
    first = lane_iota((HALF, 128)) < 64
    low = acc_ref[t, 0:HALF, :]
    high = acc_ref[t, HALF:VOX, :]
    low = low + pltpu.roll(low, 64, 1)
    high = high + pltpu.roll(high, 64, 1)
    return jnp.where(first, low, high)


def emit_sends(acc_ref, sends):
    slots = sends[0].shape[0]
    for m, send_ref in enumerate(sends):

        def emit(i, c, send_ref=send_ref, base=slots * m):
            send_ref[i] = folded(acc_ref, base + i).astype(BF)
            return c

        lax.fori_loop(0, slots, emit, 0, unroll=16)


def far_kernel(count, table, tile_count, rules_hbm, f_hbm, w_hbm, *rest):
    sends, rest = rest[:count], rest[count:]
    f_ref, y_refs, rest = rest[0], rest[1 : 1 + PARTS], rest[1 + PARTS :]
    words_v, lists_v, acc_ref, w_ref, rules_ref, words_s, lists, sems = rest
    rows = tile_count * VOX
    span = rows + 2 * PAD
    rule_rows = rules_ref.shape[1]
    wide = words_v.shape[1]
    slots = tile_count // 4
    copies = [
        pltpu.make_async_copy(src, dst, sems.at[i])
        for i, (src, dst) in enumerate(((rules_hbm, rules_ref), (w_hbm, w_ref), (f_hbm, f_ref)))
    ]
    for copy in copies:
        copy.start()
    before = lax.broadcasted_iota(jnp.int32, (rule_rows, rule_rows), 0)
    before = (before <= lane_iota((rule_rows, rule_rows))).astype(F32).astype(BF)
    zero_blocks(acc_ref)
    copies[0].wait()
    tile = rules_ref[0:1, :]
    kernel = rules_ref[1:2, :]
    heading = rules_ref[2:3, :]
    target = rules_ref[3:4, :]
    code = jnp.minimum(kernel, 26)
    shift = jnp.zeros_like(code)
    need = jnp.where(lax.rem(code, 2) == 0, 1 << 21, 1 << 22)
    for dim, (step, turn) in enumerate(zip(dims_of(code), dims_of(heading))):
        move = step - 4 * turn
        shift = shift + move * (16, 4, 1)[dim]
        need = need + jnp.left_shift(jnp.full_like(move, 1), move + (3 + 7 * dim))
    sent = jnp.maximum(target - tile_count, 0)
    group = lax.div(sent, slots)
    coded = jnp.full_like(group, pick(lax.axis_index("tiles"), table[:, 15]))
    way = lax.shift_right_logical(coded, 4 * group) & 15
    near = way >= count
    place = jnp.where(near, way - count, way) * slots + lax.rem(sent, slots)
    part = jnp.where(target < tile_count, 2, jnp.where(near, 1, 0))
    pair = lax.div(code, 2)
    part = jnp.where(kernel < 27, part * PARTS + lax.div(pair, PER_PART), 3 * PARTS)
    kind = lax.broadcasted_iota(jnp.int32, (8, rule_rows), 0)
    flags = jnp.where(kind == part, 1.0, 0.0)
    upto = jnp.dot(flags.astype(BF), before, preferred_element_type=F32)
    at = jnp.sum(flags * (upto - 1.0 + (kind * wide).astype(F32)), axis=0, keepdims=True)
    first_row = lax.rem(pair, PER_PART) * span + PAD + tile * VOX + shift
    words_v[...] = jnp.zeros(words_v.shape, jnp.int32)
    words_v[0:1, 0:rule_rows] = first_row * 256 + jnp.where(target < tile_count, target, place)
    words_v[1:2, 0:rule_rows] = need
    words_v[2:3, 0:rule_rows] = at.astype(jnp.int32)
    words_v[0:1, rule_rows:wide] = jnp.full((1, wide - rule_rows), PAD * 256, jnp.int32)
    words_v[1:2, rule_rows:wide] = jnp.full((1, wide - rule_rows), 1 << 23, jnp.int32)
    for c in range(3 * PARTS):
        total = upto[c : c + 1, rule_rows - 1 : rule_rows]
        words_v[3:4, 128 * c : 128 * c + 128] = jnp.broadcast_to(total, (1, 128)).astype(jnp.int32)
    to_scalars = pltpu.make_async_copy(words_v, words_s, sems.at[3])
    to_scalars.start()
    copies[1].wait()
    copies[2].wait()

    def list_some(number, steps):
        if number == 0:
            to_scalars.wait()
        share = -(-rule_rows // (steps - 1))
        for r in range(number * share, min(rule_rows, (number + 1) * share)):
            lists[words_s[2, r]] = r

    rules_matmul(f_ref, w_ref, y_refs, list_some)
    for c in range(3 * PARTS):
        for u in range(UNROLL):
            lists[c * wide + words_s[3, 128 * c] + u] = rule_rows
    hand_on = pltpu.make_async_copy(lists, lists_v, sems.at[4])
    hand_on.start()
    rules_add(words_s, lists, 0, y_refs, acc_ref)
    emit_sends(acc_ref, sends)
    hand_on.wait()


def near_kernel(words_v, lists_v, *rest):
    y_refs, sends = rest[:PARTS], rest[PARTS:-4]
    acc_ref, words, lists, sems = rest[-4:]
    copies = [
        pltpu.make_async_copy(words_v, words, sems.at[0]),
        pltpu.make_async_copy(lists_v, lists, sems.at[1]),
    ]
    for copy in copies:
        copy.start()
    zero_blocks(acc_ref)
    for copy in copies:
        copy.wait()
    rules_add(words, lists, 1, y_refs, acc_ref)
    emit_sends(acc_ref, sends)


def add_arrivals(first, table, blocks, list_ref, out_ref):
    e = lax.axis_index("tiles")
    slots = blocks[0].shape[0]
    for m, block in enumerate(blocks):
        group = pick(e, table[:, first + m])

        @pl.when(group >= 0)
        def _(block=block, group=group):
            for i in range(slots):
                t = list_ref[0, group * slots + i]
                out_ref[t] = out_ref[t] + block[i].astype(F32)


def local_kernel(words_v, lists_v, _after, *rest):
    y_refs, (local_ref, acc_ref, words, lists, sems) = rest[:PARTS], rest[PARTS:]
    copies = [
        pltpu.make_async_copy(words_v, words, sems.at[0]),
        pltpu.make_async_copy(lists_v, lists, sems.at[1]),
    ]
    for copy in copies:
        copy.start()
    zero_blocks(acc_ref)
    for copy in copies:
        copy.wait()
    rules_add(words, lists, 2, y_refs, acc_ref)

    def keep(t, c):
        local_ref[t] = folded(acc_ref, t)
        return c

    lax.fori_loop(0, acc_ref.shape[0], keep, 0, unroll=16)


def arrive_kernel(first, table, list_v, local_ref, *rest):
    blocks = rest[:-3]
    out_ref, list_ref, sem = rest[-3:]
    copy = pltpu.make_async_copy(list_v, list_ref, sem)
    copy.start()
    out_ref[...] = local_ref[...]
    copy.wait()
    add_arrivals(first, table, blocks, list_ref, out_ref)


def own_kernel(f_ref, _after, own_ref):
    c = lax.axis_index("chan")
    at = pl.multiple_of(lax.div(c, 2) * 128, 128)
    odd = lax.rem(c, 2) == 1
    first = lane_iota((HALF, 128)) < 64

    def pack(t, c):
        block = f_ref[pl.ds(pl.multiple_of(t * VOX, VOX), VOX), pl.ds(at, 128)].astype(F32)
        low, high = block[:HALF], block[HALF:]
        even_form = jnp.where(first, low, pltpu.roll(high, 64, 1))
        odd_form = jnp.where(first, pltpu.roll(low, 64, 1), high)
        own_ref[t] = jnp.where(odd, odd_form, even_form)
        return c

    lax.fori_loop(0, own_ref.shape[0], pack, 0, unroll=8)


def combine_kernel(first, table, list_v, local_ref, *rest):
    blocks = rest[:-4]
    conv_ref, sums_ref, list_ref, sem = rest[-4:]
    copy = pltpu.make_async_copy(list_v, list_ref, sem)
    copy.start()
    tile_count = local_ref.shape[0]
    conv_ref[...] = local_ref[...]
    copy.wait()
    add_arrivals(first, table, blocks, list_ref, conv_ref)
    rows = tile_count * HALF
    pick = (lane_iota((2, 256)) // 64 % 2 == lax.broadcasted_iota(jnp.int32, (2, 256), 0)).astype(BF)
    step = 512
    for at in range(0, rows, step):
        value = conv_ref[at // HALF : (at + step) // HALF].reshape(step, 128)
        square = value * value
        top = square.astype(BF)
        rest_of = (square - top.astype(F32)).astype(BF)
        sums_ref[:, at : at + step] = lax.dot_general(
            pick,
            jnp.concatenate([top, rest_of], axis=1),
            (((1,), (1,)), ((), ())),
            preferred_element_type=F32,
        )


def norm_kernel(channels, conv_ref, own_ref, gain_ref, pool_ref, slot_v, s0, s1, s2, s3, whole_ref, out_ref, slot_ref, sem):
    copy = pltpu.make_async_copy(slot_v, slot_ref, sem)
    copy.start()
    tile_count = conv_ref.shape[0]
    total = (s0[...] + s1[...]) + (s2[...] + s3[...])
    rest = lax.rsqrt(total * (1.0 / channels) + EPS)
    parts = []
    for _ in range(3):
        top = rest.astype(BF).astype(F32)
        parts.append(top)
        rest = rest - top
    parts = jnp.concatenate(parts, axis=0).astype(BF)
    count = parts.shape[0]
    spread = (lane_iota((count, 128)) // 64 == lax.broadcasted_iota(jnp.int32, (count, 128), 0) % 2).astype(BF)
    gain = 0.5 * gain_ref[...]
    for k in range(tile_count // 8):
        part = lax.dot_general(
            parts[:, k * 256 : (k + 1) * 256],
            spread,
            (((0,), (0,)), ((), ())),
            preferred_element_type=F32,
        )
        half = gain * conv_ref[8 * k : 8 * k + 8].reshape(256, 128) * part
        hidden = half + half * jnp.tanh(half)
        whole = (own_ref[8 * k : 8 * k + 8].reshape(256, 128) + hidden).astype(BF)
        whole_ref[8 * k : 8 * k + 8] = whole.reshape(8, HALF, 128)
    copy.wait()
    for k in range(tile_count // 8):
        whole = whole_ref[8 * k : 8 * k + 8].reshape(256, 128)
        out_ref[slot_ref[0, k]] = jnp.dot(pool_ref[...], whole, preferred_element_type=F32).astype(BF)


def unpack_kernel(whole_ref, skip_ref):
    skip_ref[:, 0:HALF, :] = whole_ref[:, :, 0:64]
    skip_ref[:, HALF:VOX, :] = whole_ref[:, :, 64:128]


def place_kernel(place_ref, landed_ref, out_ref):
    slots = landed_ref.shape[0]
    where = [jnp.broadcast_to(place_ref[:, i : i + 1], (HALF, 128)) for i in range(slots)]
    for p in range(out_ref.shape[0]):
        block = landed_ref[0].astype(F32)
        for i in range(1, slots):
            block = jnp.where(where[i] == p, landed_ref[i].astype(F32), block)
        block = block.astype(BF)
        for ox in range(2):
            for px in range(2):
                row = 16 * (2 * ox + px)
                out_ref[p, row : row + 16, :] = block[16 * ox : 16 * ox + 16, 64 * px : 64 * px + 64]


def pool_matrix():
    out = np.zeros((2, 4, 4, 2, 2, 2, 2, 4, 4), np.float32)
    for ox in range(2):
        for y in range(4):
            for z in range(4):
                out[ox, y, z, ox, y // 2, z // 2, :, 2 * (y % 2) : 2 * (y % 2) + 2, 2 * (z % 2) : 2 * (z % 2) + 2] = 0.125
    return out.reshape(32, 256)


VM = pl.BlockSpec(memory_space=pltpu.VMEM)
SM = pl.BlockSpec(memory_space=pltpu.SMEM)
ANY = pl.BlockSpec(memory_space=pl.ANY)
HBM = pl.BlockSpec(memory_space=pltpu.HBM)


def call_rules(n, features, weights, rulebook, recv_list):
    tile_count, _, channels = features.shape
    offsets, _, quarter = weights.shape
    rule_rows = rulebook.shape[0]
    routes, table = matchings(n)
    count = len(routes) // 2
    slots = tile_count // 4
    span = tile_count * VOX + 2 * PAD
    wide = rule_rows + 128
    lists_shape = ((3 * PARTS + 1) * wide,)
    scalars = [pltpu.SMEM((8, wide), jnp.int32), pltpu.SMEM(lists_shape, jnp.int32)]
    flat = features.reshape(tile_count * VOX, channels)
    flat_weights = weights.transpose(0, 2, 1).reshape(offsets * quarter, channels)
    block = jax.ShapeDtypeStruct((slots, HALF, 128), BF)
    whole = jax.ShapeDtypeStruct((tile_count, HALF, 128), F32)
    work = [pltpu.VMEM((tile_count, VOX, 128), F32)]
    flops = 2 * tile_count * VOX * channels * offsets * quarter
    shared = dict(
        compiler_params=pltpu.CompilerParams(vmem_limit_bytes=16 * 1024 * 1024),
        cost_estimate=pl.CostEstimate(flops=flops, bytes_accessed=8 << 20, transcendentals=0),
    )
    made = pl.pallas_call(
        functools.partial(far_kernel, count, table, tile_count),
        out_shape=[block] * count
        + [jax.ShapeDtypeStruct(flat.shape, BF), jax.ShapeDtypeStruct((PER_PART * span, 128), F32)]
        + [jax.ShapeDtypeStruct((PER_PART * span, 128), F32)] * (PARTS - 1)
        + [jax.ShapeDtypeStruct((8, wide), jnp.int32), jax.ShapeDtypeStruct(lists_shape, jnp.int32)],
        in_specs=[HBM] * 3,
        out_specs=[VM] * (count + 3 + PARTS),
        scratch_shapes=work
        + [
            pltpu.VMEM(flat_weights.shape, BF),
            pltpu.VMEM((4, rule_rows), jnp.int32),
            *scalars,
            pltpu.SemaphoreType.DMA((5,)),
        ],
        name="far",
        **shared,
    )(*(pltpu.with_memory_space_constraint(x, pltpu.HBM) for x in (rulebook.T, flat, flat_weights)))
    far_sends = made[:count]
    held, *products, words, lists = made[count:]
    arrivals = [lax.ppermute(x, "tiles", route) for x, route in zip(far_sends, routes[:count])]
    near_sends = pl.pallas_call(
        near_kernel,
        out_shape=[block] * (len(routes) - count),
        in_specs=[VM] * (2 + PARTS),
        out_specs=[VM] * (len(routes) - count),
        scratch_shapes=work + scalars + [pltpu.SemaphoreType.DMA((2,))],
        name="near",
        **shared,
    )(words, lists, *products)
    near_arrivals = [lax.ppermute(x, "tiles", route) for x, route in zip(near_sends, routes[count:])]
    local = pl.pallas_call(
        local_kernel,
        out_shape=whole,
        in_specs=[VM, VM, ANY] + [VM] * PARTS,
        out_specs=VM,
        scratch_shapes=work + scalars + [pltpu.SemaphoreType.DMA((2,))],
        name="local",
        **shared,
    )(words, lists, near_sends[0], *products)
    local = pl.pallas_call(
        functools.partial(arrive_kernel, 0, table),
        out_shape=whole,
        in_specs=[VM] * (2 + count),
        out_specs=VM,
        scratch_shapes=[pltpu.SMEM(recv_list.shape, jnp.int32), pltpu.SemaphoreType.DMA],
        compiler_params=pltpu.CompilerParams(vmem_limit_bytes=12 * 1024 * 1024),
        name="arrive",
    )(recv_list, local, *arrivals)
    return count, table, held, local, near_arrivals


def body(n, features, weights, gain, rulebook, recv_list, coarse_send, coarse_place):
    tile_count, _, channels = features.shape
    quarter = weights.shape[2]
    small = pltpu.CompilerParams(vmem_limit_bytes=12 * 1024 * 1024)

    count, table, held, local, arrivals = call_rules(n, features, weights, rulebook, recv_list)
    conv, sums = pl.pallas_call(
        functools.partial(combine_kernel, count, table),
        out_shape=[
            jax.ShapeDtypeStruct((tile_count, HALF, 128), F32),
            jax.ShapeDtypeStruct((2, tile_count * HALF), F32),
        ],
        in_specs=[VM] * (2 + len(arrivals)),
        out_specs=[VM, VM],
        scratch_shapes=[pltpu.SMEM(recv_list.shape, jnp.int32), pltpu.SemaphoreType.DMA],
        compiler_params=small,
        name="combine",
    )(recv_list, local, *arrivals)
    own = pl.pallas_call(
        own_kernel,
        out_shape=jax.ShapeDtypeStruct((tile_count, HALF, 128), F32),
        in_specs=[VM, ANY],
        out_specs=VM,
        compiler_params=small,
        name="own",
    )(held, sums)
    wide = lax.axis_size("chan")
    others = [lax.ppermute(sums, "chan", [(i, i ^ m) for i in range(wide)]) for m in range(1, wide)]
    slot_count = coarse_place.shape[1]
    parent_count = tile_count // 8
    packed, outbound = pl.pallas_call(
        functools.partial(norm_kernel, channels),
        out_shape=[
            jax.ShapeDtypeStruct((tile_count, HALF, 128), BF),
            jax.ShapeDtypeStruct((slot_count, HALF, 128), BF),
        ],
        in_specs=[VM] * 9,
        out_specs=[VM, VM],
        scratch_shapes=[pltpu.SMEM(coarse_send.shape, jnp.int32), pltpu.SemaphoreType.DMA],
        compiler_params=small,
        name="norm",
    )(
        conv,
        own,
        jnp.tile(gain.astype(F32), 2).reshape(1, 128),
        jnp.asarray(pool_matrix(), BF),
        coarse_send,
        sums,
        *others,
    )
    landed = lax.all_to_all(outbound, "tiles", split_axis=0, concat_axis=0, tiled=True)
    skip = pl.pallas_call(
        unpack_kernel,
        out_shape=jax.ShapeDtypeStruct((tile_count, VOX, quarter), BF),
        in_specs=[VM],
        out_specs=VM,
        compiler_params=small,
        name="unpack",
    )(packed)
    coarse = pl.pallas_call(
        place_kernel,
        out_shape=jax.ShapeDtypeStruct((parent_count, VOX, quarter), BF),
        in_specs=[VM, VM],
        out_specs=VM,
        compiler_params=small,
        name="place",
    )(coarse_place, landed)
    return (skip, coarse)


def solution(mesh):
    in_specs = (
        P("tiles", None, None),
        P(None, None, "chan"),
        P("chan"),
        P("tiles", None),
        P("tiles", None),
        P("tiles", None),
        P("tiles", None),
    )
    out_specs = (P("tiles", None, "chan"), P("tiles", None, "chan"))
    return jax.shard_map(
        functools.partial(body, mesh.shape["tiles"]),
        mesh=mesh,
        in_specs=in_specs,
        out_specs=out_specs,
        check_vma=False,
    )
```

```python
import functools

import jax
import jax.numpy as jnp
import numpy as np
from jax import lax
from jax.experimental import pallas as pl
from jax.experimental.pallas import tpu as pltpu
from jax.sharding import PartitionSpec as P

EPS = 1e-05
REACH = 4
VOX = 64
HALF = 32
BF = jnp.bfloat16
F32 = jnp.float32
PAD = 64
UNROLL = 8
F_PARTS = 1
PARTS = 2
PER_PART = 7
ORDER = (0, 5, 4, 1, 2, 6, 3)


def perfect(n):
    real = [(i, j) for i in range(n) for j in range(i + 1, n) if j - i <= REACH]
    fill = [(0, 1), (0, 1), (0, 2), (6, 7), (6, 7), (5, 7)]
    first = [(i, i + REACH) for i in range(n - REACH)]
    start = [(p, True) for p in real if p not in first] + [(p, False) for p in fill]

    def crossing(found):
        return -sum(i < n // 2 <= j for (i, j), _ in found)

    def split(left):
        if not left:
            return []
        here = left[0]

        def grow(chosen, rest):
            used = {i for p, _ in chosen for i in p}
            if len(used) == n:
                yield chosen, rest
                return
            low = min(set(range(n)) - used)
            for k, item in enumerate(rest):
                if low in item[0] and not used & set(item[0]):
                    yield from grow(chosen + [item], rest[:k] + rest[k + 1 :])

        for chosen, rest in grow([here], left[1:]):
            more = split(rest)
            if more is not None:
                return [chosen] + more
        return None

    found = split(start)
    return None if found is None else [[(p, True) for p in first]] + sorted(found, key=crossing)


def matchings(n):
    found = perfect(n) if n == 2 * REACH else None
    if found is not None:
        found = [found[i] for i in ORDER]
    if found is None:
        found = []
        for d in range(REACH, 0, -1):
            for parity in (0, 1):
                pairs = [(i, i + d) for i in range(n - d) if (i // d) % 2 == parity]
                rest = [i for i in range(n) if all(i not in p for p in pairs)]
                if pairs:
                    found.append([(p, True) for p in pairs] + [(p, False) for p in zip(rest[::2], rest[1::2])])
    routes = [[q for p, _ in way for q in (p, p[::-1])] for way in found]
    table = np.full((n, 16), -1, np.int32)
    table[:, 15] = 0
    for m, way in enumerate(found):
        for pair, is_real in way:
            for e, other in (pair, pair[::-1]):
                if is_real:
                    gap = other - e
                    table[e, m] = REACH - 1 + gap if gap > 0 else -gap - 1
                    table[e, 15] += m << (4 * (gap - 1 if gap > 0 else REACH - 1 - gap))
    return routes, table


def pick(e, values):
    found = jnp.int32(int(values[0]))
    for i in range(1, len(values)):
        found = jnp.where(e == i, jnp.int32(int(values[i])), found)
    return found


def lane_iota(shape):
    return lax.broadcasted_iota(jnp.int32, shape, len(shape) - 1)


def dims_of(code):
    return (lax.div(code, 9) - 1, lax.rem(lax.div(code, 3), 3) - 1, lax.rem(code, 3) - 1)


def rules_matmul(f_ref, w_ref, y_refs, ready, beside):
    rows = f_ref.shape[0]
    span = rows + 2 * PAD
    depth = w_ref.shape[0]
    steps = range(0, depth, 256)
    for number, q in enumerate(steps):
        width = min(256, depth - q)
        cuts = F_PARTS if number == 0 else 1
        size = rows // cuts
        for h in range(cuts):
            ready(number, h)
            part = lax.dot_general(
                f_ref[h * size : (h + 1) * size, :],
                w_ref[q : q + width, :],
                (((1,), (1,)), ((), ())),
                preferred_element_type=F32,
            )
            for s in range(0, width, 128):
                wide = min(128, width - s)
                y_ref = y_refs[(q + s) // 128 // PER_PART]
                base = ((q + s) // 128 % PER_PART) * span + PAD + h * size
                y_ref[base : base + size, 0:wide] = part[:, s : s + wide]
        beside(number, len(steps))


def rules_add(words, lists, part, y_refs, acc_ref):
    voxel = lax.broadcasted_iota(jnp.int32, (VOX, 128), 0)
    have = jnp.where(lane_iota((VOX, 128)) < 64, 1 << 21, 1 << 22)
    for dim, place in enumerate((lax.div(voxel, 16), lax.rem(lax.div(voxel, 4), 4), lax.rem(voxel, 4))):
        have = have + jnp.left_shift(jnp.full_like(place, 15), 3 - place + 7 * dim)

    for which, y_ref in enumerate(y_refs):
        kind = part * PARTS + which
        add_listed(words, lists, kind * words.shape[1], words[3, 128 * kind], have, y_ref, acc_ref)


def add_listed(words, lists, start, count, have, y_ref, acc_ref):
    def several(i, c):
        for u in range(UNROLL):
            r = lists[start + i * UNROLL + u]
            packed = words[0, r]
            need = words[1, r]
            taken = y_ref[pl.ds(lax.shift_right_logical(packed, 8), VOX), :]
            t = packed & 255
            half = acc_ref[u % 2]
            half[t] = half[t] + jnp.where((have & need) == need, taken, 0.0)
        return c

    lax.fori_loop(0, lax.div(count + (UNROLL - 1), UNROLL), several, 0)


def zero_blocks(acc_ref):
    def zero(i, c):
        for half in acc_ref:
            half[i] = jnp.zeros((VOX, 128), F32)
        return c

    lax.fori_loop(0, acc_ref[0].shape[0], zero, 0, unroll=8)


def folded(acc_ref, t):
    first = lane_iota((HALF, 128)) < 64
    low = acc_ref[0][t, 0:HALF, :] + acc_ref[1][t, 0:HALF, :]
    high = acc_ref[0][t, HALF:VOX, :] + acc_ref[1][t, HALF:VOX, :]
    low = low + pltpu.roll(low, 64, 1)
    high = high + pltpu.roll(high, 64, 1)
    return jnp.where(first, low, high)


def emit_sends(acc_ref, sends):
    slots = sends[0].shape[0]
    for m, send_ref in enumerate(sends):

        def emit(i, c, send_ref=send_ref, base=slots * m):
            send_ref[i] = folded(acc_ref, base + i).astype(BF)
            return c

        lax.fori_loop(0, slots, emit, 0, unroll=16)


def far_kernel(count, table, tile_count, rules_hbm, f_hbm, w_hbm, *rest):
    sends, rest = rest[:count], rest[count:]
    f_ref, y_refs, rest = rest[0], rest[1 : 1 + PARTS], rest[1 + PARTS :]
    words_v, lists_v, *acc_ref, w_ref, rules_ref, words_s, lists, sems = rest
    rows = tile_count * VOX
    span = rows + 2 * PAD
    rule_rows = rules_ref.shape[1]
    wide = words_v.shape[1]
    slots = tile_count // 4
    depth = w_ref.shape[0]
    size = rows // F_PARTS
    rules_copy = pltpu.make_async_copy(rules_hbm, rules_ref, sems.at[0])
    f_copies = [
        pltpu.make_async_copy(f_hbm.at[pl.ds(h * size, size)], f_ref.at[pl.ds(h * size, size)], sems.at[3 + h])
        for h in range(F_PARTS)
    ]
    w_copies = [
        pltpu.make_async_copy(w_hbm.at[pl.ds(q, width)], w_ref.at[pl.ds(q, width)], sems.at[3 + F_PARTS + i])
        for i, (q, width) in enumerate([(0, 256), (256, depth - 256)])
    ]
    for copy in [rules_copy, w_copies[0], *f_copies, w_copies[1]]:
        copy.start()
    before = lax.broadcasted_iota(jnp.int32, (rule_rows, rule_rows), 0)
    before = (before <= lane_iota((rule_rows, rule_rows))).astype(F32).astype(BF)
    zero_blocks(acc_ref)
    rules_copy.wait()
    tile = rules_ref[0:1, :]
    kernel = rules_ref[1:2, :]
    heading = rules_ref[2:3, :]
    target = rules_ref[3:4, :]
    code = jnp.minimum(kernel, 26)
    shift = jnp.zeros_like(code)
    need = jnp.where(lax.rem(code, 2) == 0, 1 << 21, 1 << 22)
    for dim, (step, turn) in enumerate(zip(dims_of(code), dims_of(heading))):
        move = step - 4 * turn
        shift = shift + move * (16, 4, 1)[dim]
        need = need + jnp.left_shift(jnp.full_like(move, 1), move + (3 + 7 * dim))
    sent = jnp.maximum(target - tile_count, 0)
    group = lax.div(sent, slots)
    coded = jnp.full_like(group, pick(lax.axis_index("tiles"), table[:, 15]))
    way = lax.shift_right_logical(coded, 4 * group) & 15
    near = way >= count
    place = jnp.where(near, way - count, way) * slots + lax.rem(sent, slots)
    part = jnp.where(target < tile_count, 2, jnp.where(near, 1, 0))
    pair = lax.div(code, 2)
    part = jnp.where(kernel < 27, part * PARTS + lax.div(pair, PER_PART), 3 * PARTS)
    kind = lax.broadcasted_iota(jnp.int32, (8, rule_rows), 0)
    flags = jnp.where(kind == part, 1.0, 0.0)
    upto = jnp.dot(flags.astype(BF), before, preferred_element_type=F32)
    at = jnp.sum(flags * (upto - 1.0 + (kind * wide).astype(F32)), axis=0, keepdims=True)
    first_row = lax.rem(pair, PER_PART) * span + PAD + tile * VOX + shift
    words_v[...] = jnp.zeros(words_v.shape, jnp.int32)
    words_v[0:1, 0:rule_rows] = first_row * 256 + jnp.where(target < tile_count, target, place)
    words_v[1:2, 0:rule_rows] = need
    words_v[2:3, 0:rule_rows] = at.astype(jnp.int32)
    words_v[0:1, rule_rows:wide] = jnp.full((1, wide - rule_rows), PAD * 256, jnp.int32)
    words_v[1:2, rule_rows:wide] = jnp.full((1, wide - rule_rows), 1 << 23, jnp.int32)
    for c in range(3 * PARTS):
        total = upto[c : c + 1, rule_rows - 1 : rule_rows]
        words_v[3:4, 128 * c : 128 * c + 128] = jnp.broadcast_to(total, (1, 128)).astype(jnp.int32)
    to_scalars = pltpu.make_async_copy(words_v, words_s, sems.at[1])
    to_scalars.start()

    def ready(number, h):
        if number == 0:
            if h == 0:
                w_copies[0].wait()
            f_copies[h].wait()
        if number == 1:
            w_copies[1].wait()

    def list_some(number, steps):
        if number == 0:
            to_scalars.wait()
        share = -(-rule_rows // (steps - 1))
        for r in range(number * share, min(rule_rows, (number + 1) * share)):
            lists[words_s[2, r]] = r

    rules_matmul(f_ref, w_ref, y_refs, ready, list_some)
    for c in range(3 * PARTS):
        for u in range(UNROLL):
            lists[c * wide + words_s[3, 128 * c] + u] = rule_rows
    hand_on = pltpu.make_async_copy(lists, lists_v, sems.at[2])
    hand_on.start()
    rules_add(words_s, lists, 0, y_refs, acc_ref)
    emit_sends(acc_ref, sends)
    hand_on.wait()


def near_kernel(words_v, lists_v, *rest):
    y_refs, sends = rest[:PARTS], rest[PARTS:-5]
    *acc_ref, words, lists, sems = rest[-5:]
    copies = [
        pltpu.make_async_copy(words_v, words, sems.at[0]),
        pltpu.make_async_copy(lists_v, lists, sems.at[1]),
    ]
    for copy in copies:
        copy.start()
    zero_blocks(acc_ref)
    for copy in copies:
        copy.wait()
    rules_add(words, lists, 1, y_refs, acc_ref)
    emit_sends(acc_ref, sends)


def add_arrivals(first, table, blocks, list_ref, out_ref):
    e = lax.axis_index("tiles")
    slots = blocks[0].shape[0]
    for m, block in enumerate(blocks):
        group = pick(e, table[:, first + m])

        @pl.when(group >= 0)
        def _(block=block, group=group):
            for i in range(slots):
                t = list_ref[0, group * slots + i]
                out_ref[t] = out_ref[t] + block[i].astype(F32)


def local_kernel(words_v, lists_v, _after, *rest):
    y_refs, (local_ref, *acc_ref, words, lists, sems) = rest[:PARTS], rest[PARTS:]
    copies = [
        pltpu.make_async_copy(words_v, words, sems.at[0]),
        pltpu.make_async_copy(lists_v, lists, sems.at[1]),
    ]
    for copy in copies:
        copy.start()
    zero_blocks(acc_ref)
    for copy in copies:
        copy.wait()
    rules_add(words, lists, 2, y_refs, acc_ref)

    def keep(t, c):
        local_ref[t] = folded(acc_ref, t)
        return c

    lax.fori_loop(0, acc_ref[0].shape[0], keep, 0, unroll=16)


def arrive_kernel(first, table, list_v, local_ref, *rest):
    blocks = rest[:-3]
    out_ref, list_ref, sem = rest[-3:]
    copy = pltpu.make_async_copy(list_v, list_ref, sem)
    copy.start()
    out_ref[...] = local_ref[...]
    copy.wait()
    add_arrivals(first, table, blocks, list_ref, out_ref)


def own_kernel(f_ref, _after, own_ref):
    c = lax.axis_index("chan")
    at = pl.multiple_of(lax.div(c, 2) * 128, 128)
    odd = lax.rem(c, 2) == 1
    first = lane_iota((HALF, 128)) < 64

    def pack(t, c):
        block = f_ref[pl.ds(pl.multiple_of(t * VOX, VOX), VOX), pl.ds(at, 128)].astype(F32)
        low, high = block[:HALF], block[HALF:]
        even_form = jnp.where(first, low, pltpu.roll(high, 64, 1))
        odd_form = jnp.where(first, pltpu.roll(low, 64, 1), high)
        own_ref[t] = jnp.where(odd, odd_form, even_form)
        return c

    lax.fori_loop(0, own_ref.shape[0], pack, 0, unroll=8)


def combine_kernel(first, table, list_v, local_ref, *rest):
    blocks = rest[:-4]
    conv_ref, sums_ref, list_ref, sem = rest[-4:]
    copy = pltpu.make_async_copy(list_v, list_ref, sem)
    copy.start()
    tile_count = local_ref.shape[0]
    conv_ref[...] = local_ref[...]
    copy.wait()
    add_arrivals(first, table, blocks, list_ref, conv_ref)
    rows = tile_count * HALF
    pick = (lane_iota((2, 256)) // 64 % 2 == lax.broadcasted_iota(jnp.int32, (2, 256), 0)).astype(BF)
    step = rows
    for at in range(0, rows, step):
        value = conv_ref[at // HALF : (at + step) // HALF].reshape(step, 128)
        square = value * value
        top = square.astype(BF)
        rest_of = (square - top.astype(F32)).astype(BF)
        sums_ref[:, at : at + step] = lax.dot_general(
            pick,
            jnp.concatenate([top, rest_of], axis=1),
            (((1,), (1,)), ((), ())),
            preferred_element_type=F32,
        )


def norm_kernel(channels, conv_ref, own_ref, gain_ref, pool_ref, slot_v, s0, s1, s2, s3, whole_ref, out_ref, slot_ref, sem):
    copy = pltpu.make_async_copy(slot_v, slot_ref, sem)
    copy.start()
    tile_count = conv_ref.shape[0]
    total = (s0[...] + s1[...]) + (s2[...] + s3[...])
    rest = lax.rsqrt(total * (1.0 / channels) + EPS)
    parts = []
    for _ in range(3):
        top = rest.astype(BF).astype(F32)
        parts.append(top)
        rest = rest - top
    parts = jnp.concatenate(parts, axis=0).astype(BF)
    count = parts.shape[0]
    spread = (lane_iota((count, 128)) // 64 == lax.broadcasted_iota(jnp.int32, (count, 128), 0) % 2).astype(BF)
    gain = 0.5 * gain_ref[...]
    for k in range(tile_count // 8):
        part = lax.dot_general(
            parts[:, k * 256 : (k + 1) * 256],
            spread,
            (((0,), (0,)), ((), ())),
            preferred_element_type=F32,
        )
        half = gain * conv_ref[8 * k : 8 * k + 8].reshape(256, 128) * part
        hidden = half + half * jnp.tanh(half)
        whole = (own_ref[8 * k : 8 * k + 8].reshape(256, 128) + hidden).astype(BF)
        whole_ref[8 * k : 8 * k + 8] = whole.reshape(8, HALF, 128)
    copy.wait()
    for k in range(tile_count // 8):
        whole = whole_ref[8 * k : 8 * k + 8].reshape(256, 128)
        out_ref[slot_ref[0, k]] = jnp.dot(pool_ref[...], whole, preferred_element_type=F32).astype(BF)


def unpack_kernel(whole_ref, skip_ref):
    skip_ref[:, 0:HALF, :] = whole_ref[:, :, 0:64]
    skip_ref[:, HALF:VOX, :] = whole_ref[:, :, 64:128]


def place_kernel(place_ref, landed_ref, out_ref):
    slots = landed_ref.shape[0]
    where = [jnp.broadcast_to(place_ref[:, i : i + 1], (HALF, 128)) for i in range(slots)]
    for p in range(out_ref.shape[0]):
        block = landed_ref[0].astype(F32)
        for i in range(1, slots):
            block = jnp.where(where[i] == p, landed_ref[i].astype(F32), block)
        block = block.astype(BF)
        for ox in range(2):
            for px in range(2):
                row = 16 * (2 * ox + px)
                out_ref[p, row : row + 16, :] = block[16 * ox : 16 * ox + 16, 64 * px : 64 * px + 64]


def pool_matrix():
    out = np.zeros((2, 4, 4, 2, 2, 2, 2, 4, 4), np.float32)
    for ox in range(2):
        for y in range(4):
            for z in range(4):
                out[ox, y, z, ox, y // 2, z // 2, :, 2 * (y % 2) : 2 * (y % 2) + 2, 2 * (z % 2) : 2 * (z % 2) + 2] = 0.125
    return out.reshape(32, 256)


VM = pl.BlockSpec(memory_space=pltpu.VMEM)
SM = pl.BlockSpec(memory_space=pltpu.SMEM)
ANY = pl.BlockSpec(memory_space=pl.ANY)
HBM = pl.BlockSpec(memory_space=pltpu.HBM)


def call_rules(n, features, weights, rulebook, recv_list):
    tile_count, _, channels = features.shape
    offsets, _, quarter = weights.shape
    rule_rows = rulebook.shape[0]
    routes, table = matchings(n)
    count = len(routes) // 2
    slots = tile_count // 4
    span = tile_count * VOX + 2 * PAD
    wide = rule_rows + 128
    lists_shape = ((3 * PARTS + 1) * wide,)
    scalars = [pltpu.SMEM((8, wide), jnp.int32), pltpu.SMEM(lists_shape, jnp.int32)]
    flat = features.reshape(tile_count * VOX, channels)
    flat_weights = weights.transpose(0, 2, 1).reshape(offsets * quarter, channels)
    block = jax.ShapeDtypeStruct((slots, HALF, 128), BF)
    whole = jax.ShapeDtypeStruct((tile_count, HALF, 128), F32)
    work = [pltpu.VMEM((tile_count, VOX, 128), F32)] * 2
    flops = 2 * tile_count * VOX * channels * offsets * quarter
    shared = dict(
        compiler_params=pltpu.CompilerParams(vmem_limit_bytes=16 * 1024 * 1024),
        cost_estimate=pl.CostEstimate(flops=flops, bytes_accessed=8 << 20, transcendentals=0),
    )
    made = pl.pallas_call(
        functools.partial(far_kernel, count, table, tile_count),
        out_shape=[block] * count
        + [jax.ShapeDtypeStruct(flat.shape, BF), jax.ShapeDtypeStruct((PER_PART * span, 128), F32)]
        + [jax.ShapeDtypeStruct((PER_PART * span, 128), F32)] * (PARTS - 1)
        + [jax.ShapeDtypeStruct((8, wide), jnp.int32), jax.ShapeDtypeStruct(lists_shape, jnp.int32)],
        in_specs=[HBM] * 3,
        out_specs=[VM] * (count + 3 + PARTS),
        scratch_shapes=work
        + [
            pltpu.VMEM(flat_weights.shape, BF),
            pltpu.VMEM((4, rule_rows), jnp.int32),
            *scalars,
            pltpu.SemaphoreType.DMA((5 + F_PARTS,)),
        ],
        name="far",
        **shared,
    )(*(pltpu.with_memory_space_constraint(x, pltpu.HBM) for x in (rulebook.T, flat, flat_weights)))
    far_sends = made[:count]
    held, *products, words, lists = made[count:]
    arrivals = [lax.ppermute(x, "tiles", route) for x, route in zip(far_sends, routes[:count])]
    near_sends = pl.pallas_call(
        near_kernel,
        out_shape=[block] * (len(routes) - count),
        in_specs=[VM] * (2 + PARTS),
        out_specs=[VM] * (len(routes) - count),
        scratch_shapes=work + scalars + [pltpu.SemaphoreType.DMA((2,))],
        name="near",
        **shared,
    )(words, lists, *products)
    near_arrivals = [lax.ppermute(x, "tiles", route) for x, route in zip(near_sends, routes[count:])]
    local = pl.pallas_call(
        local_kernel,
        out_shape=whole,
        in_specs=[VM, VM, ANY] + [VM] * PARTS,
        out_specs=VM,
        scratch_shapes=work + scalars + [pltpu.SemaphoreType.DMA((2,))],
        name="local",
        **shared,
    )(words, lists, near_sends[0], *products)
    local = pl.pallas_call(
        functools.partial(arrive_kernel, 0, table),
        out_shape=whole,
        in_specs=[VM] * (2 + count),
        out_specs=VM,
        scratch_shapes=[pltpu.SMEM(recv_list.shape, jnp.int32), pltpu.SemaphoreType.DMA],
        compiler_params=pltpu.CompilerParams(vmem_limit_bytes=12 * 1024 * 1024),
        name="arrive",
    )(recv_list, local, *arrivals)
    return count, table, held, local, near_arrivals


def body(n, features, weights, gain, rulebook, recv_list, coarse_send, coarse_place):
    tile_count, _, channels = features.shape
    quarter = weights.shape[2]
    small = pltpu.CompilerParams(vmem_limit_bytes=12 * 1024 * 1024)

    count, table, held, local, arrivals = call_rules(n, features, weights, rulebook, recv_list)
    conv, sums = pl.pallas_call(
        functools.partial(combine_kernel, count, table),
        out_shape=[
            jax.ShapeDtypeStruct((tile_count, HALF, 128), F32),
            jax.ShapeDtypeStruct((2, tile_count * HALF), F32),
        ],
        in_specs=[VM] * (2 + len(arrivals)),
        out_specs=[VM, VM],
        scratch_shapes=[pltpu.SMEM(recv_list.shape, jnp.int32), pltpu.SemaphoreType.DMA],
        compiler_params=small,
        name="combine",
    )(recv_list, local, *arrivals)
    own = pl.pallas_call(
        own_kernel,
        out_shape=jax.ShapeDtypeStruct((tile_count, HALF, 128), F32),
        in_specs=[VM, ANY],
        out_specs=VM,
        compiler_params=small,
        name="own",
    )(held, sums)
    wide = lax.axis_size("chan")
    others = [lax.ppermute(sums, "chan", [(i, i ^ m) for i in range(wide)]) for m in range(1, wide)]
    slot_count = coarse_place.shape[1]
    parent_count = tile_count // 8
    packed, outbound = pl.pallas_call(
        functools.partial(norm_kernel, channels),
        out_shape=[
            jax.ShapeDtypeStruct((tile_count, HALF, 128), BF),
            jax.ShapeDtypeStruct((slot_count, HALF, 128), BF),
        ],
        in_specs=[VM] * 9,
        out_specs=[VM, VM],
        scratch_shapes=[pltpu.SMEM(coarse_send.shape, jnp.int32), pltpu.SemaphoreType.DMA],
        compiler_params=small,
        name="norm",
    )(
        conv,
        own,
        jnp.tile(gain.astype(F32), 2).reshape(1, 128),
        jnp.asarray(pool_matrix(), BF),
        coarse_send,
        sums,
        *others,
    )
    landed = lax.all_to_all(outbound, "tiles", split_axis=0, concat_axis=0, tiled=True)
    skip = pl.pallas_call(
        unpack_kernel,
        out_shape=jax.ShapeDtypeStruct((tile_count, VOX, quarter), BF),
        in_specs=[VM],
        out_specs=VM,
        compiler_params=small,
        name="unpack",
    )(packed)
    coarse = pl.pallas_call(
        place_kernel,
        out_shape=jax.ShapeDtypeStruct((parent_count, VOX, quarter), BF),
        in_specs=[VM, VM],
        out_specs=VM,
        compiler_params=small,
        name="place",
    )(coarse_place, landed)
    return (skip, coarse)


def solution(mesh):
    in_specs = (
        P("tiles", None, None),
        P(None, None, "chan"),
        P("chan"),
        P("tiles", None),
        P("tiles", None),
        P("tiles", None),
        P("tiles", None),
    )
    out_specs = (P("tiles", None, "chan"), P("tiles", None, "chan"))
    return jax.shard_map(
        functools.partial(body, mesh.shape["tiles"]),
        mesh=mesh,
        in_specs=in_specs,
        out_specs=out_specs,
        check_vma=False,
    )
```

```python
import functools

import jax
import jax.numpy as jnp
import numpy as np
from jax import lax
from jax.experimental import pallas as pl
from jax.experimental.pallas import tpu as pltpu
from jax.sharding import PartitionSpec as P

EPS = 1e-05
BF_MAX = float(jnp.finfo(jnp.bfloat16).max)
REACH = 4
VOX = 64
HALF = 32
BF = jnp.bfloat16
F32 = jnp.float32
PAD = 64
UNROLL = 8
F_PARTS = 1
PARTS = 2
PER_PART = 7
ORDER = (0, 5, 4, 1, 2, 6, 3)


def perfect(n):
    real = [(i, j) for i in range(n) for j in range(i + 1, n) if j - i <= REACH]
    fill = [(0, 1), (0, 1), (0, 2), (6, 7), (6, 7), (5, 7)]
    first = [(i, i + REACH) for i in range(n - REACH)]
    start = [(p, True) for p in real if p not in first] + [(p, False) for p in fill]

    def crossing(found):
        return -sum(i < n // 2 <= j for (i, j), _ in found)

    def split(left):
        if not left:
            return []
        here = left[0]

        def grow(chosen, rest):
            used = {i for p, _ in chosen for i in p}
            if len(used) == n:
                yield chosen, rest
                return
            low = min(set(range(n)) - used)
            for k, item in enumerate(rest):
                if low in item[0] and not used & set(item[0]):
                    yield from grow(chosen + [item], rest[:k] + rest[k + 1 :])

        for chosen, rest in grow([here], left[1:]):
            more = split(rest)
            if more is not None:
                return [chosen] + more
        return None

    found = split(start)
    return None if found is None else [[(p, True) for p in first]] + sorted(found, key=crossing)


def matchings(n):
    found = perfect(n) if n == 2 * REACH else None
    if found is not None:
        found = [found[i] for i in ORDER]
    if found is None:
        found = []
        for d in range(REACH, 0, -1):
            for parity in (0, 1):
                pairs = [(i, i + d) for i in range(n - d) if (i // d) % 2 == parity]
                rest = [i for i in range(n) if all(i not in p for p in pairs)]
                if pairs:
                    found.append([(p, True) for p in pairs] + [(p, False) for p in zip(rest[::2], rest[1::2])])
    routes = [[q for p, _ in way for q in (p, p[::-1])] for way in found]
    table = np.full((n, 16), -1, np.int32)
    table[:, 15] = 0
    for m, way in enumerate(found):
        for pair, is_real in way:
            for e, other in (pair, pair[::-1]):
                if is_real:
                    gap = other - e
                    table[e, m] = REACH - 1 + gap if gap > 0 else -gap - 1
                    table[e, 15] += m << (4 * (gap - 1 if gap > 0 else REACH - 1 - gap))
    return routes, table


def pick(e, values):
    found = jnp.int32(int(values[0]))
    for i in range(1, len(values)):
        found = jnp.where(e == i, jnp.int32(int(values[i])), found)
    return found


def lane_iota(shape):
    return lax.broadcasted_iota(jnp.int32, shape, len(shape) - 1)


def dims_of(code):
    return (lax.div(code, 9) - 1, lax.rem(lax.div(code, 3), 3) - 1, lax.rem(code, 3) - 1)


def rules_matmul(f_ref, w_ref, y_refs, ready, beside):
    rows = f_ref.shape[0]
    span = rows + 2 * PAD
    depth = w_ref.shape[0]
    steps = range(0, depth, 256)
    for number, q in enumerate(steps):
        width = min(256, depth - q)
        cuts = F_PARTS if number == 0 else 1
        size = rows // cuts
        for h in range(cuts):
            ready(number, h)
            part = lax.dot_general(
                f_ref[h * size : (h + 1) * size, :],
                w_ref[q : q + width, :],
                (((1,), (1,)), ((), ())),
                preferred_element_type=F32,
            )
            for s in range(0, width, 128):
                wide = min(128, width - s)
                y_ref = y_refs[(q + s) // 128 // PER_PART]
                base = ((q + s) // 128 % PER_PART) * span + PAD + h * size
                y_ref[base : base + size, 0:wide] = part[:, s : s + wide]
        beside(number, len(steps))


def rules_add(words, lists, part, y_refs, acc_ref):
    voxel = lax.broadcasted_iota(jnp.int32, (VOX, 128), 0)
    have = jnp.where(lane_iota((VOX, 128)) < 64, 1 << 21, 1 << 22)
    for dim, place in enumerate((lax.div(voxel, 16), lax.rem(lax.div(voxel, 4), 4), lax.rem(voxel, 4))):
        have = have + jnp.left_shift(jnp.full_like(place, 15), 3 - place + 7 * dim)

    for which, y_ref in enumerate(y_refs):
        kind = part * PARTS + which
        add_listed(words, lists, kind * words.shape[1], words[3, 128 * kind], have, y_ref, acc_ref)


def add_listed(words, lists, start, count, have, y_ref, acc_ref):
    def several(i, c):
        for u in range(UNROLL):
            r = lists[start + i * UNROLL + u]
            packed = words[0, r]
            need = words[1, r]
            taken = y_ref[pl.ds(lax.shift_right_logical(packed, 8), VOX), :]
            t = packed & 255
            half = acc_ref[u % 2]
            half[t] = half[t] + jnp.where((have & need) == need, taken, 0.0)
        return c

    lax.fori_loop(0, lax.div(count + (UNROLL - 1), UNROLL), several, 0)


def zero_blocks(acc_ref):
    def zero(i, c):
        for half in acc_ref:
            half[i] = jnp.zeros((VOX, 128), F32)
        return c

    lax.fori_loop(0, acc_ref[0].shape[0], zero, 0, unroll=8)


def folded(acc_ref, t):
    first = lane_iota((HALF, 128)) < 64
    low = acc_ref[0][t, 0:HALF, :] + acc_ref[1][t, 0:HALF, :]
    high = acc_ref[0][t, HALF:VOX, :] + acc_ref[1][t, HALF:VOX, :]
    low = low + pltpu.roll(low, 64, 1)
    high = high + pltpu.roll(high, 64, 1)
    return jnp.where(first, low, high)


def emit_sends(acc_ref, sends):
    slots = sends[0].shape[0]
    for m, send_ref in enumerate(sends):

        def emit(i, c, send_ref=send_ref, base=slots * m):
            send_ref[i] = folded(acc_ref, base + i).astype(BF)
            return c

        lax.fori_loop(0, slots, emit, 0, unroll=16)


def far_kernel(count, table, tile_count, rules_hbm, f_hbm, w_hbm, *rest):
    sends, rest = rest[:count], rest[count:]
    f_ref, y_refs, rest = rest[0], rest[1 : 1 + PARTS], rest[1 + PARTS :]
    words_v, lists_v, *acc_ref, w_ref, rules_ref, words_s, lists, sems = rest
    rows = tile_count * VOX
    span = rows + 2 * PAD
    rule_rows = rules_ref.shape[1]
    wide = words_v.shape[1]
    slots = tile_count // 4
    depth = w_ref.shape[0]
    size = rows // F_PARTS
    rules_copy = pltpu.make_async_copy(rules_hbm, rules_ref, sems.at[0])
    f_copies = [
        pltpu.make_async_copy(f_hbm.at[pl.ds(h * size, size)], f_ref.at[pl.ds(h * size, size)], sems.at[3 + h])
        for h in range(F_PARTS)
    ]
    w_copies = [
        pltpu.make_async_copy(w_hbm.at[pl.ds(q, width)], w_ref.at[pl.ds(q, width)], sems.at[3 + F_PARTS + i])
        for i, (q, width) in enumerate([(0, 256), (256, depth - 256)])
    ]
    for copy in [rules_copy, w_copies[0], *f_copies, w_copies[1]]:
        copy.start()
    before = lax.broadcasted_iota(jnp.int32, (rule_rows, rule_rows), 0)
    before = (before <= lane_iota((rule_rows, rule_rows))).astype(F32).astype(BF)
    zero_blocks(acc_ref)
    rules_copy.wait()
    tile = rules_ref[0:1, :]
    kernel = rules_ref[1:2, :]
    heading = rules_ref[2:3, :]
    target = rules_ref[3:4, :]
    code = jnp.minimum(kernel, 26)
    shift = jnp.zeros_like(code)
    need = jnp.where(lax.rem(code, 2) == 0, 1 << 21, 1 << 22)
    for dim, (step, turn) in enumerate(zip(dims_of(code), dims_of(heading))):
        move = step - 4 * turn
        shift = shift + move * (16, 4, 1)[dim]
        need = need + jnp.left_shift(jnp.full_like(move, 1), move + (3 + 7 * dim))
    sent = jnp.maximum(target - tile_count, 0)
    group = lax.div(sent, slots)
    coded = jnp.full_like(group, pick(lax.axis_index("tiles"), table[:, 15]))
    way = lax.shift_right_logical(coded, 4 * group) & 15
    near = way >= count
    place = jnp.where(near, way - count, way) * slots + lax.rem(sent, slots)
    part = jnp.where(target < tile_count, 2, jnp.where(near, 1, 0))
    pair = lax.div(code, 2)
    part = jnp.where(kernel < 27, part * PARTS + lax.div(pair, PER_PART), 3 * PARTS)
    kind = lax.broadcasted_iota(jnp.int32, (8, rule_rows), 0)
    flags = jnp.where(kind == part, 1.0, 0.0)
    upto = jnp.dot(flags.astype(BF), before, preferred_element_type=F32)
    at = jnp.sum(flags * (upto - 1.0 + (kind * wide).astype(F32)), axis=0, keepdims=True)
    first_row = lax.rem(pair, PER_PART) * span + PAD + tile * VOX + shift
    words_v[...] = jnp.zeros(words_v.shape, jnp.int32)
    words_v[0:1, 0:rule_rows] = first_row * 256 + jnp.where(target < tile_count, target, place)
    words_v[1:2, 0:rule_rows] = need
    words_v[2:3, 0:rule_rows] = at.astype(jnp.int32)
    words_v[0:1, rule_rows:wide] = jnp.full((1, wide - rule_rows), PAD * 256, jnp.int32)
    words_v[1:2, rule_rows:wide] = jnp.full((1, wide - rule_rows), 1 << 23, jnp.int32)
    for c in range(3 * PARTS):
        total = upto[c : c + 1, rule_rows - 1 : rule_rows]
        words_v[3:4, 128 * c : 128 * c + 128] = jnp.broadcast_to(total, (1, 128)).astype(jnp.int32)
    to_scalars = pltpu.make_async_copy(words_v, words_s, sems.at[1])
    to_scalars.start()

    def ready(number, h):
        if number == 0:
            if h == 0:
                w_copies[0].wait()
            f_copies[h].wait()
        if number == 1:
            w_copies[1].wait()

    def list_some(number, steps):
        if number == 0:
            to_scalars.wait()
        share = -(-rule_rows // (steps - 1))
        for r in range(number * share, min(rule_rows, (number + 1) * share)):
            lists[words_s[2, r]] = r

    rules_matmul(f_ref, w_ref, y_refs, ready, list_some)
    for c in range(3 * PARTS):
        for u in range(UNROLL):
            lists[c * wide + words_s[3, 128 * c] + u] = rule_rows
    hand_on = pltpu.make_async_copy(lists, lists_v, sems.at[2])
    hand_on.start()
    rules_add(words_s, lists, 0, y_refs, acc_ref)
    emit_sends(acc_ref, sends)
    hand_on.wait()


def near_kernel(words_v, lists_v, *rest):
    y_refs, sends = rest[:PARTS], rest[PARTS:-5]
    *acc_ref, words, lists, sems = rest[-5:]
    copies = [
        pltpu.make_async_copy(words_v, words, sems.at[0]),
        pltpu.make_async_copy(lists_v, lists, sems.at[1]),
    ]
    for copy in copies:
        copy.start()
    zero_blocks(acc_ref)
    for copy in copies:
        copy.wait()
    rules_add(words, lists, 1, y_refs, acc_ref)
    emit_sends(acc_ref, sends)


def add_arrivals(first, table, blocks, list_ref, out_ref):
    e = lax.axis_index("tiles")
    slots = blocks[0].shape[0]
    for m, block in enumerate(blocks):
        group = pick(e, table[:, first + m])

        @pl.when(group >= 0)
        def _(block=block, group=group):
            for i in range(slots):
                t = list_ref[0, group * slots + i]
                out_ref[t] = out_ref[t] + block[i].astype(F32)


def local_kernel(words_v, lists_v, _after, *rest):
    y_refs, (local_ref, *acc_ref, words, lists, sems) = rest[:PARTS], rest[PARTS:]
    copies = [
        pltpu.make_async_copy(words_v, words, sems.at[0]),
        pltpu.make_async_copy(lists_v, lists, sems.at[1]),
    ]
    for copy in copies:
        copy.start()
    zero_blocks(acc_ref)
    for copy in copies:
        copy.wait()
    rules_add(words, lists, 2, y_refs, acc_ref)

    def keep(t, c):
        local_ref[t] = folded(acc_ref, t)
        return c

    lax.fori_loop(0, acc_ref[0].shape[0], keep, 0, unroll=16)


def arrive_kernel(first, table, list_v, local_ref, *rest):
    blocks = rest[:-3]
    out_ref, list_ref, sem = rest[-3:]
    copy = pltpu.make_async_copy(list_v, list_ref, sem)
    copy.start()
    out_ref[...] = local_ref[...]
    copy.wait()
    add_arrivals(first, table, blocks, list_ref, out_ref)


def own_kernel(f_ref, _after, own_ref):
    c = lax.axis_index("chan")
    at = pl.multiple_of(lax.div(c, 2) * 128, 128)
    odd = lax.rem(c, 2) == 1
    first = lane_iota((HALF, 128)) < 64

    def pack(t, c):
        block = f_ref[pl.ds(pl.multiple_of(t * VOX, VOX), VOX), pl.ds(at, 128)].astype(F32)
        low, high = block[:HALF], block[HALF:]
        even_form = jnp.where(first, low, pltpu.roll(high, 64, 1))
        odd_form = jnp.where(first, pltpu.roll(low, 64, 1), high)
        own_ref[t] = jnp.where(odd, odd_form, even_form)
        return c

    lax.fori_loop(0, own_ref.shape[0], pack, 0, unroll=8)


def combine_kernel(first, table, list_v, local_ref, *rest):
    blocks = rest[:-4]
    conv_ref, sums_ref, list_ref, sem = rest[-4:]
    copy = pltpu.make_async_copy(list_v, list_ref, sem)
    copy.start()
    tile_count = local_ref.shape[0]
    conv_ref[...] = local_ref[...]
    copy.wait()
    add_arrivals(first, table, blocks, list_ref, conv_ref)
    rows = tile_count * HALF
    pick = (lane_iota((2, 256)) // 64 % 2 == lax.broadcasted_iota(jnp.int32, (2, 256), 0)).astype(BF)
    step = rows
    for at in range(0, rows, step):
        value = conv_ref[at // HALF : (at + step) // HALF].reshape(step, 128)
        square = value * value
        top = jnp.minimum(square, BF_MAX).astype(BF)
        rest_of = (square - top.astype(F32)).astype(BF)
        sums_ref[:, at : at + step] = lax.dot_general(
            pick,
            jnp.concatenate([top, rest_of], axis=1),
            (((1,), (1,)), ((), ())),
            preferred_element_type=F32,
        )


def norm_kernel(channels, conv_ref, own_ref, gain_ref, pool_ref, slot_v, s0, s1, s2, s3, whole_ref, out_ref, slot_ref, sem):
    copy = pltpu.make_async_copy(slot_v, slot_ref, sem)
    copy.start()
    tile_count = conv_ref.shape[0]
    total = (s0[...] + s1[...]) + (s2[...] + s3[...])
    rest = lax.rsqrt(total * (1.0 / channels) + EPS)
    parts = []
    for _ in range(3):
        top = rest.astype(BF).astype(F32)
        parts.append(top)
        rest = rest - top
    parts = jnp.concatenate(parts, axis=0).astype(BF)
    count = parts.shape[0]
    spread = (lane_iota((count, 128)) // 64 == lax.broadcasted_iota(jnp.int32, (count, 128), 0) % 2).astype(BF)
    gain = 0.5 * gain_ref[...]
    for k in range(tile_count // 8):
        part = lax.dot_general(
            parts[:, k * 256 : (k + 1) * 256],
            spread,
            (((0,), (0,)), ((), ())),
            preferred_element_type=F32,
        )
        half = gain * conv_ref[8 * k : 8 * k + 8].reshape(256, 128) * part
        hidden = half + half * jnp.tanh(half)
        whole = (own_ref[8 * k : 8 * k + 8].reshape(256, 128) + hidden).astype(BF)
        whole_ref[8 * k : 8 * k + 8] = whole.reshape(8, HALF, 128)
    copy.wait()
    for k in range(tile_count // 8):
        whole = whole_ref[8 * k : 8 * k + 8].reshape(256, 128)
        out_ref[slot_ref[0, k]] = jnp.dot(pool_ref[...], whole, preferred_element_type=F32).astype(BF)


def unpack_kernel(whole_ref, skip_ref):
    skip_ref[:, 0:HALF, :] = whole_ref[:, :, 0:64]
    skip_ref[:, HALF:VOX, :] = whole_ref[:, :, 64:128]


def place_kernel(place_ref, landed_ref, out_ref):
    slots = landed_ref.shape[0]
    where = [jnp.broadcast_to(place_ref[:, i : i + 1], (HALF, 128)) for i in range(slots)]
    for p in range(out_ref.shape[0]):
        block = landed_ref[0].astype(F32)
        for i in range(1, slots):
            block = jnp.where(where[i] == p, landed_ref[i].astype(F32), block)
        block = block.astype(BF)
        for ox in range(2):
            for px in range(2):
                row = 16 * (2 * ox + px)
                out_ref[p, row : row + 16, :] = block[16 * ox : 16 * ox + 16, 64 * px : 64 * px + 64]


def pool_matrix():
    out = np.zeros((2, 4, 4, 2, 2, 2, 2, 4, 4), np.float32)
    for ox in range(2):
        for y in range(4):
            for z in range(4):
                out[ox, y, z, ox, y // 2, z // 2, :, 2 * (y % 2) : 2 * (y % 2) + 2, 2 * (z % 2) : 2 * (z % 2) + 2] = 0.125
    return out.reshape(32, 256)


VM = pl.BlockSpec(memory_space=pltpu.VMEM)
SM = pl.BlockSpec(memory_space=pltpu.SMEM)
ANY = pl.BlockSpec(memory_space=pl.ANY)
HBM = pl.BlockSpec(memory_space=pltpu.HBM)


def call_rules(n, features, weights, rulebook, recv_list):
    tile_count, _, channels = features.shape
    offsets, _, quarter = weights.shape
    rule_rows = rulebook.shape[0]
    routes, table = matchings(n)
    count = len(routes) // 2
    slots = tile_count // 4
    span = tile_count * VOX + 2 * PAD
    wide = rule_rows + 128
    lists_shape = ((3 * PARTS + 1) * wide,)
    scalars = [pltpu.SMEM((8, wide), jnp.int32), pltpu.SMEM(lists_shape, jnp.int32)]
    flat = features.reshape(tile_count * VOX, channels)
    flat_weights = weights.transpose(0, 2, 1).reshape(offsets * quarter, channels)
    block = jax.ShapeDtypeStruct((slots, HALF, 128), BF)
    whole = jax.ShapeDtypeStruct((tile_count, HALF, 128), F32)
    work = [pltpu.VMEM((tile_count, VOX, 128), F32)] * 2
    flops = 2 * tile_count * VOX * channels * offsets * quarter
    shared = dict(
        compiler_params=pltpu.CompilerParams(vmem_limit_bytes=16 * 1024 * 1024),
        cost_estimate=pl.CostEstimate(flops=flops, bytes_accessed=8 << 20, transcendentals=0),
    )
    made = pl.pallas_call(
        functools.partial(far_kernel, count, table, tile_count),
        out_shape=[block] * count
        + [jax.ShapeDtypeStruct(flat.shape, BF), jax.ShapeDtypeStruct((PER_PART * span, 128), F32)]
        + [jax.ShapeDtypeStruct((PER_PART * span, 128), F32)] * (PARTS - 1)
        + [jax.ShapeDtypeStruct((8, wide), jnp.int32), jax.ShapeDtypeStruct(lists_shape, jnp.int32)],
        in_specs=[HBM] * 3,
        out_specs=[VM] * (count + 3 + PARTS),
        scratch_shapes=work
        + [
            pltpu.VMEM(flat_weights.shape, BF),
            pltpu.VMEM((4, rule_rows), jnp.int32),
            *scalars,
            pltpu.SemaphoreType.DMA((5 + F_PARTS,)),
        ],
        name="far",
        **shared,
    )(*(pltpu.with_memory_space_constraint(x, pltpu.HBM) for x in (rulebook.T, flat, flat_weights)))
    far_sends = made[:count]
    held, *products, words, lists = made[count:]
    arrivals = [lax.ppermute(x, "tiles", route) for x, route in zip(far_sends, routes[:count])]
    near_sends = pl.pallas_call(
        near_kernel,
        out_shape=[block] * (len(routes) - count),
        in_specs=[VM] * (2 + PARTS),
        out_specs=[VM] * (len(routes) - count),
        scratch_shapes=work + scalars + [pltpu.SemaphoreType.DMA((2,))],
        name="near",
        **shared,
    )(words, lists, *products)
    near_arrivals = [lax.ppermute(x, "tiles", route) for x, route in zip(near_sends, routes[count:])]
    local = pl.pallas_call(
        local_kernel,
        out_shape=whole,
        in_specs=[VM, VM, ANY] + [VM] * PARTS,
        out_specs=VM,
        scratch_shapes=work + scalars + [pltpu.SemaphoreType.DMA((2,))],
        name="local",
        **shared,
    )(words, lists, near_sends[0], *products)
    local = pl.pallas_call(
        functools.partial(arrive_kernel, 0, table),
        out_shape=whole,
        in_specs=[VM] * (2 + count),
        out_specs=VM,
        scratch_shapes=[pltpu.SMEM(recv_list.shape, jnp.int32), pltpu.SemaphoreType.DMA],
        compiler_params=pltpu.CompilerParams(vmem_limit_bytes=12 * 1024 * 1024),
        name="arrive",
    )(recv_list, local, *arrivals)
    return count, table, held, local, near_arrivals


def body(n, features, weights, gain, rulebook, recv_list, coarse_send, coarse_place):
    tile_count, _, channels = features.shape
    quarter = weights.shape[2]
    small = pltpu.CompilerParams(vmem_limit_bytes=12 * 1024 * 1024)

    count, table, held, local, arrivals = call_rules(n, features, weights, rulebook, recv_list)
    conv, sums = pl.pallas_call(
        functools.partial(combine_kernel, count, table),
        out_shape=[
            jax.ShapeDtypeStruct((tile_count, HALF, 128), F32),
            jax.ShapeDtypeStruct((2, tile_count * HALF), F32),
        ],
        in_specs=[VM] * (2 + len(arrivals)),
        out_specs=[VM, VM],
        scratch_shapes=[pltpu.SMEM(recv_list.shape, jnp.int32), pltpu.SemaphoreType.DMA],
        compiler_params=small,
        name="combine",
    )(recv_list, local, *arrivals)
    own = pl.pallas_call(
        own_kernel,
        out_shape=jax.ShapeDtypeStruct((tile_count, HALF, 128), F32),
        in_specs=[VM, ANY],
        out_specs=VM,
        compiler_params=small,
        name="own",
    )(held, sums)
    wide = lax.axis_size("chan")
    others = [lax.ppermute(sums, "chan", [(i, i ^ m) for i in range(wide)]) for m in range(1, wide)]
    slot_count = coarse_place.shape[1]
    parent_count = tile_count // 8
    packed, outbound = pl.pallas_call(
        functools.partial(norm_kernel, channels),
        out_shape=[
            jax.ShapeDtypeStruct((tile_count, HALF, 128), BF),
            jax.ShapeDtypeStruct((slot_count, HALF, 128), BF),
        ],
        in_specs=[VM] * 9,
        out_specs=[VM, VM],
        scratch_shapes=[pltpu.SMEM(coarse_send.shape, jnp.int32), pltpu.SemaphoreType.DMA],
        compiler_params=small,
        name="norm",
    )(
        conv,
        own,
        jnp.tile(gain.astype(F32), 2).reshape(1, 128),
        jnp.asarray(pool_matrix(), BF),
        coarse_send,
        sums,
        *others,
    )
    landed = lax.all_to_all(outbound, "tiles", split_axis=0, concat_axis=0, tiled=True)
    skip = pl.pallas_call(
        unpack_kernel,
        out_shape=jax.ShapeDtypeStruct((tile_count, VOX, quarter), BF),
        in_specs=[VM],
        out_specs=VM,
        compiler_params=small,
        name="unpack",
    )(packed)
    coarse = pl.pallas_call(
        place_kernel,
        out_shape=jax.ShapeDtypeStruct((parent_count, VOX, quarter), BF),
        in_specs=[VM, VM],
        out_specs=VM,
        compiler_params=small,
        name="place",
    )(coarse_place, landed)
    return (skip, coarse)


def solution(mesh):
    in_specs = (
        P("tiles", None, None),
        P(None, None, "chan"),
        P("chan"),
        P("tiles", None),
        P("tiles", None),
        P("tiles", None),
        P("tiles", None),
    )
    out_specs = (P("tiles", None, "chan"), P("tiles", None, "chan"))
    return jax.shard_map(
        functools.partial(body, mesh.shape["tiles"]),
        mesh=mesh,
        in_specs=in_specs,
        out_specs=out_specs,
        check_vma=False,
    )
```

```python
import functools

import jax
import jax.numpy as jnp
import numpy as np
from jax import lax
from jax.experimental import pallas as pl
from jax.experimental.pallas import tpu as pltpu
from jax.sharding import PartitionSpec as P

EPS = 1e-05
BF_MAX = float(jnp.finfo(jnp.bfloat16).max)
REACH = 4
VOX = 64
HALF = 32
BF = jnp.bfloat16
F32 = jnp.float32
PAD = 64
UNROLL = 8
F_PARTS = 1
PARTS = 2
PER_PART = 7
ORDER = (0, 5, 4, 2, 1, 6, 3)


def perfect(n):
    real = [(i, j) for i in range(n) for j in range(i + 1, n) if j - i <= REACH]
    fill = [(0, 1), (0, 1), (0, 2), (6, 7), (6, 7), (5, 7)]
    first = [(i, i + REACH) for i in range(n - REACH)]
    start = [(p, True) for p in real if p not in first] + [(p, False) for p in fill]

    def crossing(found):
        return -sum(i < n // 2 <= j for (i, j), _ in found)

    def split(left):
        if not left:
            return []
        here = left[0]

        def grow(chosen, rest):
            used = {i for p, _ in chosen for i in p}
            if len(used) == n:
                yield chosen, rest
                return
            low = min(set(range(n)) - used)
            for k, item in enumerate(rest):
                if low in item[0] and not used & set(item[0]):
                    yield from grow(chosen + [item], rest[:k] + rest[k + 1 :])

        for chosen, rest in grow([here], left[1:]):
            more = split(rest)
            if more is not None:
                return [chosen] + more
        return None

    found = split(start)
    return None if found is None else [[(p, True) for p in first]] + sorted(found, key=crossing)


def matchings(n):
    found = perfect(n) if n == 2 * REACH else None
    if found is not None:
        found = [found[i] for i in ORDER]
    if found is None:
        found = []
        for d in range(REACH, 0, -1):
            for parity in (0, 1):
                pairs = [(i, i + d) for i in range(n - d) if (i // d) % 2 == parity]
                rest = [i for i in range(n) if all(i not in p for p in pairs)]
                if pairs:
                    found.append([(p, True) for p in pairs] + [(p, False) for p in zip(rest[::2], rest[1::2])])
    routes = [[q for p, _ in way for q in (p, p[::-1])] for way in found]
    table = np.full((n, 16), -1, np.int32)
    table[:, 15] = 0
    for m, way in enumerate(found):
        for pair, is_real in way:
            for e, other in (pair, pair[::-1]):
                if is_real:
                    gap = other - e
                    table[e, m] = REACH - 1 + gap if gap > 0 else -gap - 1
                    table[e, 15] += m << (4 * (gap - 1 if gap > 0 else REACH - 1 - gap))
    return routes, table


def pick(e, values):
    found = jnp.int32(int(values[0]))
    for i in range(1, len(values)):
        found = jnp.where(e == i, jnp.int32(int(values[i])), found)
    return found


def lane_iota(shape):
    return lax.broadcasted_iota(jnp.int32, shape, len(shape) - 1)


def dims_of(code):
    return (lax.div(code, 9) - 1, lax.rem(lax.div(code, 3), 3) - 1, lax.rem(code, 3) - 1)


def rules_matmul(f_ref, w_ref, y_refs, ready, beside):
    rows = f_ref.shape[0]
    span = rows + 2 * PAD
    depth = w_ref.shape[0]
    steps = range(0, depth, 256)
    for number, q in enumerate(steps):
        width = min(256, depth - q)
        cuts = F_PARTS if number == 0 else 1
        size = rows // cuts
        for h in range(cuts):
            ready(number, h)
            part = lax.dot_general(
                f_ref[h * size : (h + 1) * size, :],
                w_ref[q : q + width, :],
                (((1,), (1,)), ((), ())),
                preferred_element_type=F32,
            )
            for s in range(0, width, 128):
                wide = min(128, width - s)
                y_ref = y_refs[(q + s) // 128 // PER_PART]
                base = ((q + s) // 128 % PER_PART) * span + PAD + h * size
                y_ref[base : base + size, 0:wide] = part[:, s : s + wide]
        beside(number, len(steps))


def rules_add(words, lists, part, y_refs, acc_ref):
    voxel = lax.broadcasted_iota(jnp.int32, (VOX, 128), 0)
    have = jnp.where(lane_iota((VOX, 128)) < 64, 1 << 21, 1 << 22)
    for dim, place in enumerate((lax.div(voxel, 16), lax.rem(lax.div(voxel, 4), 4), lax.rem(voxel, 4))):
        have = have + jnp.left_shift(jnp.full_like(place, 15), 3 - place + 7 * dim)

    for which, y_ref in enumerate(y_refs):
        kind = part * PARTS + which
        add_listed(words, lists, kind * words.shape[1], words[3, 128 * kind], have, y_ref, acc_ref)


def add_listed(words, lists, start, count, have, y_ref, acc_ref):
    def several(i, c):
        for u in range(UNROLL):
            r = lists[start + i * UNROLL + u]
            packed = words[0, r]
            need = words[1, r]
            taken = y_ref[pl.ds(lax.shift_right_logical(packed, 8), VOX), :]
            t = packed & 255
            half = acc_ref[u % 2]
            half[t] = half[t] + jnp.where((have & need) == need, taken, 0.0)
        return c

    lax.fori_loop(0, lax.div(count + (UNROLL - 1), UNROLL), several, 0)


def zero_blocks(acc_ref):
    def zero(i, c):
        for half in acc_ref:
            half[i] = jnp.zeros((VOX, 128), F32)
        return c

    lax.fori_loop(0, acc_ref[0].shape[0], zero, 0, unroll=8)


def folded(acc_ref, t):
    first = lane_iota((HALF, 128)) < 64
    low = acc_ref[0][t, 0:HALF, :] + acc_ref[1][t, 0:HALF, :]
    high = acc_ref[0][t, HALF:VOX, :] + acc_ref[1][t, HALF:VOX, :]
    low = low + pltpu.roll(low, 64, 1)
    high = high + pltpu.roll(high, 64, 1)
    return jnp.where(first, low, high)


def emit_sends(acc_ref, sends):
    slots = sends[0].shape[0]
    for m, send_ref in enumerate(sends):

        def emit(i, c, send_ref=send_ref, base=slots * m):
            send_ref[i] = folded(acc_ref, base + i).astype(BF)
            return c

        lax.fori_loop(0, slots, emit, 0, unroll=16)


def far_kernel(count, table, tile_count, rules_hbm, f_hbm, w_hbm, *rest):
    sends, rest = rest[:count], rest[count:]
    f_ref, y_refs, rest = rest[0], rest[1 : 1 + PARTS], rest[1 + PARTS :]
    words_v, lists_v, *acc_ref, w_ref, rules_ref, words_s, lists, sems = rest
    rows = tile_count * VOX
    span = rows + 2 * PAD
    rule_rows = rules_ref.shape[1]
    wide = words_v.shape[1]
    slots = tile_count // 4
    depth = w_ref.shape[0]
    size = rows // F_PARTS
    rules_copy = pltpu.make_async_copy(rules_hbm, rules_ref, sems.at[0])
    f_copies = [
        pltpu.make_async_copy(f_hbm.at[pl.ds(h * size, size)], f_ref.at[pl.ds(h * size, size)], sems.at[3 + h])
        for h in range(F_PARTS)
    ]
    w_copies = [
        pltpu.make_async_copy(w_hbm.at[pl.ds(q, width)], w_ref.at[pl.ds(q, width)], sems.at[3 + F_PARTS + i])
        for i, (q, width) in enumerate([(0, 256), (256, depth - 256)])
    ]
    for copy in [rules_copy, w_copies[0], *f_copies, w_copies[1]]:
        copy.start()
    before = lax.broadcasted_iota(jnp.int32, (rule_rows, rule_rows), 0)
    before = (before <= lane_iota((rule_rows, rule_rows))).astype(F32).astype(BF)
    zero_blocks(acc_ref)
    rules_copy.wait()
    tile = rules_ref[0:1, :]
    kernel = rules_ref[1:2, :]
    heading = rules_ref[2:3, :]
    target = rules_ref[3:4, :]
    code = jnp.minimum(kernel, 26)
    shift = jnp.zeros_like(code)
    need = jnp.where(lax.rem(code, 2) == 0, 1 << 21, 1 << 22)
    for dim, (step, turn) in enumerate(zip(dims_of(code), dims_of(heading))):
        move = step - 4 * turn
        shift = shift + move * (16, 4, 1)[dim]
        need = need + jnp.left_shift(jnp.full_like(move, 1), move + (3 + 7 * dim))
    sent = jnp.maximum(target - tile_count, 0)
    group = lax.div(sent, slots)
    coded = jnp.full_like(group, pick(lax.axis_index("tiles"), table[:, 15]))
    way = lax.shift_right_logical(coded, 4 * group) & 15
    near = way >= count
    place = jnp.where(near, way - count, way) * slots + lax.rem(sent, slots)
    part = jnp.where(target < tile_count, 2, jnp.where(near, 1, 0))
    pair = lax.div(code, 2)
    part = jnp.where(kernel < 27, part * PARTS + lax.div(pair, PER_PART), 3 * PARTS)
    kind = lax.broadcasted_iota(jnp.int32, (8, rule_rows), 0)
    flags = jnp.where(kind == part, 1.0, 0.0)
    upto = jnp.dot(flags.astype(BF), before, preferred_element_type=F32)
    at = jnp.sum(flags * (upto - 1.0 + (kind * wide).astype(F32)), axis=0, keepdims=True)
    first_row = lax.rem(pair, PER_PART) * span + PAD + tile * VOX + shift
    words_v[...] = jnp.zeros(words_v.shape, jnp.int32)
    words_v[0:1, 0:rule_rows] = first_row * 256 + jnp.where(target < tile_count, target, place)
    words_v[1:2, 0:rule_rows] = need
    words_v[2:3, 0:rule_rows] = at.astype(jnp.int32)
    words_v[0:1, rule_rows:wide] = jnp.full((1, wide - rule_rows), PAD * 256, jnp.int32)
    words_v[1:2, rule_rows:wide] = jnp.full((1, wide - rule_rows), 1 << 23, jnp.int32)
    for c in range(3 * PARTS):
        total = upto[c : c + 1, rule_rows - 1 : rule_rows]
        words_v[3:4, 128 * c : 128 * c + 128] = jnp.broadcast_to(total, (1, 128)).astype(jnp.int32)
    to_scalars = pltpu.make_async_copy(words_v, words_s, sems.at[1])
    to_scalars.start()

    def ready(number, h):
        if number == 0:
            if h == 0:
                w_copies[0].wait()
            f_copies[h].wait()
        if number == 1:
            w_copies[1].wait()

    def list_some(number, steps):
        if number == 0:
            to_scalars.wait()
        share = -(-rule_rows // (steps - 1))
        for r in range(number * share, min(rule_rows, (number + 1) * share)):
            lists[words_s[2, r]] = r

    rules_matmul(f_ref, w_ref, y_refs, ready, list_some)
    for c in range(3 * PARTS):
        for u in range(UNROLL):
            lists[c * wide + words_s[3, 128 * c] + u] = rule_rows
    hand_on = pltpu.make_async_copy(lists, lists_v, sems.at[2])
    hand_on.start()
    rules_add(words_s, lists, 0, y_refs, acc_ref)
    emit_sends(acc_ref, sends)
    hand_on.wait()


def near_kernel(words_v, lists_v, *rest):
    y_refs, sends = rest[:PARTS], rest[PARTS:-5]
    *acc_ref, words, lists, sems = rest[-5:]
    copies = [
        pltpu.make_async_copy(words_v, words, sems.at[0]),
        pltpu.make_async_copy(lists_v, lists, sems.at[1]),
    ]
    for copy in copies:
        copy.start()
    zero_blocks(acc_ref)
    for copy in copies:
        copy.wait()
    rules_add(words, lists, 1, y_refs, acc_ref)
    emit_sends(acc_ref, sends)


def add_arrivals(first, table, blocks, list_ref, out_ref):
    e = lax.axis_index("tiles")
    slots = blocks[0].shape[0]
    for m, block in enumerate(blocks):
        group = pick(e, table[:, first + m])

        @pl.when(group >= 0)
        def _(block=block, group=group):
            for i in range(slots):
                t = list_ref[0, group * slots + i]
                out_ref[t] = out_ref[t] + block[i].astype(F32)


def local_kernel(words_v, lists_v, _after, *rest):
    y_refs, (local_ref, *acc_ref, words, lists, sems) = rest[:PARTS], rest[PARTS:]
    copies = [
        pltpu.make_async_copy(words_v, words, sems.at[0]),
        pltpu.make_async_copy(lists_v, lists, sems.at[1]),
    ]
    for copy in copies:
        copy.start()
    zero_blocks(acc_ref)
    for copy in copies:
        copy.wait()
    rules_add(words, lists, 2, y_refs, acc_ref)

    def keep(t, c):
        local_ref[t] = folded(acc_ref, t)
        return c

    lax.fori_loop(0, acc_ref[0].shape[0], keep, 0, unroll=16)


def arrive_kernel(first, table, list_v, local_ref, *rest):
    blocks = rest[:-3]
    out_ref, list_ref, sem = rest[-3:]
    copy = pltpu.make_async_copy(list_v, list_ref, sem)
    copy.start()
    out_ref[...] = local_ref[...]
    copy.wait()
    add_arrivals(first, table, blocks, list_ref, out_ref)


def own_kernel(f_ref, _after, own_ref):
    c = lax.axis_index("chan")
    at = pl.multiple_of(lax.div(c, 2) * 128, 128)
    odd = lax.rem(c, 2) == 1
    first = lane_iota((HALF, 128)) < 64

    def pack(t, c):
        block = f_ref[pl.ds(pl.multiple_of(t * VOX, VOX), VOX), pl.ds(at, 128)].astype(F32)
        low, high = block[:HALF], block[HALF:]
        even_form = jnp.where(first, low, pltpu.roll(high, 64, 1))
        odd_form = jnp.where(first, pltpu.roll(low, 64, 1), high)
        own_ref[t] = jnp.where(odd, odd_form, even_form)
        return c

    lax.fori_loop(0, own_ref.shape[0], pack, 0, unroll=8)


def combine_kernel(first, table, list_v, local_ref, *rest):
    blocks = rest[:-4]
    conv_ref, sums_ref, list_ref, sem = rest[-4:]
    copy = pltpu.make_async_copy(list_v, list_ref, sem)
    copy.start()
    tile_count = local_ref.shape[0]
    conv_ref[...] = local_ref[...]
    copy.wait()
    add_arrivals(first, table, blocks, list_ref, conv_ref)
    rows = tile_count * HALF
    pick = (lane_iota((2, 256)) // 64 % 2 == lax.broadcasted_iota(jnp.int32, (2, 256), 0)).astype(BF)
    step = rows
    for at in range(0, rows, step):
        value = conv_ref[at // HALF : (at + step) // HALF].reshape(step, 128)
        square = value * value
        top = jnp.minimum(square, BF_MAX).astype(BF)
        rest_of = (square - top.astype(F32)).astype(BF)
        sums_ref[:, at : at + step] = lax.dot_general(
            pick,
            jnp.concatenate([top, rest_of], axis=1),
            (((1,), (1,)), ((), ())),
            preferred_element_type=F32,
        )


def norm_kernel(channels, conv_ref, own_ref, gain_ref, pool_ref, slot_v, s0, s1, s2, s3, whole_ref, out_ref, slot_ref, sem):
    copy = pltpu.make_async_copy(slot_v, slot_ref, sem)
    copy.start()
    tile_count = conv_ref.shape[0]
    total = (s0[...] + s1[...]) + (s2[...] + s3[...])
    rest = lax.rsqrt(total * (1.0 / channels) + EPS)
    parts = []
    for _ in range(3):
        top = rest.astype(BF).astype(F32)
        parts.append(top)
        rest = rest - top
    parts = jnp.concatenate(parts, axis=0).astype(BF)
    count = parts.shape[0]
    spread = (lane_iota((count, 128)) // 64 == lax.broadcasted_iota(jnp.int32, (count, 128), 0) % 2).astype(BF)
    gain = 0.5 * gain_ref[...]
    for k in range(tile_count // 8):
        part = lax.dot_general(
            parts[:, k * 256 : (k + 1) * 256],
            spread,
            (((0,), (0,)), ((), ())),
            preferred_element_type=F32,
        )
        half = gain * conv_ref[8 * k : 8 * k + 8].reshape(256, 128) * part
        hidden = half + half * jnp.tanh(half)
        whole = (own_ref[8 * k : 8 * k + 8].reshape(256, 128) + hidden).astype(BF)
        whole_ref[8 * k : 8 * k + 8] = whole.reshape(8, HALF, 128)
    copy.wait()
    for k in range(tile_count // 8):
        whole = whole_ref[8 * k : 8 * k + 8].reshape(256, 128)
        out_ref[slot_ref[0, k]] = jnp.dot(pool_ref[...], whole, preferred_element_type=F32).astype(BF)


def unpack_kernel(whole_ref, skip_ref):
    skip_ref[:, 0:HALF, :] = whole_ref[:, :, 0:64]
    skip_ref[:, HALF:VOX, :] = whole_ref[:, :, 64:128]


def place_kernel(place_ref, landed_ref, out_ref):
    slots = landed_ref.shape[0]
    where = [jnp.broadcast_to(place_ref[:, i : i + 1], (HALF, 128)) for i in range(slots)]
    for p in range(out_ref.shape[0]):
        block = landed_ref[0].astype(F32)
        for i in range(1, slots):
            block = jnp.where(where[i] == p, landed_ref[i].astype(F32), block)
        block = block.astype(BF)
        for ox in range(2):
            for px in range(2):
                row = 16 * (2 * ox + px)
                out_ref[p, row : row + 16, :] = block[16 * ox : 16 * ox + 16, 64 * px : 64 * px + 64]


def pool_matrix():
    out = np.zeros((2, 4, 4, 2, 2, 2, 2, 4, 4), np.float32)
    for ox in range(2):
        for y in range(4):
            for z in range(4):
                out[ox, y, z, ox, y // 2, z // 2, :, 2 * (y % 2) : 2 * (y % 2) + 2, 2 * (z % 2) : 2 * (z % 2) + 2] = 0.125
    return out.reshape(32, 256)


VM = pl.BlockSpec(memory_space=pltpu.VMEM)
SM = pl.BlockSpec(memory_space=pltpu.SMEM)
ANY = pl.BlockSpec(memory_space=pl.ANY)
HBM = pl.BlockSpec(memory_space=pltpu.HBM)


def call_rules(n, features, weights, rulebook, recv_list):
    tile_count, _, channels = features.shape
    offsets, _, quarter = weights.shape
    rule_rows = rulebook.shape[0]
    routes, table = matchings(n)
    count = len(routes) // 2
    slots = tile_count // 4
    span = tile_count * VOX + 2 * PAD
    wide = rule_rows + 128
    lists_shape = ((3 * PARTS + 1) * wide,)
    scalars = [pltpu.SMEM((8, wide), jnp.int32), pltpu.SMEM(lists_shape, jnp.int32)]
    flat = features.reshape(tile_count * VOX, channels)
    flat_weights = weights.transpose(0, 2, 1).reshape(offsets * quarter, channels)
    block = jax.ShapeDtypeStruct((slots, HALF, 128), BF)
    whole = jax.ShapeDtypeStruct((tile_count, HALF, 128), F32)
    work = [pltpu.VMEM((tile_count, VOX, 128), F32)] * 2
    flops = 2 * tile_count * VOX * channels * offsets * quarter
    shared = dict(
        compiler_params=pltpu.CompilerParams(vmem_limit_bytes=16 * 1024 * 1024),
        cost_estimate=pl.CostEstimate(flops=flops, bytes_accessed=8 << 20, transcendentals=0),
    )
    made = pl.pallas_call(
        functools.partial(far_kernel, count, table, tile_count),
        out_shape=[block] * count
        + [jax.ShapeDtypeStruct(flat.shape, BF), jax.ShapeDtypeStruct((PER_PART * span, 128), F32)]
        + [jax.ShapeDtypeStruct((PER_PART * span, 128), F32)] * (PARTS - 1)
        + [jax.ShapeDtypeStruct((8, wide), jnp.int32), jax.ShapeDtypeStruct(lists_shape, jnp.int32)],
        in_specs=[HBM] * 3,
        out_specs=[VM] * (count + 3 + PARTS),
        scratch_shapes=work
        + [
            pltpu.VMEM(flat_weights.shape, BF),
            pltpu.VMEM((4, rule_rows), jnp.int32),
            *scalars,
            pltpu.SemaphoreType.DMA((5 + F_PARTS,)),
        ],
        name="far",
        **shared,
    )(*(pltpu.with_memory_space_constraint(x, pltpu.HBM) for x in (rulebook.T, flat, flat_weights)))
    far_sends = made[:count]
    held, *products, words, lists = made[count:]
    arrivals = [lax.ppermute(x, "tiles", route) for x, route in zip(far_sends, routes[:count])]
    near_sends = pl.pallas_call(
        near_kernel,
        out_shape=[block] * (len(routes) - count),
        in_specs=[VM] * (2 + PARTS),
        out_specs=[VM] * (len(routes) - count),
        scratch_shapes=work + scalars + [pltpu.SemaphoreType.DMA((2,))],
        name="near",
        **shared,
    )(words, lists, *products)
    near_arrivals = [lax.ppermute(x, "tiles", route) for x, route in zip(near_sends, routes[count:])]
    local = pl.pallas_call(
        local_kernel,
        out_shape=whole,
        in_specs=[VM, VM, ANY] + [VM] * PARTS,
        out_specs=VM,
        scratch_shapes=work + scalars + [pltpu.SemaphoreType.DMA((2,))],
        name="local",
        **shared,
    )(words, lists, near_sends[0], *products)
    local = pl.pallas_call(
        functools.partial(arrive_kernel, 0, table),
        out_shape=whole,
        in_specs=[VM] * (2 + count),
        out_specs=VM,
        scratch_shapes=[pltpu.SMEM(recv_list.shape, jnp.int32), pltpu.SemaphoreType.DMA],
        compiler_params=pltpu.CompilerParams(vmem_limit_bytes=12 * 1024 * 1024),
        name="arrive",
    )(recv_list, local, *arrivals)
    return count, table, held, local, near_arrivals


def body(n, features, weights, gain, rulebook, recv_list, coarse_send, coarse_place):
    tile_count, _, channels = features.shape
    quarter = weights.shape[2]
    small = pltpu.CompilerParams(vmem_limit_bytes=12 * 1024 * 1024)

    count, table, held, local, arrivals = call_rules(n, features, weights, rulebook, recv_list)
    conv, sums = pl.pallas_call(
        functools.partial(combine_kernel, count, table),
        out_shape=[
            jax.ShapeDtypeStruct((tile_count, HALF, 128), F32),
            jax.ShapeDtypeStruct((2, tile_count * HALF), F32),
        ],
        in_specs=[VM] * (2 + len(arrivals)),
        out_specs=[VM, VM],
        scratch_shapes=[pltpu.SMEM(recv_list.shape, jnp.int32), pltpu.SemaphoreType.DMA],
        compiler_params=small,
        name="combine",
    )(recv_list, local, *arrivals)
    own = pl.pallas_call(
        own_kernel,
        out_shape=jax.ShapeDtypeStruct((tile_count, HALF, 128), F32),
        in_specs=[VM, ANY],
        out_specs=VM,
        compiler_params=small,
        name="own",
    )(held, sums)
    wide = lax.axis_size("chan")
    others = [lax.ppermute(sums, "chan", [(i, i ^ m) for i in range(wide)]) for m in range(1, wide)]
    slot_count = coarse_place.shape[1]
    parent_count = tile_count // 8
    packed, outbound = pl.pallas_call(
        functools.partial(norm_kernel, channels),
        out_shape=[
            jax.ShapeDtypeStruct((tile_count, HALF, 128), BF),
            jax.ShapeDtypeStruct((slot_count, HALF, 128), BF),
        ],
        in_specs=[VM] * 9,
        out_specs=[VM, VM],
        scratch_shapes=[pltpu.SMEM(coarse_send.shape, jnp.int32), pltpu.SemaphoreType.DMA],
        compiler_params=small,
        name="norm",
    )(
        conv,
        own,
        jnp.tile(gain.astype(F32), 2).reshape(1, 128),
        jnp.asarray(pool_matrix(), BF),
        coarse_send,
        sums,
        *others,
    )
    landed = lax.all_to_all(outbound, "tiles", split_axis=0, concat_axis=0, tiled=True)
    skip = pl.pallas_call(
        unpack_kernel,
        out_shape=jax.ShapeDtypeStruct((tile_count, VOX, quarter), BF),
        in_specs=[VM],
        out_specs=VM,
        compiler_params=small,
        name="unpack",
    )(packed)
    coarse = pl.pallas_call(
        place_kernel,
        out_shape=jax.ShapeDtypeStruct((parent_count, VOX, quarter), BF),
        in_specs=[VM, VM],
        out_specs=VM,
        compiler_params=small,
        name="place",
    )(coarse_place, landed)
    return (skip, coarse)


def solution(mesh):
    in_specs = (
        P("tiles", None, None),
        P(None, None, "chan"),
        P("chan"),
        P("tiles", None),
        P("tiles", None),
        P("tiles", None),
        P("tiles", None),
    )
    out_specs = (P("tiles", None, "chan"), P("tiles", None, "chan"))
    return jax.shard_map(
        functools.partial(body, mesh.shape["tiles"]),
        mesh=mesh,
        in_specs=in_specs,
        out_specs=out_specs,
        check_vma=False,
    )
```

```python
import functools

import jax
import jax.numpy as jnp
import numpy as np
from jax import lax
from jax.experimental import pallas as pl
from jax.experimental.pallas import tpu as pltpu
from jax.sharding import PartitionSpec as P

EPS = 1e-05
BF_MAX = float(jnp.finfo(jnp.bfloat16).max)
REACH = 4
VOX = 64
HALF = 32
BF = jnp.bfloat16
F32 = jnp.float32
PAD = 64
UNROLL = 16
F_PARTS = 1
PARTS = 2
PER_PART = 7
ORDER = (0, 5, 4, 1, 2, 6, 3)


def perfect(n):
    real = [(i, j) for i in range(n) for j in range(i + 1, n) if j - i <= REACH]
    fill = [(0, 1), (0, 1), (0, 2), (6, 7), (6, 7), (5, 7)]
    first = [(i, i + REACH) for i in range(n - REACH)]
    start = [(p, True) for p in real if p not in first] + [(p, False) for p in fill]

    def crossing(found):
        return -sum(i < n // 2 <= j for (i, j), _ in found)

    def split(left):
        if not left:
            return []
        here = left[0]

        def grow(chosen, rest):
            used = {i for p, _ in chosen for i in p}
            if len(used) == n:
                yield chosen, rest
                return
            low = min(set(range(n)) - used)
            for k, item in enumerate(rest):
                if low in item[0] and not used & set(item[0]):
                    yield from grow(chosen + [item], rest[:k] + rest[k + 1 :])

        for chosen, rest in grow([here], left[1:]):
            more = split(rest)
            if more is not None:
                return [chosen] + more
        return None

    found = split(start)
    return None if found is None else [[(p, True) for p in first]] + sorted(found, key=crossing)


def matchings(n):
    found = perfect(n) if n == 2 * REACH else None
    if found is not None:
        found = [found[i] for i in ORDER]
    if found is None:
        found = []
        for d in range(REACH, 0, -1):
            for parity in (0, 1):
                pairs = [(i, i + d) for i in range(n - d) if (i // d) % 2 == parity]
                rest = [i for i in range(n) if all(i not in p for p in pairs)]
                if pairs:
                    found.append([(p, True) for p in pairs] + [(p, False) for p in zip(rest[::2], rest[1::2])])
    routes = [[q for p, _ in way for q in (p, p[::-1])] for way in found]
    table = np.full((n, 16), -1, np.int32)
    table[:, 15] = 0
    for m, way in enumerate(found):
        for pair, is_real in way:
            for e, other in (pair, pair[::-1]):
                if is_real:
                    gap = other - e
                    table[e, m] = REACH - 1 + gap if gap > 0 else -gap - 1
                    table[e, 15] += m << (4 * (gap - 1 if gap > 0 else REACH - 1 - gap))
    return routes, table


def pick(e, values):
    found = jnp.int32(int(values[0]))
    for i in range(1, len(values)):
        found = jnp.where(e == i, jnp.int32(int(values[i])), found)
    return found


def lane_iota(shape):
    return lax.broadcasted_iota(jnp.int32, shape, len(shape) - 1)


def dims_of(code):
    return (lax.div(code, 9) - 1, lax.rem(lax.div(code, 3), 3) - 1, lax.rem(code, 3) - 1)


def rules_matmul(f_ref, w_ref, y_refs, ready, beside):
    rows = f_ref.shape[0]
    span = rows + 2 * PAD
    depth = w_ref.shape[0]
    steps = range(0, depth, 256)
    for number, q in enumerate(steps):
        width = min(256, depth - q)
        cuts = F_PARTS if number == 0 else 1
        size = rows // cuts
        for h in range(cuts):
            ready(number, h)
            part = lax.dot_general(
                f_ref[h * size : (h + 1) * size, :],
                w_ref[q : q + width, :],
                (((1,), (1,)), ((), ())),
                preferred_element_type=F32,
            )
            for s in range(0, width, 128):
                wide = min(128, width - s)
                y_ref = y_refs[(q + s) // 128 // PER_PART]
                base = ((q + s) // 128 % PER_PART) * span + PAD + h * size
                y_ref[base : base + size, 0:wide] = part[:, s : s + wide]
        beside(number, len(steps))


def rules_add(words, lists, part, y_refs, acc_ref):
    voxel = lax.broadcasted_iota(jnp.int32, (VOX, 128), 0)
    have = jnp.where(lane_iota((VOX, 128)) < 64, 1 << 21, 1 << 22)
    for dim, place in enumerate((lax.div(voxel, 16), lax.rem(lax.div(voxel, 4), 4), lax.rem(voxel, 4))):
        have = have + jnp.left_shift(jnp.full_like(place, 15), 3 - place + 7 * dim)

    for which, y_ref in enumerate(y_refs):
        kind = part * PARTS + which
        add_listed(words, lists, kind * words.shape[1], words[3, 128 * kind], have, y_ref, acc_ref)


def add_listed(words, lists, start, count, have, y_ref, acc_ref):
    def several(i, c):
        for u in range(UNROLL):
            r = lists[start + i * UNROLL + u]
            packed = words[0, r]
            need = words[1, r]
            taken = y_ref[pl.ds(lax.shift_right_logical(packed, 8), VOX), :]
            t = packed & 255
            half = acc_ref[u % 2]
            half[t] = half[t] + jnp.where((have & need) == need, taken, 0.0)
        return c

    lax.fori_loop(0, lax.div(count + (UNROLL - 1), UNROLL), several, 0)


def zero_blocks(acc_ref):
    def zero(i, c):
        for half in acc_ref:
            half[i] = jnp.zeros((VOX, 128), F32)
        return c

    lax.fori_loop(0, acc_ref[0].shape[0], zero, 0, unroll=8)


def folded(acc_ref, t):
    first = lane_iota((HALF, 128)) < 64
    low = acc_ref[0][t, 0:HALF, :] + acc_ref[1][t, 0:HALF, :]
    high = acc_ref[0][t, HALF:VOX, :] + acc_ref[1][t, HALF:VOX, :]
    low = low + pltpu.roll(low, 64, 1)
    high = high + pltpu.roll(high, 64, 1)
    return jnp.where(first, low, high)


def emit_sends(acc_ref, sends):
    slots = sends[0].shape[0]
    for m, send_ref in enumerate(sends):

        def emit(i, c, send_ref=send_ref, base=slots * m):
            send_ref[i] = folded(acc_ref, base + i).astype(BF)
            return c

        lax.fori_loop(0, slots, emit, 0, unroll=16)


def far_kernel(count, table, tile_count, rules_hbm, f_hbm, w_hbm, *rest):
    sends, rest = rest[:count], rest[count:]
    f_ref, y_refs, rest = rest[0], rest[1 : 1 + PARTS], rest[1 + PARTS :]
    words_v, lists_v, *acc_ref, w_ref, rules_ref, words_s, lists, sems = rest
    rows = tile_count * VOX
    span = rows + 2 * PAD
    rule_rows = rules_ref.shape[1]
    wide = words_v.shape[1]
    slots = tile_count // 4
    depth = w_ref.shape[0]
    size = rows // F_PARTS
    rules_copy = pltpu.make_async_copy(rules_hbm, rules_ref, sems.at[0])
    f_copies = [
        pltpu.make_async_copy(f_hbm.at[pl.ds(h * size, size)], f_ref.at[pl.ds(h * size, size)], sems.at[3 + h])
        for h in range(F_PARTS)
    ]
    w_copies = [
        pltpu.make_async_copy(w_hbm.at[pl.ds(q, width)], w_ref.at[pl.ds(q, width)], sems.at[3 + F_PARTS + i])
        for i, (q, width) in enumerate([(0, 256), (256, depth - 256)])
    ]
    for copy in [rules_copy, w_copies[0], *f_copies, w_copies[1]]:
        copy.start()
    before = lax.broadcasted_iota(jnp.int32, (rule_rows, rule_rows), 0)
    before = (before <= lane_iota((rule_rows, rule_rows))).astype(F32).astype(BF)
    zero_blocks(acc_ref)
    rules_copy.wait()
    tile = rules_ref[0:1, :]
    kernel = rules_ref[1:2, :]
    heading = rules_ref[2:3, :]
    target = rules_ref[3:4, :]
    code = jnp.minimum(kernel, 26)
    shift = jnp.zeros_like(code)
    need = jnp.where(lax.rem(code, 2) == 0, 1 << 21, 1 << 22)
    for dim, (step, turn) in enumerate(zip(dims_of(code), dims_of(heading))):
        move = step - 4 * turn
        shift = shift + move * (16, 4, 1)[dim]
        need = need + jnp.left_shift(jnp.full_like(move, 1), move + (3 + 7 * dim))
    sent = jnp.maximum(target - tile_count, 0)
    group = lax.div(sent, slots)
    coded = jnp.full_like(group, pick(lax.axis_index("tiles"), table[:, 15]))
    way = lax.shift_right_logical(coded, 4 * group) & 15
    near = way >= count
    place = jnp.where(near, way - count, way) * slots + lax.rem(sent, slots)
    part = jnp.where(target < tile_count, 2, jnp.where(near, 1, 0))
    pair = lax.div(code, 2)
    part = jnp.where(kernel < 27, part * PARTS + lax.div(pair, PER_PART), 3 * PARTS)
    kind = lax.broadcasted_iota(jnp.int32, (8, rule_rows), 0)
    flags = jnp.where(kind == part, 1.0, 0.0)
    upto = jnp.dot(flags.astype(BF), before, preferred_element_type=F32)
    at = jnp.sum(flags * (upto - 1.0 + (kind * wide).astype(F32)), axis=0, keepdims=True)
    first_row = lax.rem(pair, PER_PART) * span + PAD + tile * VOX + shift
    words_v[...] = jnp.zeros(words_v.shape, jnp.int32)
    words_v[0:1, 0:rule_rows] = first_row * 256 + jnp.where(target < tile_count, target, place)
    words_v[1:2, 0:rule_rows] = need
    words_v[2:3, 0:rule_rows] = at.astype(jnp.int32)
    words_v[0:1, rule_rows:wide] = jnp.full((1, wide - rule_rows), PAD * 256, jnp.int32)
    words_v[1:2, rule_rows:wide] = jnp.full((1, wide - rule_rows), 1 << 23, jnp.int32)
    for c in range(3 * PARTS):
        total = upto[c : c + 1, rule_rows - 1 : rule_rows]
        words_v[3:4, 128 * c : 128 * c + 128] = jnp.broadcast_to(total, (1, 128)).astype(jnp.int32)
    to_scalars = pltpu.make_async_copy(words_v, words_s, sems.at[1])
    to_scalars.start()

    def ready(number, h):
        if number == 0:
            if h == 0:
                w_copies[0].wait()
            f_copies[h].wait()
        if number == 1:
            w_copies[1].wait()

    def list_some(number, steps):
        if number == 0:
            to_scalars.wait()
        share = -(-rule_rows // (steps - 1))
        for r in range(number * share, min(rule_rows, (number + 1) * share)):
            lists[words_s[2, r]] = r

    rules_matmul(f_ref, w_ref, y_refs, ready, list_some)
    for c in range(3 * PARTS):
        for u in range(UNROLL):
            lists[c * wide + words_s[3, 128 * c] + u] = rule_rows
    hand_on = pltpu.make_async_copy(lists, lists_v, sems.at[2])
    hand_on.start()
    rules_add(words_s, lists, 0, y_refs, acc_ref)
    emit_sends(acc_ref, sends)
    hand_on.wait()


def near_kernel(words_v, lists_v, *rest):
    y_refs, sends = rest[:PARTS], rest[PARTS:-5]
    *acc_ref, words, lists, sems = rest[-5:]
    copies = [
        pltpu.make_async_copy(words_v, words, sems.at[0]),
        pltpu.make_async_copy(lists_v, lists, sems.at[1]),
    ]
    for copy in copies:
        copy.start()
    zero_blocks(acc_ref)
    for copy in copies:
        copy.wait()
    rules_add(words, lists, 1, y_refs, acc_ref)
    emit_sends(acc_ref, sends)


def add_arrivals(first, table, blocks, list_ref, out_ref):
    e = lax.axis_index("tiles")
    slots = blocks[0].shape[0]
    for m, block in enumerate(blocks):
        group = pick(e, table[:, first + m])

        @pl.when(group >= 0)
        def _(block=block, group=group):
            for i in range(slots):
                t = list_ref[0, group * slots + i]
                out_ref[t] = out_ref[t] + block[i].astype(F32)


def local_kernel(words_v, lists_v, _after, *rest):
    y_refs, (local_ref, *acc_ref, words, lists, sems) = rest[:PARTS], rest[PARTS:]
    copies = [
        pltpu.make_async_copy(words_v, words, sems.at[0]),
        pltpu.make_async_copy(lists_v, lists, sems.at[1]),
    ]
    for copy in copies:
        copy.start()
    zero_blocks(acc_ref)
    for copy in copies:
        copy.wait()
    rules_add(words, lists, 2, y_refs, acc_ref)

    def keep(t, c):
        local_ref[t] = folded(acc_ref, t)
        return c

    lax.fori_loop(0, acc_ref[0].shape[0], keep, 0, unroll=16)


def arrive_kernel(first, table, list_v, local_ref, *rest):
    blocks = rest[:-3]
    out_ref, list_ref, sem = rest[-3:]
    copy = pltpu.make_async_copy(list_v, list_ref, sem)
    copy.start()
    out_ref[...] = local_ref[...]
    copy.wait()
    add_arrivals(first, table, blocks, list_ref, out_ref)


def own_kernel(f_ref, _after, own_ref):
    c = lax.axis_index("chan")
    at = pl.multiple_of(lax.div(c, 2) * 128, 128)
    odd = lax.rem(c, 2) == 1
    first = lane_iota((HALF, 128)) < 64

    def pack(t, c):
        block = f_ref[pl.ds(pl.multiple_of(t * VOX, VOX), VOX), pl.ds(at, 128)].astype(F32)
        low, high = block[:HALF], block[HALF:]
        even_form = jnp.where(first, low, pltpu.roll(high, 64, 1))
        odd_form = jnp.where(first, pltpu.roll(low, 64, 1), high)
        own_ref[t] = jnp.where(odd, odd_form, even_form)
        return c

    lax.fori_loop(0, own_ref.shape[0], pack, 0, unroll=8)


def combine_kernel(first, table, list_v, local_ref, *rest):
    blocks = rest[:-4]
    conv_ref, sums_ref, list_ref, sem = rest[-4:]
    copy = pltpu.make_async_copy(list_v, list_ref, sem)
    copy.start()
    tile_count = local_ref.shape[0]
    conv_ref[...] = local_ref[...]
    copy.wait()
    add_arrivals(first, table, blocks, list_ref, conv_ref)
    rows = tile_count * HALF
    pick = (lane_iota((2, 256)) // 64 % 2 == lax.broadcasted_iota(jnp.int32, (2, 256), 0)).astype(BF)
    step = rows
    for at in range(0, rows, step):
        value = conv_ref[at // HALF : (at + step) // HALF].reshape(step, 128)
        square = value * value
        top = jnp.minimum(square, BF_MAX).astype(BF)
        rest_of = (square - top.astype(F32)).astype(BF)
        sums_ref[:, at : at + step] = lax.dot_general(
            pick,
            jnp.concatenate([top, rest_of], axis=1),
            (((1,), (1,)), ((), ())),
            preferred_element_type=F32,
        )


def norm_kernel(channels, conv_ref, own_ref, gain_ref, pool_ref, slot_v, s0, s1, s2, s3, whole_ref, out_ref, slot_ref, sem):
    copy = pltpu.make_async_copy(slot_v, slot_ref, sem)
    copy.start()
    tile_count = conv_ref.shape[0]
    total = (s0[...] + s1[...]) + (s2[...] + s3[...])
    rest = lax.rsqrt(total * (1.0 / channels) + EPS)
    parts = []
    for _ in range(3):
        top = rest.astype(BF).astype(F32)
        parts.append(top)
        rest = rest - top
    parts = jnp.concatenate(parts, axis=0).astype(BF)
    count = parts.shape[0]
    spread = (lane_iota((count, 128)) // 64 == lax.broadcasted_iota(jnp.int32, (count, 128), 0) % 2).astype(BF)
    gain = 0.5 * gain_ref[...]
    for k in range(tile_count // 8):
        part = lax.dot_general(
            parts[:, k * 256 : (k + 1) * 256],
            spread,
            (((0,), (0,)), ((), ())),
            preferred_element_type=F32,
        )
        half = gain * conv_ref[8 * k : 8 * k + 8].reshape(256, 128) * part
        hidden = half + half * jnp.tanh(half)
        whole = (own_ref[8 * k : 8 * k + 8].reshape(256, 128) + hidden).astype(BF)
        whole_ref[8 * k : 8 * k + 8] = whole.reshape(8, HALF, 128)
    copy.wait()
    for k in range(tile_count // 8):
        whole = whole_ref[8 * k : 8 * k + 8].reshape(256, 128)
        out_ref[slot_ref[0, k]] = jnp.dot(pool_ref[...], whole, preferred_element_type=F32).astype(BF)


def unpack_kernel(whole_ref, skip_ref):
    skip_ref[:, 0:HALF, :] = whole_ref[:, :, 0:64]
    skip_ref[:, HALF:VOX, :] = whole_ref[:, :, 64:128]


def place_kernel(place_ref, landed_ref, out_ref):
    slots = landed_ref.shape[0]
    where = [jnp.broadcast_to(place_ref[:, i : i + 1], (HALF, 128)) for i in range(slots)]
    for p in range(out_ref.shape[0]):
        block = landed_ref[0].astype(F32)
        for i in range(1, slots):
            block = jnp.where(where[i] == p, landed_ref[i].astype(F32), block)
        block = block.astype(BF)
        for ox in range(2):
            for px in range(2):
                row = 16 * (2 * ox + px)
                out_ref[p, row : row + 16, :] = block[16 * ox : 16 * ox + 16, 64 * px : 64 * px + 64]


def pool_matrix():
    out = np.zeros((2, 4, 4, 2, 2, 2, 2, 4, 4), np.float32)
    for ox in range(2):
        for y in range(4):
            for z in range(4):
                out[ox, y, z, ox, y // 2, z // 2, :, 2 * (y % 2) : 2 * (y % 2) + 2, 2 * (z % 2) : 2 * (z % 2) + 2] = 0.125
    return out.reshape(32, 256)


VM = pl.BlockSpec(memory_space=pltpu.VMEM)
SM = pl.BlockSpec(memory_space=pltpu.SMEM)
ANY = pl.BlockSpec(memory_space=pl.ANY)
HBM = pl.BlockSpec(memory_space=pltpu.HBM)


def call_rules(n, features, weights, rulebook, recv_list):
    tile_count, _, channels = features.shape
    offsets, _, quarter = weights.shape
    rule_rows = rulebook.shape[0]
    routes, table = matchings(n)
    count = len(routes) // 2
    slots = tile_count // 4
    span = tile_count * VOX + 2 * PAD
    wide = rule_rows + 128
    lists_shape = ((3 * PARTS + 1) * wide,)
    scalars = [pltpu.SMEM((8, wide), jnp.int32), pltpu.SMEM(lists_shape, jnp.int32)]
    flat = features.reshape(tile_count * VOX, channels)
    flat_weights = weights.transpose(0, 2, 1).reshape(offsets * quarter, channels)
    block = jax.ShapeDtypeStruct((slots, HALF, 128), BF)
    whole = jax.ShapeDtypeStruct((tile_count, HALF, 128), F32)
    work = [pltpu.VMEM((tile_count, VOX, 128), F32)] * 2
    flops = 2 * tile_count * VOX * channels * offsets * quarter
    shared = dict(
        compiler_params=pltpu.CompilerParams(vmem_limit_bytes=16 * 1024 * 1024),
        cost_estimate=pl.CostEstimate(flops=flops, bytes_accessed=8 << 20, transcendentals=0),
    )
    made = pl.pallas_call(
        functools.partial(far_kernel, count, table, tile_count),
        out_shape=[block] * count
        + [jax.ShapeDtypeStruct(flat.shape, BF), jax.ShapeDtypeStruct((PER_PART * span, 128), F32)]
        + [jax.ShapeDtypeStruct((PER_PART * span, 128), F32)] * (PARTS - 1)
        + [jax.ShapeDtypeStruct((8, wide), jnp.int32), jax.ShapeDtypeStruct(lists_shape, jnp.int32)],
        in_specs=[HBM] * 3,
        out_specs=[VM] * (count + 3 + PARTS),
        scratch_shapes=work
        + [
            pltpu.VMEM(flat_weights.shape, BF),
            pltpu.VMEM((4, rule_rows), jnp.int32),
            *scalars,
            pltpu.SemaphoreType.DMA((5 + F_PARTS,)),
        ],
        name="far",
        **shared,
    )(*(pltpu.with_memory_space_constraint(x, pltpu.HBM) for x in (rulebook.T, flat, flat_weights)))
    far_sends = made[:count]
    held, *products, words, lists = made[count:]
    arrivals = [lax.ppermute(x, "tiles", route) for x, route in zip(far_sends, routes[:count])]
    near_sends = pl.pallas_call(
        near_kernel,
        out_shape=[block] * (len(routes) - count),
        in_specs=[VM] * (2 + PARTS),
        out_specs=[VM] * (len(routes) - count),
        scratch_shapes=work + scalars + [pltpu.SemaphoreType.DMA((2,))],
        name="near",
        **shared,
    )(words, lists, *products)
    near_arrivals = [lax.ppermute(x, "tiles", route) for x, route in zip(near_sends, routes[count:])]
    local = pl.pallas_call(
        local_kernel,
        out_shape=whole,
        in_specs=[VM, VM, ANY] + [VM] * PARTS,
        out_specs=VM,
        scratch_shapes=work + scalars + [pltpu.SemaphoreType.DMA((2,))],
        name="local",
        **shared,
    )(words, lists, near_sends[0], *products)
    local = pl.pallas_call(
        functools.partial(arrive_kernel, 0, table),
        out_shape=whole,
        in_specs=[VM] * (2 + count),
        out_specs=VM,
        scratch_shapes=[pltpu.SMEM(recv_list.shape, jnp.int32), pltpu.SemaphoreType.DMA],
        compiler_params=pltpu.CompilerParams(vmem_limit_bytes=12 * 1024 * 1024),
        name="arrive",
    )(recv_list, local, *arrivals)
    return count, table, held, local, near_arrivals


def body(n, features, weights, gain, rulebook, recv_list, coarse_send, coarse_place):
    tile_count, _, channels = features.shape
    quarter = weights.shape[2]
    small = pltpu.CompilerParams(vmem_limit_bytes=12 * 1024 * 1024)

    count, table, held, local, arrivals = call_rules(n, features, weights, rulebook, recv_list)
    conv, sums = pl.pallas_call(
        functools.partial(combine_kernel, count, table),
        out_shape=[
            jax.ShapeDtypeStruct((tile_count, HALF, 128), F32),
            jax.ShapeDtypeStruct((2, tile_count * HALF), F32),
        ],
        in_specs=[VM] * (2 + len(arrivals)),
        out_specs=[VM, VM],
        scratch_shapes=[pltpu.SMEM(recv_list.shape, jnp.int32), pltpu.SemaphoreType.DMA],
        compiler_params=small,
        name="combine",
    )(recv_list, local, *arrivals)
    own = pl.pallas_call(
        own_kernel,
        out_shape=jax.ShapeDtypeStruct((tile_count, HALF, 128), F32),
        in_specs=[VM, ANY],
        out_specs=VM,
        compiler_params=small,
        name="own",
    )(held, sums)
    wide = lax.axis_size("chan")
    others = [lax.ppermute(sums, "chan", [(i, i ^ m) for i in range(wide)]) for m in range(1, wide)]
    slot_count = coarse_place.shape[1]
    parent_count = tile_count // 8
    packed, outbound = pl.pallas_call(
        functools.partial(norm_kernel, channels),
        out_shape=[
            jax.ShapeDtypeStruct((tile_count, HALF, 128), BF),
            jax.ShapeDtypeStruct((slot_count, HALF, 128), BF),
        ],
        in_specs=[VM] * 9,
        out_specs=[VM, VM],
        scratch_shapes=[pltpu.SMEM(coarse_send.shape, jnp.int32), pltpu.SemaphoreType.DMA],
        compiler_params=small,
        name="norm",
    )(
        conv,
        own,
        jnp.tile(gain.astype(F32), 2).reshape(1, 128),
        jnp.asarray(pool_matrix(), BF),
        coarse_send,
        sums,
        *others,
    )
    landed = lax.all_to_all(outbound, "tiles", split_axis=0, concat_axis=0, tiled=True)
    skip = pl.pallas_call(
        unpack_kernel,
        out_shape=jax.ShapeDtypeStruct((tile_count, VOX, quarter), BF),
        in_specs=[VM],
        out_specs=VM,
        compiler_params=small,
        name="unpack",
    )(packed)
    coarse = pl.pallas_call(
        place_kernel,
        out_shape=jax.ShapeDtypeStruct((parent_count, VOX, quarter), BF),
        in_specs=[VM, VM],
        out_specs=VM,
        compiler_params=small,
        name="place",
    )(coarse_place, landed)
    return (skip, coarse)


def solution(mesh):
    in_specs = (
        P("tiles", None, None),
        P(None, None, "chan"),
        P("chan"),
        P("tiles", None),
        P("tiles", None),
        P("tiles", None),
        P("tiles", None),
    )
    out_specs = (P("tiles", None, "chan"), P("tiles", None, "chan"))
    return jax.shard_map(
        functools.partial(body, mesh.shape["tiles"]),
        mesh=mesh,
        in_specs=in_specs,
        out_specs=out_specs,
        check_vma=False,
    )
```
